32 devices in a mesh: dp: 8 (over z, x), tensor: 4 (over y, core).
Axes of the slice: x: 2, y: 2, z: 4, core: 2. Of those that a mesh axis runs over, the one named last changes fastest.
Arguments:
- tokens_in: bfloat16 [8192, 1024], P(('dp', 'tensor')), may hold values from -6 to 6
- cotangent: bfloat16 [8192, 1024], P(('dp', 'tensor')), may hold values from -6 to 6
- routes: int32 [2, 8192, 8], P(None, 'dp'), may hold values from 0 to 15, all different within a row
- attn_gain: bfloat16 [2, 1024], P(None, 'dp'), may hold values from 0.5 to 1.5
- w_query: bfloat16 [2, 1024, 1024], P(None, 'dp', 'tensor'), may hold values from -0.1875 to 0.1875
- key_projection: bfloat16 [2, 1024, 512], P(None, 'dp', 'tensor'), may hold values from -0.1875 to 0.1875
- value_projection: bfloat16 [2, 1024, 512], P(None, 'dp', 'tensor'), may hold values from -0.1875 to 0.1875
- w_out: bfloat16 [2, 1024, 1024], P(None, 'tensor', 'dp'), may hold values from -0.75 to 0.75
- moe_gain: bfloat16 [2, 1024], P(None, 'dp'), may hold values from 0.5 to 1.5
- w_router: bfloat16 [2, 1024, 16], P(None, 'dp'), may hold values from -0.09375 to 0.09375
- w_gate: bfloat16 [2, 16, 1024, 512], P(None, None, 'dp', 'tensor'), may hold values from -0.1875 to 0.1875
- w_up: bfloat16 [2, 16, 1024, 512], P(None, None, 'dp', 'tensor'), may hold values from -0.1875 to 0.1875
- w_down: bfloat16 [2, 16, 512, 1024], P(None, None, 'tensor', 'dp'), may hold values from -1 to 1
Outputs:
- result: float32 [8192, 1024], P(('dp', 'tensor'))
- input_grad: float32 [8192, 1024], P(('dp', 'tensor'))
- grad_attn_gain: float32 [2, 1024], P(None, 'dp')
- grad_w_query: float32 [2, 1024, 1024], P(None, 'dp', 'tensor')
- grad_w_key: float32 [2, 1024, 512], P(None, 'dp', 'tensor')
- grad_w_value: float32 [2, 1024, 512], P(None, 'dp', 'tensor')
- grad_w_out: float32 [2, 1024, 1024], P(None, 'tensor', 'dp')
- grad_moe_gain: float32 [2, 1024], P(None, 'dp')
- grad_w_router: float32 [2, 1024, 16], P(None, 'dp')
- grad_w_gate: float32 [2, 16, 1024, 512], P(None, None, 'dp', 'tensor')
- grad_w_up: float32 [2, 16, 1024, 512], P(None, None, 'dp', 'tensor')
- grad_w_down: float32 [2, 16, 512, 1024], P(None, None, 'tensor', 'dp')
The draws below stay inside these ranges and needn't reach their ends.
Inputs may be any that keep to these rules, and one draw needn't show every extreme that they name: `routes`: each row names 8 different experts, and every expert is named by some row.
All inputs are finite; a program needn't handle non-finite values.
Results may differ from the reference program's by a relative error of at most 0.03.
Values may be sent and summed in bfloat16 or wider, within the bound.
No kernel may reach another device: no remote copies, remote signals or barrier semaphores. Data moves between devices by JAX's collectives and lax.ppermute only.
A program may use at most 256 MiB of HBM per device.

```python
import jax
import jax.numpy as jnp
from jax import lax

MODEL_WIDTH = 1024
QUERY_HEADS = 16
KEY_VALUE_HEADS = 8
HEAD_SIZE = 64
FE = 512
TOPK = 8
EXPERTS = 16
LAYER_COUNT = 2
SEQUENCE_LENGTH = 1024
CAP = 512
SEQS = 8
TOKENS = 8192


def steps_of(key, extent, split, smallest, top_value):
    def one(position, shards_of):
        steps = jax.random.uniform(jax.random.fold_in(jax.random.fold_in(key, 6), position), (shards_of,), jnp.float32, smallest / len(split), top_value / len(split))
        return jnp.repeat(jnp.exp(steps), extent[position] // shards_of).reshape((-1,) + (1,) * (len(extent) - position - 1))

    level = one(*split[0])
    for cut in split[1:]:
        level = level * one(*cut)
    return level


def different_ones(rng, rows, number_of, top, lift):
    ranking = jax.random.permutation(jax.random.fold_in(rng, 1), number_of)
    pull = ranking
    for power in range(3):
        pull = pull * pull // number_of
    pull = pull * lift // number_of
    lots = jax.random.randint(jax.random.fold_in(rng, 2), (rows, number_of), 0, 4096) + pull
    holders = jax.random.permutation(jax.random.fold_in(rng, 3), rows)[jnp.arange(number_of) % rows]
    lots = jnp.where(jnp.arange(rows)[:, None] == holders[None, :], 1 << 14, lots)
    merit = lots * number_of + jnp.arange(number_of)
    return lax.top_k(merit.astype(jnp.int32), top)[1].astype(jnp.int32)


def noise(key, dims, width, bound, shards=(), kind=jnp.bfloat16):
    drawn = jax.random.normal(key, dims, jnp.float32) * width
    if len(shards) > 0:
        drawn = steps_of(key, dims, shards, -0.22, 0.18) * drawn
    return jnp.clip(drawn, min=-bound, max=bound).astype(kind)


def setup_inputs(seed: int = 0) -> dict:
    key_of = jax.random.split(jax.random.key(seed), 14)
    tokens_in = noise(key_of[0], (TOKENS, MODEL_WIDTH), 1.0, 6.0, ((0, 32),))
    cotangent = noise(key_of[1], (TOKENS, MODEL_WIDTH), 1.0, 6.0, ((0, 32),))
    routes = different_ones(key_of[2], LAYER_COUNT * TOKENS, EXPERTS, TOPK, 4096).reshape((LAYER_COUNT, TOKENS, TOPK))
    attn_gain = jnp.clip(1.0 + 0.1 * jax.random.normal(key_of[3], (LAYER_COUNT, MODEL_WIDTH), jnp.float32), 0.5, 1.5).astype(jnp.bfloat16)
    w_query = noise(key_of[4], (LAYER_COUNT, MODEL_WIDTH, QUERY_HEADS * HEAD_SIZE), MODEL_WIDTH ** -0.5, 0.1875, ((1, 8), (2, 4)))
    key_projection = noise(key_of[5], (LAYER_COUNT, MODEL_WIDTH, KEY_VALUE_HEADS * HEAD_SIZE), MODEL_WIDTH ** -0.5, 0.1875, ((1, 8), (2, 4)))
    value_projection = noise(key_of[6], (LAYER_COUNT, MODEL_WIDTH, KEY_VALUE_HEADS * HEAD_SIZE), MODEL_WIDTH ** -0.5, 0.1875, ((1, 8), (2, 4)))
    w_out = noise(key_of[7], (LAYER_COUNT, QUERY_HEADS * HEAD_SIZE, MODEL_WIDTH), (QUERY_HEADS * HEAD_SIZE // 16) ** -0.5, 0.75, ((1, 4), (2, 8)))
    moe_gain = jnp.clip(1.0 + 0.1 * jax.random.normal(key_of[8], (LAYER_COUNT, MODEL_WIDTH), jnp.float32), 0.5, 1.5).astype(jnp.bfloat16)
    w_router = noise(key_of[9], (LAYER_COUNT, MODEL_WIDTH, EXPERTS), (4 * MODEL_WIDTH) ** -0.5, 0.09375, ((1, 8),))
    w_gate = noise(key_of[10], (LAYER_COUNT, EXPERTS, MODEL_WIDTH, FE), MODEL_WIDTH ** -0.5, 0.1875, ((2, 8), (3, 4)))
    w_up = noise(key_of[11], (LAYER_COUNT, EXPERTS, MODEL_WIDTH, FE), MODEL_WIDTH ** -0.5, 0.1875, ((2, 8), (3, 4)))
    w_down = noise(key_of[12], (LAYER_COUNT, EXPERTS, FE, MODEL_WIDTH), (FE // 16) ** -0.5, 1.0, ((2, 4), (3, 8)))
    return {"tokens_in": tokens_in, "cotangent": cotangent, "routes": routes, "attn_gain": attn_gain, "w_query": w_query, "key_projection": key_projection, "value_projection": value_projection, "w_out": w_out, "moe_gain": moe_gain, "w_router": w_router, "w_gate": w_gate, "w_up": w_up, "w_down": w_down}


@jax.custom_vjp
def lowered_input(v):
    return lax.optimization_barrier(v.astype(jnp.bfloat16)).astype(jnp.float32)

@jax.custom_vjp
def lowered_gradient(v):
    return v

def low_keep(v):
    return (lowered_input(v), None)

def low_pass(kept, grad):
    return (grad,)

def back_keep(v):
    return (v, None)

def back_low(kept, grad):
    return (lowered_input(grad),)
lowered_input.defvjp(low_keep, low_pass)
lowered_gradient.defvjp(back_keep, back_low)
highest_precision = lax.Precision.HIGHEST
epsilon = 1e-06
rope_base = 10000.0
masked_score = -1e+30

def rms_norm(residual, norm_gain):
    root_scale = lax.rsqrt(lax.optimization_barrier(jnp.mean(residual * residual, axis=-1, keepdims=True)) + epsilon)
    return residual * root_scale * norm_gain

def rope_tables():
    positions = jnp.arange(SEQUENCE_LENGTH, dtype=jnp.float32)
    frequency = rope_base ** (-jnp.arange(0, HEAD_SIZE // 2, dtype=jnp.float32) * 2.0 / HEAD_SIZE)
    angles = positions[:, None] * frequency[None, :]
    return (jnp.cos(angles)[:, None, :], jnp.sin(angles)[:, None, :])

def apply_rotation(heads, cosine_table, sine_values):
    half_width = heads.shape[-1] // 2
    front_half = heads[..., :half_width]
    back_half = heads[..., half_width:]
    return jnp.concatenate([front_half * cosine_table - back_half * sine_values, back_half * cosine_table + front_half * sine_values], axis=-1)

def attend(hidden_state, query_weight, key_matrix, value_matrix, out_weight, cosine_table, sine_values):
    query_group_width = QUERY_HEADS // KEY_VALUE_HEADS
    query_rows = lowered_input(apply_rotation(lowered_gradient(jnp.dot(hidden_state, query_weight, precision=highest_precision)).reshape(SEQUENCE_LENGTH, QUERY_HEADS, HEAD_SIZE), cosine_table, sine_values))
    key_head_rows = lowered_input(apply_rotation(lowered_gradient(jnp.dot(hidden_state, key_matrix, precision=highest_precision)).reshape(SEQUENCE_LENGTH, KEY_VALUE_HEADS, HEAD_SIZE), cosine_table, sine_values))
    value_head_rows = lowered_input(lowered_gradient(jnp.dot(hidden_state, value_matrix, precision=highest_precision))).reshape(SEQUENCE_LENGTH, KEY_VALUE_HEADS, HEAD_SIZE)
    grouped_heads = query_rows.reshape(SEQUENCE_LENGTH, KEY_VALUE_HEADS, query_group_width, HEAD_SIZE)
    scores = lowered_gradient(jnp.einsum('qkgd,ckd->kgqc', grouped_heads, key_head_rows, precision=highest_precision) * HEAD_SIZE ** (-0.5))
    causal = jnp.arange(SEQUENCE_LENGTH)[:, None] >= jnp.arange(SEQUENCE_LENGTH)[None, :]
    scores = jnp.where(causal, scores, masked_score)
    row_max = lax.optimization_barrier(jnp.max(scores, axis=-1, keepdims=True))
    exponent = jnp.exp(scores - row_max)
    probs = exponent / lax.optimization_barrier(jnp.sum(exponent, axis=-1, keepdims=True))
    mixed = jnp.einsum('kgqc,ckd->qkgd', lowered_input(probs), value_head_rows, precision=highest_precision).reshape(SEQUENCE_LENGTH, QUERY_HEADS * HEAD_SIZE)
    mixed = lowered_input(lowered_gradient(mixed))
    return lowered_gradient(jnp.dot(mixed, out_weight, precision=highest_precision))

def mix_experts(hidden_state, route_rows, router_weight, gate_weight, up_weight, down_weight):
    logits = lowered_gradient(jnp.dot(hidden_state, router_weight, precision=highest_precision))
    chosen = jnp.take_along_axis(logits, route_rows, axis=1)
    gate_probs = jax.nn.softmax(chosen, axis=-1)
    flat_routes = route_rows.reshape(-1)
    onehot = (flat_routes[:, None] == jnp.arange(EXPERTS, dtype=jnp.int32)[None, :]).astype(jnp.int32)
    before = jnp.cumsum(onehot, axis=0) - onehot
    slot_place = lax.optimization_barrier(jnp.sum(before * onehot, axis=1))
    target = jnp.where(slot_place < CAP, flat_routes * CAP + slot_place, EXPERTS * CAP)
    token_index = jnp.arange(SEQUENCE_LENGTH * TOPK, dtype=jnp.int32) // TOPK
    source = jnp.full((EXPERTS * CAP,), SEQUENCE_LENGTH, jnp.int32).at[target].set(token_index, mode='drop')
    slot_gate = jnp.zeros((EXPERTS * CAP,), jnp.float32).at[target].set(gate_probs.reshape(-1), mode='drop')
    padded = jnp.concatenate([hidden_state, jnp.zeros((1, MODEL_WIDTH), jnp.float32)], axis=0)
    buffer = padded[source].reshape(EXPERTS, CAP, MODEL_WIDTH)
    gate_part = lowered_gradient(jnp.einsum('ecd,edf->ecf', buffer, gate_weight, precision=highest_precision))
    up_part = lowered_gradient(jnp.einsum('ecd,edf->ecf', buffer, up_weight, precision=highest_precision))
    active = lowered_input(slot_gate.reshape(EXPERTS, CAP, 1) * jax.nn.silu(gate_part) * up_part)
    produced = jnp.einsum('ecf,efd->ecd', active, down_weight, precision=highest_precision).reshape(EXPERTS * CAP, MODEL_WIDTH)
    combined = jnp.zeros((SEQUENCE_LENGTH + 1, MODEL_WIDTH), jnp.float32).at[source].add(produced)
    return lowered_gradient(combined[:SEQUENCE_LENGTH])

def forward(residual, attn_gain, w_query, key_projection, value_projection, w_out, moe_gain, w_router, w_gate, w_up, w_down, routes):
    cosine_table, sine_values = rope_tables()
    for layer_index in range(LAYER_COUNT):
        hidden_state = lowered_input(rms_norm(residual, attn_gain[layer_index]))

        def attend_one(piece):
            return attend(piece, w_query[layer_index], key_projection[layer_index], value_projection[layer_index], w_out[layer_index], cosine_table, sine_values)
        branch = lax.map(jax.checkpoint(attend_one), hidden_state.reshape(SEQS, SEQUENCE_LENGTH, MODEL_WIDTH))
        residual = residual + branch.reshape(TOKENS, MODEL_WIDTH)
        hidden_state = lowered_input(rms_norm(residual, moe_gain[layer_index]))

        def mix_one(pieces):
            return mix_experts(pieces[0], pieces[1], w_router[layer_index], w_gate[layer_index], w_up[layer_index], w_down[layer_index])
        branch = lax.map(jax.checkpoint(mix_one), (hidden_state.reshape(SEQS, SEQUENCE_LENGTH, MODEL_WIDTH), routes[layer_index].reshape(SEQS, SEQUENCE_LENGTH, TOPK)))
        residual = residual + branch.reshape(TOKENS, MODEL_WIDTH)
    return residual

def reference(tokens_in, cotangent, routes, attn_gain, w_query, key_projection, value_projection, w_out, moe_gain, w_router, w_gate, w_up, w_down):

    def run(residual, gain_attn, query_weight, key_matrix, value_matrix, out_weight, gain_moe, router_weight, gate_weight, up_weight, down_weight):
        return forward(residual, gain_attn, query_weight, key_matrix, value_matrix, out_weight, gain_moe, router_weight, gate_weight, up_weight, down_weight, routes)
    result, pullback = jax.vjp(run, tokens_in.astype(jnp.float32), attn_gain.astype(jnp.float32), w_query.astype(jnp.float32), key_projection.astype(jnp.float32), value_projection.astype(jnp.float32), w_out.astype(jnp.float32), moe_gain.astype(jnp.float32), w_router.astype(jnp.float32), w_gate.astype(jnp.float32), w_up.astype(jnp.float32), w_down.astype(jnp.float32))
    grads = pullback(cotangent.astype(jnp.float32))
    return (result, grads[0], grads[1], grads[2], grads[3], grads[4], grads[5], grads[6], grads[7], grads[8], grads[9], grads[10])
```

```python
import jax
import jax.numpy as jnp
from jax import lax
from jax.experimental import pallas as pl
from jax.experimental.pallas import tpu as pltpu
from jax.sharding import PartitionSpec as P

HEAD_SIZE = 64
TOPK = 8
EXPERTS = 16
LAYER_COUNT = 2
SEQUENCE_LENGTH = 1024
CAP = 512

EPSILON = 1e-06
ROPE_BASE = 10000.0
MASKED = -1e30
LANES = 128
BLOCK = 256
F32 = jnp.float32
BF16 = jnp.bfloat16
MIB = 1 << 20


def dot_nn(a, b):
    return lax.dot_general(a, b, (((1,), (0,)), ((), ())), preferred_element_type=F32)


def dot_nt(a, b):
    return lax.dot_general(a, b, (((1,), (1,)), ((), ())), preferred_element_type=F32)


def dot_tn(a, b):
    return lax.dot_general(a, b, (((0,), (0,)), ((), ())), preferred_element_type=F32)


def half_mask(rows):
    return lax.broadcasted_iota(jnp.int32, (rows, LANES), 1) < HEAD_SIZE


def swap_halves(t):
    lane = lax.broadcasted_iota(jnp.int32, t.shape, 1) % HEAD_SIZE
    return jnp.where(
        lane < HEAD_SIZE // 2,
        pltpu.roll(t, LANES - HEAD_SIZE // 2, 1),
        pltpu.roll(t, HEAD_SIZE // 2, 1),
    )


def both_halves(t, low):
    turned = pltpu.roll(t, HEAD_SIZE, 1)
    return jnp.where(low, t, turned), jnp.where(low, turned, t)


def diagonal_mask(scores, row_block):
    rows = lax.broadcasted_iota(jnp.int32, scores.shape, 0) % BLOCK + row_block * BLOCK
    columns = lax.broadcasted_iota(jnp.int32, scores.shape, 1)
    return jnp.where(rows >= columns, scores, MASKED)


def attention_forward_kernel(
    x_ref, w_ref, cos_ref, sin_ref, wo_ref, q_ref, k_ref, v_ref, o_ref, lse_ref, out_ref, kd, vd
):
    rows = x_ref.shape[0]
    low = half_mask(BLOCK)
    lane = lax.broadcasted_iota(jnp.int32, (BLOCK, LANES), 1)
    for i in range(rows // BLOCK):
        here = pl.ds(i * BLOCK, BLOCK)
        qkv = dot_nn(x_ref[here, :], w_ref[...])
        cos, sin = cos_ref[here, :], sin_ref[here, :]

        def rope(t):
            return t * cos + swap_halves(t) * sin

        q = [(rope(qkv[:, j * LANES : (j + 1) * LANES]) * HEAD_SIZE ** (-0.5)).astype(BF16) for j in range(2)]
        k = rope(qkv[:, 2 * LANES : 3 * LANES])
        v = qkv[:, 3 * LANES :]
        k_ref[here, :] = k.astype(BF16)
        v_ref[here, :] = v.astype(BF16)
        for j, (kj, vj) in enumerate(zip(both_halves(k, low), both_halves(v, low))):
            kd[j, here, :] = kj.astype(BF16)
            vd[j, here, :] = vj.astype(BF16)
        context = (i + 1) * BLOCK
        lse_all = jnp.zeros((BLOCK, LANES), F32)
        for j in range(2):
            q_ref[here, j * LANES : (j + 1) * LANES] = q[j]
            zero = jnp.zeros_like(q[j])
            stacked = jnp.concatenate([jnp.where(low, q[j], zero), jnp.where(low, zero, q[j])], axis=0)
            scores = diagonal_mask(dot_nt(stacked, kd[j, :context, :]), i)
            row_max = jnp.max(scores, axis=1, keepdims=True)
            weights = jnp.exp(scores - row_max)
            total = jnp.sum(weights, axis=1, keepdims=True)
            lse = row_max + jnp.log(total)
            probs = (weights * (1.0 / total)).astype(BF16)
            mixed = dot_nn(probs, vd[j, :context, :])
            o_ref[here, j * LANES : (j + 1) * LANES] = jnp.where(low, mixed[:BLOCK], mixed[BLOCK:]).astype(BF16)
            lse_all = jnp.where(lane == 2 * j, lse[:BLOCK], lse_all)
            lse_all = jnp.where(lane == 2 * j + 1, lse[BLOCK:], lse_all)
        lse_ref[here, :] = lse_all
        out_ref[here, :] = dot_nt(o_ref[here, :], wo_ref[...]).astype(BF16)


def attention_forward(x, w, cos, sin, wo):
    rows, width = x.shape
    shapes = (
        jax.ShapeDtypeStruct((rows, 2 * LANES), BF16),
        jax.ShapeDtypeStruct((rows, LANES), BF16),
        jax.ShapeDtypeStruct((rows, LANES), BF16),
        jax.ShapeDtypeStruct((rows, 2 * LANES), BF16),
        jax.ShapeDtypeStruct((rows, LANES), F32),
        jax.ShapeDtypeStruct((rows, width), BF16),
    )
    return pl.pallas_call(
        attention_forward_kernel,
        out_shape=shapes,
        scratch_shapes=[pltpu.VMEM((2, rows, LANES), BF16)] * 2,
        compiler_params=pltpu.CompilerParams(vmem_limit_bytes=40 * MIB),
        cost_estimate=pl.CostEstimate(
            flops=2 * rows * width * 768 + 4 * rows * rows * 256, bytes_accessed=12 * MIB, transcendentals=rows * rows * 2
        ),
        name="attention_forward",
    )(x, w, cos, sin, wo)


def attention_backward_kernel(
    dy_ref, wo_ref, q_ref, k_ref, v_ref, lse_ref, w_ref, cos_ref, sin_ref, dqkv_ref, dx_ref, kd, vd, dk, dv
):
    rows = dy_ref.shape[0]
    low = half_mask(BLOCK)
    for i in range(rows // BLOCK):
        here = pl.ds(i * BLOCK, BLOCK)
        k, v = k_ref[here, :].astype(F32), v_ref[here, :].astype(F32)
        for j, (kj, vj) in enumerate(zip(both_halves(k, low), both_halves(v, low))):
            kd[j, here, :] = kj.astype(BF16)
            vd[j, here, :] = vj.astype(BF16)
    dk[...] = jnp.zeros_like(dk)
    dv[...] = jnp.zeros_like(dv)
    for i in range(rows // BLOCK):
        here = pl.ds(i * BLOCK, BLOCK)
        cos, sin = cos_ref[here, :], sin_ref[here, :]
        grad_mixed = dot_nn(dy_ref[here, :], wo_ref[...]).astype(BF16)
        lse_all = lse_ref[here, :]
        context = (i + 1) * BLOCK
        for j in range(2):
            qj = q_ref[here, j * LANES : (j + 1) * LANES]
            gj = grad_mixed[:, j * LANES : (j + 1) * LANES]
            zero = jnp.zeros_like(qj)
            q2 = jnp.concatenate([jnp.where(low, qj, zero), jnp.where(low, zero, qj)], axis=0)
            g2 = jnp.concatenate([jnp.where(low, gj, zero), jnp.where(low, zero, gj)], axis=0)
            lse = jnp.concatenate([lse_all[:, 2 * j : 2 * j + 1], lse_all[:, 2 * j + 1 : 2 * j + 2]], axis=0)
            scores = diagonal_mask(dot_nt(q2, kd[j, :context, :]), i)
            probs = jnp.exp(scores - lse)
            grad_probs = dot_nt(g2, vd[j, :context, :])
            inner = jnp.sum(probs * grad_probs, axis=1, keepdims=True)
            grad_scores = (probs * (grad_probs - inner)).astype(BF16)
            dk[j, :context, :] += dot_tn(grad_scores, q2)
            dv[j, :context, :] += dot_tn(probs.astype(BF16), g2)
            grad_q = dot_nn(grad_scores, kd[j, :context, :])
            grad_q = jnp.where(low, grad_q[:BLOCK], grad_q[BLOCK:]) * HEAD_SIZE ** (-0.5)
            dqkv_ref[here, j * LANES : (j + 1) * LANES] = (grad_q * cos - swap_halves(grad_q) * sin).astype(BF16)
    for i in range(rows // BLOCK):
        here = pl.ds(i * BLOCK, BLOCK)
        cos, sin = cos_ref[here, :], sin_ref[here, :]

        def folded(total):
            pair = [total[j, here, :] for j in range(2)]
            pair = [t + pltpu.roll(t, HEAD_SIZE, 1) for t in pair]
            return jnp.where(low, pair[0], pair[1])

        grad_k = folded(dk)
        dqkv_ref[here, 2 * LANES : 3 * LANES] = (grad_k * cos - swap_halves(grad_k) * sin).astype(BF16)
        dqkv_ref[here, 3 * LANES :] = folded(dv).astype(BF16)
        dx_ref[here, :] = dot_nt(dqkv_ref[here, :], w_ref[...]).astype(BF16)


def attention_backward(dy, wo, q, k, v, lse, w, cos, sin):
    rows, width = dy.shape
    return pl.pallas_call(
        attention_backward_kernel,
        out_shape=(jax.ShapeDtypeStruct((rows, 4 * LANES), BF16), jax.ShapeDtypeStruct((rows, width), BF16)),
        scratch_shapes=[pltpu.VMEM((2, rows, LANES), BF16)] * 2 + [pltpu.VMEM((2, rows, LANES), F32)] * 2,
        compiler_params=pltpu.CompilerParams(vmem_limit_bytes=48 * MIB),
        cost_estimate=pl.CostEstimate(
            flops=2 * rows * width * 768 + 10 * rows * rows * 256, bytes_accessed=12 * MIB, transcendentals=rows * rows * 2
        ),
        name="attention_backward",
    )(dy, wo, q, k, v, lse, w, cos, sin)


HIDDEN_STEP = 512


def spread_gates(gates, step, count):
    lane = lax.broadcasted_iota(jnp.int32, gates.shape, 1)
    return [
        jnp.sum(jnp.where(lane == step * count + n, gates, 0.0), axis=1, keepdims=True) for n in range(count)
    ]


def experts_forward_kernel(x_ref, wg_ref, wu_ref, wd_ref, gates_ref, g_ref, u_ref, out_ref, total):
    step = pl.program_id(0)
    count = g_ref.shape[1] // LANES
    columns = spread_gates(gates_ref[...], step, count)
    x = x_ref[...]
    parts = []
    for n in range(count // 2):
        at = slice(2 * n * LANES, (2 * n + 2) * LANES)
        g = dot_nn(x, wg_ref[:, at])
        u = dot_nn(x, wu_ref[:, at])
        g_ref[:, at] = g.astype(BF16)
        u_ref[:, at] = u.astype(BF16)
        shape = (x.shape[0], LANES)
        gate = jnp.concatenate(
            [jnp.broadcast_to(columns[2 * n], shape), jnp.broadcast_to(columns[2 * n + 1], shape)], axis=1
        )
        parts.append((gate * (g * jax.nn.sigmoid(g)) * u).astype(BF16))
    product = dot_nt(jnp.concatenate(parts, axis=1), wd_ref[...])

    @pl.when(step == 0)
    def _():
        total[...] = product

    @pl.when(step > 0)
    def _():
        total[...] += product

    @pl.when(step == pl.num_programs(0) - 1)
    def _():
        out_ref[...] = total[...].astype(BF16)


def experts_forward(x, wg, wu, wd, gates):
    rows, width = x.shape
    hidden = wg.shape[1]
    whole = lambda s: (0, 0)
    tile = lambda s: (0, s)
    weight = pl.BlockSpec((width, HIDDEN_STEP), tile)
    saved = pl.BlockSpec((rows, HIDDEN_STEP), tile)
    return pl.pallas_call(
        experts_forward_kernel,
        grid=(hidden // HIDDEN_STEP,),
        in_specs=[pl.BlockSpec((rows, width), whole), weight, weight, weight, pl.BlockSpec((rows, LANES), whole)],
        out_specs=[saved, saved, pl.BlockSpec((rows, width), whole)],
        out_shape=(
            jax.ShapeDtypeStruct((rows, hidden), BF16),
            jax.ShapeDtypeStruct((rows, hidden), BF16),
            jax.ShapeDtypeStruct((rows, width), BF16),
        ),
        scratch_shapes=[pltpu.VMEM((rows, width), F32)],
        compiler_params=pltpu.CompilerParams(vmem_limit_bytes=48 * MIB),
        cost_estimate=pl.CostEstimate(
            flops=6 * rows * width * hidden, bytes_accessed=26 * MIB, transcendentals=rows * hidden
        ),
        name="experts_forward",
    )(x, wg, wu, wd, gates)


def experts_backward_kernel(
    dy_ref, wg_ref, wu_ref, wd_ref, g_ref, u_ref, gates_ref, a_ref, dg_ref, du_ref, out_ref, total, slots
):
    step = pl.program_id(0)
    width = dy_ref.shape[1]
    rows = dy_ref.shape[0]
    count = g_ref.shape[1] // LANES
    columns = spread_gates(gates_ref[...], step, count)
    lane = lax.broadcasted_iota(jnp.int32, (rows, LANES), 1)
    dy = dy_ref[...]
    sums = jnp.zeros((rows, LANES), F32)
    for n in range(count // 2):
        at = slice(2 * n * LANES, (2 * n + 2) * LANES)
        shape = (rows, LANES)
        gate = jnp.concatenate(
            [jnp.broadcast_to(columns[2 * n], shape), jnp.broadcast_to(columns[2 * n + 1], shape)], axis=1
        )
        da = dot_nn(dy, wd_ref[:, at])
        g = g_ref[:, at].astype(F32)
        u = u_ref[:, at].astype(F32)
        logistic = jax.nn.sigmoid(g)
        swished = g * logistic
        product = swished * u
        a_ref[:, at] = (gate * product).astype(BF16)
        inner = da * product
        for m in range(2):
            total_slot = jnp.sum(inner[:, m * LANES : (m + 1) * LANES], axis=1, keepdims=True)
            sums = jnp.where(lane == step * count + 2 * n + m, total_slot, sums)
        scaled = gate * da
        dg_ref[:, at] = (scaled * u * logistic * (1.0 + g * (1.0 - logistic))).astype(BF16)
        du_ref[:, at] = (scaled * swished).astype(BF16)
    product = dot_nt(dg_ref[...], wg_ref[...]) + dot_nt(du_ref[...], wu_ref[...])

    @pl.when(step == 0)
    def _():
        total[...] = product
        slots[...] = sums

    @pl.when(step > 0)
    def _():
        total[...] += product
        slots[...] += sums

    @pl.when(step == pl.num_programs(0) - 1)
    def _():
        out_ref[:, :width] = total[...].astype(BF16)
        out_ref[:, width:] = slots[...].astype(BF16)


def experts_backward(dy, wg, wu, wd, g, u, gates):
    rows, width = dy.shape
    hidden = wg.shape[1]
    whole = lambda s: (0, 0)
    tile = lambda s: (0, s)
    weight = pl.BlockSpec((width, HIDDEN_STEP), tile)
    saved = pl.BlockSpec((rows, HIDDEN_STEP), tile)
    return pl.pallas_call(
        experts_backward_kernel,
        grid=(hidden // HIDDEN_STEP,),
        in_specs=[
            pl.BlockSpec((rows, width), whole),
            weight,
            weight,
            weight,
            saved,
            saved,
            pl.BlockSpec((rows, LANES), whole),
        ],
        out_specs=[saved, saved, saved, pl.BlockSpec((rows, width + LANES), whole)],
        out_shape=(
            jax.ShapeDtypeStruct((rows, hidden), BF16),
            jax.ShapeDtypeStruct((rows, hidden), BF16),
            jax.ShapeDtypeStruct((rows, hidden), BF16),
            jax.ShapeDtypeStruct((rows, width + LANES), BF16),
        ),
        scratch_shapes=[pltpu.VMEM((rows, width), F32), pltpu.VMEM((rows, LANES), F32)],
        compiler_params=pltpu.CompilerParams(vmem_limit_bytes=56 * MIB),
        cost_estimate=pl.CostEstimate(
            flops=6 * rows * width * hidden, bytes_accessed=38 * MIB, transcendentals=rows * hidden
        ),
        name="experts_backward",
    )(dy, wg, wu, wd, g, u, gates)


def normalize(residual, gain):
    scale = lax.rsqrt(jnp.mean(residual * residual, axis=-1, keepdims=True) + EPSILON)
    normed = residual * scale
    return normed, scale, (normed * gain).astype(BF16)


def normalize_back(grad_hidden, normed, scale, gain):
    grad_normed = grad_hidden * gain
    inner_mean = jnp.mean(grad_normed * normed, axis=-1, keepdims=True)
    return scale * (grad_normed - normed * inner_mean)


def rope_tables(row_count):
    positions = (jnp.arange(row_count, dtype=jnp.int32) % SEQUENCE_LENGTH).astype(F32)
    frequency = ROPE_BASE ** (-jnp.arange(0, HEAD_SIZE // 2, dtype=F32) * 2.0 / HEAD_SIZE)
    angles = positions[:, None] * frequency[None, :]
    cos, sin = jnp.cos(angles), jnp.sin(angles)
    return jnp.concatenate([cos] * 4, axis=1), jnp.concatenate([-sin, sin] * 2, axis=1)


def route_masks(routes):
    lane = lax.broadcasted_iota(jnp.int32, (routes.shape[0], LANES), 1)
    chosen = routes[:, 0:1] == lane
    for k in range(1, TOPK):
        chosen = chosen | (routes[:, k : k + 1] == lane)
    low = chosen.astype(BF16)
    rows = routes.shape[0]
    earlier = (
        lax.broadcasted_iota(jnp.int32, (rows, rows), 0) > lax.broadcasted_iota(jnp.int32, (rows, rows), 1)
    ).astype(BF16)
    before = dot_nn(earlier, low)
    kept = chosen & (before < CAP)
    return chosen.astype(F32), kept.astype(F32)


def gate_probs_of(hidden, router, chosen):
    logits = jnp.where(chosen > 0, dot_nn(hidden, router), MASKED)
    raised = jnp.exp(logits - jnp.max(logits, axis=-1, keepdims=True)) * chosen
    return raised / jnp.sum(raised, axis=-1, keepdims=True)


def swap_with(values, bit):
    size = lax.axis_size("tensor")
    return lax.ppermute(values, "tensor", [(i, i ^ bit) for i in range(size)])


def widen(values):
    rows = values.shape[0]
    size = lax.axis_size("tensor")
    me = lax.axis_index("tensor")
    pieces = [(0, values)]
    bit = size // 2
    while bit:
        pieces = pieces + [(code ^ bit, swap_with(piece, bit)) for code, piece in pieces]
        bit //= 2
    whole = jnp.zeros((rows * size, values.shape[1]), values.dtype)
    for code, piece in pieces:
        whole = lax.dynamic_update_slice(whole, piece, ((me ^ code) * rows, 0))
    return whole


def narrow(values):
    size = lax.axis_size("tensor")
    me = lax.axis_index("tensor")
    rows = values.shape[0] // size
    pieces = {
        code: lax.dynamic_slice_in_dim(values, (me ^ code) * rows, rows, 0).astype(F32) for code in range(size)
    }
    bit = 1
    while bit < size:
        kept = {}
        for code in sorted(pieces, reverse=True):
            if not code & bit:
                other = swap_with(pieces[code ^ bit].astype(BF16), bit)
                kept[code] = pieces[code] + other.astype(F32)
        pieces = kept
        bit *= 2
    return pieces[0]


def sum_over_tensor(values):
    bit = 1
    while bit < lax.axis_size("tensor"):
        values = values + swap_with(values, bit)
        bit *= 2
    return values


def local(
    tokens_in,
    cotangent,
    routes,
    attn_gain,
    w_query,
    key_projection,
    value_projection,
    w_out,
    moe_gain,
    w_router,
    w_gate,
    w_up,
    w_down,
):
    rows_own = tokens_in.shape[0]
    size = lax.axis_size("tensor")
    group_rows = rows_own * size
    own_start = lax.axis_index("tensor") * rows_own
    depth = w_query.shape[1]
    q_columns, kv_columns, o_columns = w_query.shape[2], key_projection.shape[2], w_out.shape[1]
    cos, sin = rope_tables(group_rows)
    masks = [route_masks(routes[layer]) for layer in range(LAYER_COUNT)]

    def gather(values):
        return lax.all_gather(values, "dp", axis=0, tiled=True)

    def scatter(values):
        return lax.psum_scatter(values.astype(BF16), "dp", scatter_dimension=0, tiled=True).astype(F32)

    def own_rows(values):
        return lax.dynamic_slice_in_dim(values, own_start, rows_own, 0)

    packs, shards = [], []
    for layer in range(LAYER_COUNT):
        small = jnp.concatenate(
            [
                w_router[layer],
                attn_gain[layer][:, None],
                moe_gain[layer][:, None],
                jnp.zeros((depth, LANES - EXPERTS - 2), BF16),
            ],
            axis=1,
        )
        pack = jnp.concatenate(
            [w_query[layer], key_projection[layer], value_projection[layer], w_out[layer].T, small], axis=1
        )
        gate_shard = w_gate[layer].transpose(1, 0, 2).reshape(depth, -1)
        up_shard = w_up[layer].transpose(1, 0, 2).reshape(depth, -1)
        down_shard = w_down[layer].reshape(-1, depth).T
        shards.append((pack, gate_shard, up_shard, down_shard))
    weights = []
    for layer in range(LAYER_COUNT):
        pack, gate_weight, up_weight, down_weight = (gather(shard) for shard in shards[layer])
        qkv_end = q_columns + 2 * kv_columns
        small = pack[:, qkv_end + o_columns :]
        lane = lax.broadcasted_iota(jnp.int32, (1, LANES), 1)
        weights.append(
            (
                pack[:, :qkv_end],
                pack[:, qkv_end : qkv_end + o_columns],
                jnp.where(lane < EXPERTS, small, jnp.zeros_like(small)),
                small[:, EXPERTS].astype(F32)[None, :],
                small[:, EXPERTS + 1].astype(F32)[None, :],
                gate_weight,
                up_weight,
                down_weight,
            )
        )

    residual = tokens_in.astype(F32)
    tokens_all = widen(tokens_in)
    grad_all = widen(cotangent)
    records = []
    for layer in range(LAYER_COUNT):
        qkv_weight, out_weight, router, gain_attn, gain_moe, gate_weight, up_weight, down_weight = weights[layer]
        chosen, kept = masks[layer]
        if layer == 0:
            hidden_attn = normalize(tokens_all.astype(F32), gain_attn)[2]
        else:
            hidden_attn = widen(normalize(residual, gain_attn)[2])
        before_attn = residual
        q, k, v, mixed, lse, attn_part = attention_forward(hidden_attn, qkv_weight, cos, sin, out_weight)
        residual = residual + narrow(attn_part)
        before_moe = residual
        low_moe = normalize(residual, gain_moe)[2]
        hidden_moe = widen(low_moe)
        probs = gate_probs_of(hidden_moe, router, chosen)
        gates = probs * kept
        g, u, moe_part = experts_forward(hidden_moe, gate_weight, up_weight, down_weight, gates)
        residual = residual + narrow(moe_part)
        records.append(
            (before_attn, hidden_attn, q, k, v, mixed, lse, before_moe, low_moe, hidden_moe, probs, gates, g, u)
        )
    grad = cotangent.astype(F32)
    outputs = []
    for layer in reversed(range(LAYER_COUNT)):
        qkv_weight, out_weight, router, gain_attn, gain_moe, gate_weight, up_weight, down_weight = weights[layer]
        before_attn, hidden_attn, q, k, v, mixed, lse, before_moe, low_moe, hidden_moe, probs, gates, g, u = records[
            layer
        ]
        kept = masks[layer][1]
        if layer < LAYER_COUNT - 1:
            grad_all = widen(grad.astype(BF16))
        active, grad_gate, grad_up, moe_part = experts_backward(
            grad_all, gate_weight, up_weight, down_weight, g, u, gates
        )
        grad_down_weight = scatter(dot_tn(grad_all, active))
        grad_gate_weight = scatter(dot_tn(hidden_moe, grad_gate))
        grad_up_weight = scatter(dot_tn(hidden_moe, grad_up))
        own = narrow(moe_part)
        width = residual.shape[1]
        grad_moe_own, grad_pairs = own[:, :width], own[:, width:] * own_rows(kept)
        own_probs = own_rows(probs)
        grad_chosen = own_probs * (grad_pairs - jnp.sum(own_probs * grad_pairs, axis=-1, keepdims=True))
        grad_logits = grad_chosen.astype(BF16)
        grad_router = dot_tn(low_moe, grad_logits)
        grad_moe_own = grad_moe_own + dot_nt(grad_logits, router)
        normed_moe, scale_moe, _ = normalize(before_moe, gain_moe)
        grad = grad + normalize_back(grad_moe_own, normed_moe, scale_moe, gain_moe)
        grad_all = widen(grad.astype(BF16))
        grad_qkv, attn_part = attention_backward(grad_all, out_weight, q, k, v, lse, qkv_weight, cos, sin)
        grad_pack = scatter(
            jnp.concatenate(
                [
                    dot_tn(hidden_attn, grad_qkv).astype(BF16),
                    dot_tn(grad_all, mixed).astype(BF16),
                    grad_router.astype(BF16),
                ],
                axis=1,
            )
        )
        normed_attn, scale_attn, _ = normalize(before_attn, gain_attn)
        grad = grad + normalize_back(narrow(attn_part), normed_attn, scale_attn, gain_attn)

        pack, gate_shard, up_shard, _ = shards[layer]
        pack = pack.astype(F32)
        qkv_end = q_columns + 2 * kv_columns
        attn_term = jnp.sum(pack[:, :qkv_end] * grad_pack[:, :qkv_end], axis=1, keepdims=True)
        moe_term = jnp.sum(
            gate_shard.astype(F32) * grad_gate_weight + up_shard.astype(F32) * grad_up_weight, axis=1, keepdims=True
        )
        lane = lax.broadcasted_iota(jnp.int32, (depth, LANES), 1)
        stats = grad_pack[:, qkv_end + o_columns :]
        stats = jnp.where(lane == EXPERTS, attn_term, jnp.where(lane == EXPERTS + 1, moe_term, stats))
        stats = sum_over_tensor(stats)
        router_grad = stats[:, :EXPERTS]
        router_own = pack[:, qkv_end + o_columns : qkv_end + o_columns + EXPERTS]
        attn_gain_grad = stats[:, EXPERTS] / attn_gain[layer].astype(F32)
        moe_gain_grad = (stats[:, EXPERTS + 1] + jnp.sum(router_own * router_grad, axis=1)) / moe_gain[layer].astype(
            F32
        )
        outputs.insert(
            0,
            (
                attn_gain_grad,
                grad_pack[:, :q_columns],
                grad_pack[:, q_columns : q_columns + kv_columns],
                grad_pack[:, q_columns + kv_columns : qkv_end],
                grad_pack[:, qkv_end : qkv_end + o_columns].T,
                moe_gain_grad,
                router_grad,
                grad_gate_weight.reshape(depth, EXPERTS, -1).transpose(1, 0, 2),
                grad_up_weight.reshape(depth, EXPERTS, -1).transpose(1, 0, 2),
                grad_down_weight.T.reshape(EXPERTS, -1, depth),
            ),
        )
    stacked = tuple(jnp.stack([terms[n] for terms in outputs]) for n in range(10))
    return (residual, grad) + stacked


def solution(mesh):
    placed = (
        P(("dp", "tensor"), None),
        P(("dp", "tensor"), None),
        P(None, "dp", None),
        P(None, "dp"),
        P(None, "dp", "tensor"),
        P(None, "dp", "tensor"),
        P(None, "dp", "tensor"),
        P(None, "tensor", "dp"),
        P(None, "dp"),
        P(None, "dp", None),
        P(None, None, "dp", "tensor"),
        P(None, None, "dp", "tensor"),
        P(None, None, "tensor", "dp"),
    )
    return jax.shard_map(
        local,
        mesh=mesh,
        in_specs=placed,
        out_specs=(
            P(("dp", "tensor"), None),
            P(("dp", "tensor"), None),
            P(None, "dp"),
            P(None, "dp", "tensor"),
            P(None, "dp", "tensor"),
            P(None, "dp", "tensor"),
            P(None, "tensor", "dp"),
            P(None, "dp"),
            P(None, "dp", None),
            P(None, None, "dp", "tensor"),
            P(None, None, "dp", "tensor"),
            P(None, None, "tensor", "dp"),
        ),
        check_vma=False,
    )
```

```python
import jax
import jax.numpy as jnp
from jax import lax
from jax.experimental import pallas as pl
from jax.experimental.pallas import tpu as pltpu
from jax.sharding import PartitionSpec as P

HEAD_SIZE = 64
TOPK = 8
EXPERTS = 16
LAYER_COUNT = 2
SEQUENCE_LENGTH = 1024
CAP = 512

EPSILON = 1e-06
ROPE_BASE = 10000.0
MASKED = -1e30
LANES = 128
BLOCK = 256
F32 = jnp.float32
BF16 = jnp.bfloat16
MIB = 1 << 20


def dot_nn(a, b):
    return lax.dot_general(a, b, (((1,), (0,)), ((), ())), preferred_element_type=F32)


def dot_nt(a, b):
    return lax.dot_general(a, b, (((1,), (1,)), ((), ())), preferred_element_type=F32)


def dot_tn(a, b):
    return lax.dot_general(a, b, (((0,), (0,)), ((), ())), preferred_element_type=F32)


def half_mask(rows):
    return lax.broadcasted_iota(jnp.int32, (rows, LANES), 1) < HEAD_SIZE


def swap_halves(t):
    lane = lax.broadcasted_iota(jnp.int32, t.shape, 1) % HEAD_SIZE
    return jnp.where(
        lane < HEAD_SIZE // 2,
        pltpu.roll(t, LANES - HEAD_SIZE // 2, 1),
        pltpu.roll(t, HEAD_SIZE // 2, 1),
    )


def both_halves(t, low):
    turned = pltpu.roll(t, HEAD_SIZE, 1)
    return jnp.where(low, t, turned), jnp.where(low, turned, t)


def diagonal_mask(scores, row_block):
    rows = lax.broadcasted_iota(jnp.int32, scores.shape, 0) % BLOCK + row_block * BLOCK
    columns = lax.broadcasted_iota(jnp.int32, scores.shape, 1)
    return jnp.where(rows >= columns, scores, MASKED)


def attention_forward_kernel(
    x_ref, w_ref, cos_ref, sin_ref, wo_ref, q_ref, k_ref, v_ref, o_ref, lse_ref, out_ref, kd, vd
):
    rows = x_ref.shape[0]
    low = half_mask(BLOCK)
    lane = lax.broadcasted_iota(jnp.int32, (BLOCK, LANES), 1)
    for i in range(rows // BLOCK):
        here = pl.ds(i * BLOCK, BLOCK)
        qkv = dot_nn(x_ref[here, :], w_ref[...])
        cos, sin = cos_ref[here, :], sin_ref[here, :]

        def rope(t):
            return t * cos + swap_halves(t) * sin

        q = [(rope(qkv[:, j * LANES : (j + 1) * LANES]) * HEAD_SIZE ** (-0.5)).astype(BF16) for j in range(2)]
        k = rope(qkv[:, 2 * LANES : 3 * LANES])
        v = qkv[:, 3 * LANES :]
        k_ref[here, :] = k.astype(BF16)
        v_ref[here, :] = v.astype(BF16)
        for j, (kj, vj) in enumerate(zip(both_halves(k, low), both_halves(v, low))):
            kd[j, here, :] = kj.astype(BF16)
            vd[j, here, :] = vj.astype(BF16)
        context = (i + 1) * BLOCK
        lse_all = jnp.zeros((BLOCK, LANES), F32)
        for j in range(2):
            q_ref[here, j * LANES : (j + 1) * LANES] = q[j]
            zero = jnp.zeros_like(q[j])
            stacked = jnp.concatenate([jnp.where(low, q[j], zero), jnp.where(low, zero, q[j])], axis=0)
            scores = diagonal_mask(dot_nt(stacked, kd[j, :context, :]), i)
            row_max = jnp.max(scores, axis=1, keepdims=True)
            weights = jnp.exp(scores - row_max)
            total = jnp.sum(weights, axis=1, keepdims=True)
            lse = row_max + jnp.log(total)
            probs = (weights * (1.0 / total)).astype(BF16)
            mixed = dot_nn(probs, vd[j, :context, :])
            o_ref[here, j * LANES : (j + 1) * LANES] = jnp.where(low, mixed[:BLOCK], mixed[BLOCK:]).astype(BF16)
            lse_all = jnp.where(lane == 2 * j, lse[:BLOCK], lse_all)
            lse_all = jnp.where(lane == 2 * j + 1, lse[BLOCK:], lse_all)
        lse_ref[here, :] = lse_all
        out_ref[here, :] = dot_nt(o_ref[here, :], wo_ref[...]).astype(BF16)


def attention_forward(x, w, cos, sin, wo):
    rows, width = x.shape
    shapes = (
        jax.ShapeDtypeStruct((rows, 2 * LANES), BF16),
        jax.ShapeDtypeStruct((rows, LANES), BF16),
        jax.ShapeDtypeStruct((rows, LANES), BF16),
        jax.ShapeDtypeStruct((rows, 2 * LANES), BF16),
        jax.ShapeDtypeStruct((rows, LANES), F32),
        jax.ShapeDtypeStruct((rows, width), BF16),
    )
    return pl.pallas_call(
        attention_forward_kernel,
        out_shape=shapes,
        scratch_shapes=[pltpu.VMEM((2, rows, LANES), BF16)] * 2,
        compiler_params=pltpu.CompilerParams(vmem_limit_bytes=40 * MIB),
        cost_estimate=pl.CostEstimate(
            flops=2 * rows * width * 768 + 4 * rows * rows * 256, bytes_accessed=12 * MIB, transcendentals=rows * rows * 2
        ),
        name="attention_forward",
    )(x, w, cos, sin, wo)


def attention_backward_kernel(
    dy_ref, wo_ref, q_ref, k_ref, v_ref, lse_ref, w_ref, cos_ref, sin_ref, dqkv_ref, dx_ref, kd, vd, dk, dv
):
    rows = dy_ref.shape[0]
    low = half_mask(BLOCK)
    for i in range(rows // BLOCK):
        here = pl.ds(i * BLOCK, BLOCK)
        k, v = k_ref[here, :].astype(F32), v_ref[here, :].astype(F32)
        for j, (kj, vj) in enumerate(zip(both_halves(k, low), both_halves(v, low))):
            kd[j, here, :] = kj.astype(BF16)
            vd[j, here, :] = vj.astype(BF16)
    dk[...] = jnp.zeros_like(dk)
    dv[...] = jnp.zeros_like(dv)
    for i in range(rows // BLOCK):
        here = pl.ds(i * BLOCK, BLOCK)
        cos, sin = cos_ref[here, :], sin_ref[here, :]
        grad_mixed = dot_nn(dy_ref[here, :], wo_ref[...]).astype(BF16)
        lse_all = lse_ref[here, :]
        context = (i + 1) * BLOCK
        for j in range(2):
            qj = q_ref[here, j * LANES : (j + 1) * LANES]
            gj = grad_mixed[:, j * LANES : (j + 1) * LANES]
            zero = jnp.zeros_like(qj)
            q2 = jnp.concatenate([jnp.where(low, qj, zero), jnp.where(low, zero, qj)], axis=0)
            g2 = jnp.concatenate([jnp.where(low, gj, zero), jnp.where(low, zero, gj)], axis=0)
            lse = jnp.concatenate([lse_all[:, 2 * j : 2 * j + 1], lse_all[:, 2 * j + 1 : 2 * j + 2]], axis=0)
            scores = diagonal_mask(dot_nt(q2, kd[j, :context, :]), i)
            probs = jnp.exp(scores - lse)
            grad_probs = dot_nt(g2, vd[j, :context, :])
            inner = jnp.sum(probs * grad_probs, axis=1, keepdims=True)
            grad_scores = (probs * (grad_probs - inner)).astype(BF16)
            dk[j, :context, :] += dot_tn(grad_scores, q2)
            dv[j, :context, :] += dot_tn(probs.astype(BF16), g2)
            grad_q = dot_nn(grad_scores, kd[j, :context, :])
            grad_q = jnp.where(low, grad_q[:BLOCK], grad_q[BLOCK:]) * HEAD_SIZE ** (-0.5)
            dqkv_ref[here, j * LANES : (j + 1) * LANES] = (grad_q * cos - swap_halves(grad_q) * sin).astype(BF16)
    for i in range(rows // BLOCK):
        here = pl.ds(i * BLOCK, BLOCK)
        cos, sin = cos_ref[here, :], sin_ref[here, :]

        def folded(total):
            pair = [total[j, here, :] for j in range(2)]
            pair = [t + pltpu.roll(t, HEAD_SIZE, 1) for t in pair]
            return jnp.where(low, pair[0], pair[1])

        grad_k = folded(dk)
        dqkv_ref[here, 2 * LANES : 3 * LANES] = (grad_k * cos - swap_halves(grad_k) * sin).astype(BF16)
        dqkv_ref[here, 3 * LANES :] = folded(dv).astype(BF16)
        dx_ref[here, :] = dot_nt(dqkv_ref[here, :], w_ref[...]).astype(BF16)


def attention_backward(dy, wo, q, k, v, lse, w, cos, sin):
    rows, width = dy.shape
    return pl.pallas_call(
        attention_backward_kernel,
        out_shape=(jax.ShapeDtypeStruct((rows, 4 * LANES), BF16), jax.ShapeDtypeStruct((rows, width), BF16)),
        scratch_shapes=[pltpu.VMEM((2, rows, LANES), BF16)] * 2 + [pltpu.VMEM((2, rows, LANES), F32)] * 2,
        compiler_params=pltpu.CompilerParams(vmem_limit_bytes=48 * MIB),
        cost_estimate=pl.CostEstimate(
            flops=2 * rows * width * 768 + 10 * rows * rows * 256, bytes_accessed=12 * MIB, transcendentals=rows * rows * 2
        ),
        name="attention_backward",
    )(dy, wo, q, k, v, lse, w, cos, sin)


HIDDEN_STEP = 512


def spread_gates(gates, step, count):
    lane = lax.broadcasted_iota(jnp.int32, gates.shape, 1)
    return [
        jnp.sum(jnp.where(lane == step * count + n, gates, 0.0), axis=1, keepdims=True) for n in range(count)
    ]


def experts_up_kernel(x_ref, wg_ref, wu_ref, gates_ref, g_ref, u_ref, a_ref):
    step = pl.program_id(0)
    count = g_ref.shape[1] // LANES
    columns = spread_gates(gates_ref[...], step, count)
    x = x_ref[...]
    shape = (x.shape[0], LANES)
    for n in range(count // 2):
        at = slice(2 * n * LANES, (2 * n + 2) * LANES)
        g = dot_nn(x, wg_ref[:, at])
        u = dot_nn(x, wu_ref[:, at])
        g_ref[:, at] = g.astype(BF16)
        u_ref[:, at] = u.astype(BF16)
        gate = jnp.concatenate(
            [jnp.broadcast_to(columns[2 * n], shape), jnp.broadcast_to(columns[2 * n + 1], shape)], axis=1
        )
        a_ref[:, at] = (gate * (g * jax.nn.sigmoid(g)) * u).astype(BF16)


def experts_up(x, wg, wu, gates):
    rows, width = x.shape
    hidden = wg.shape[1]
    whole = lambda s: (0, 0)
    tile = lambda s: (0, s)
    weight = pl.BlockSpec((width, HIDDEN_STEP), tile)
    saved = pl.BlockSpec((rows, HIDDEN_STEP), tile)
    return pl.pallas_call(
        experts_up_kernel,
        grid=(hidden // HIDDEN_STEP,),
        in_specs=[pl.BlockSpec((rows, width), whole), weight, weight, pl.BlockSpec((rows, LANES), whole)],
        out_specs=[saved] * 3,
        out_shape=(jax.ShapeDtypeStruct((rows, hidden), BF16),) * 3,
        compiler_params=pltpu.CompilerParams(vmem_limit_bytes=48 * MIB),
        cost_estimate=pl.CostEstimate(
            flops=4 * rows * width * hidden, bytes_accessed=22 * MIB, transcendentals=rows * hidden
        ),
        name="experts_up",
    )(x, wg, wu, gates)


def experts_backward_kernel(
    dy_ref, wg_ref, wu_ref, wd_ref, g_ref, u_ref, gates_ref, dg_ref, du_ref, out_ref, total, slots
):
    step = pl.program_id(0)
    width = dy_ref.shape[1]
    rows = dy_ref.shape[0]
    count = g_ref.shape[1] // LANES
    columns = spread_gates(gates_ref[...], step, count)
    lane = lax.broadcasted_iota(jnp.int32, (rows, LANES), 1)
    dy = dy_ref[...]
    sums = jnp.zeros((rows, LANES), F32)
    for n in range(count // 2):
        at = slice(2 * n * LANES, (2 * n + 2) * LANES)
        shape = (rows, LANES)
        gate = jnp.concatenate(
            [jnp.broadcast_to(columns[2 * n], shape), jnp.broadcast_to(columns[2 * n + 1], shape)], axis=1
        )
        da = dot_nn(dy, wd_ref[:, at])
        g = g_ref[:, at].astype(F32)
        u = u_ref[:, at].astype(F32)
        logistic = jax.nn.sigmoid(g)
        swished = g * logistic
        inner = da * swished * u
        for m in range(2):
            total_slot = jnp.sum(inner[:, m * LANES : (m + 1) * LANES], axis=1, keepdims=True)
            sums = jnp.where(lane == step * count + 2 * n + m, total_slot, sums)
        scaled = gate * da
        dg_ref[:, at] = (scaled * u * logistic * (1.0 + g * (1.0 - logistic))).astype(BF16)
        du_ref[:, at] = (scaled * swished).astype(BF16)
    product = dot_nt(dg_ref[...], wg_ref[...]) + dot_nt(du_ref[...], wu_ref[...])

    @pl.when(step == 0)
    def _():
        total[...] = product
        slots[...] = sums

    @pl.when(step > 0)
    def _():
        total[...] += product
        slots[...] += sums

    @pl.when(step == pl.num_programs(0) - 1)
    def _():
        out_ref[:, :width] = total[...].astype(BF16)
        out_ref[:, width:] = slots[...].astype(BF16)


def experts_backward(dy, wg, wu, wd, g, u, gates):
    rows, width = dy.shape
    hidden = wg.shape[1]
    whole = lambda s: (0, 0)
    tile = lambda s: (0, s)
    weight = pl.BlockSpec((width, HIDDEN_STEP), tile)
    saved = pl.BlockSpec((rows, HIDDEN_STEP), tile)
    return pl.pallas_call(
        experts_backward_kernel,
        grid=(hidden // HIDDEN_STEP,),
        in_specs=[
            pl.BlockSpec((rows, width), whole),
            weight,
            weight,
            weight,
            saved,
            saved,
            pl.BlockSpec((rows, LANES), whole),
        ],
        out_specs=[saved, saved, pl.BlockSpec((rows, width + LANES), whole)],
        out_shape=(
            jax.ShapeDtypeStruct((rows, hidden), BF16),
            jax.ShapeDtypeStruct((rows, hidden), BF16),
            jax.ShapeDtypeStruct((rows, width + LANES), BF16),
        ),
        scratch_shapes=[pltpu.VMEM((rows, width), F32), pltpu.VMEM((rows, LANES), F32)],
        compiler_params=pltpu.CompilerParams(vmem_limit_bytes=56 * MIB),
        cost_estimate=pl.CostEstimate(
            flops=6 * rows * width * hidden, bytes_accessed=38 * MIB, transcendentals=rows * hidden
        ),
        name="experts_backward",
    )(dy, wg, wu, wd, g, u, gates)


def normalize(residual, gain):
    scale = lax.rsqrt(jnp.mean(residual * residual, axis=-1, keepdims=True) + EPSILON)
    normed = residual * scale
    return normed, scale, (normed * gain).astype(BF16)


def normalize_back(grad_hidden, normed, scale, gain):
    grad_normed = grad_hidden * gain
    inner_mean = jnp.mean(grad_normed * normed, axis=-1, keepdims=True)
    return scale * (grad_normed - normed * inner_mean)


def rope_tables(row_count):
    positions = (jnp.arange(row_count, dtype=jnp.int32) % SEQUENCE_LENGTH).astype(F32)
    frequency = ROPE_BASE ** (-jnp.arange(0, HEAD_SIZE // 2, dtype=F32) * 2.0 / HEAD_SIZE)
    angles = positions[:, None] * frequency[None, :]
    cos, sin = jnp.cos(angles), jnp.sin(angles)
    return jnp.concatenate([cos] * 4, axis=1), jnp.concatenate([-sin, sin] * 2, axis=1)


def route_masks(routes):
    lane = lax.broadcasted_iota(jnp.int32, (routes.shape[0], LANES), 1)
    chosen = routes[:, 0:1] == lane
    for k in range(1, TOPK):
        chosen = chosen | (routes[:, k : k + 1] == lane)
    low = chosen.astype(BF16)
    rows = routes.shape[0]
    earlier = (
        lax.broadcasted_iota(jnp.int32, (rows, rows), 0) > lax.broadcasted_iota(jnp.int32, (rows, rows), 1)
    ).astype(BF16)
    before = dot_nn(earlier, low)
    kept = chosen & (before < CAP)
    return chosen.astype(F32), kept.astype(F32)


def gate_probs_of(hidden, router, chosen):
    logits = jnp.where(chosen > 0, dot_nn(hidden, router), MASKED)
    raised = jnp.exp(logits - jnp.max(logits, axis=-1, keepdims=True)) * chosen
    return raised / jnp.sum(raised, axis=-1, keepdims=True)


def swap_with(values, bit):
    size = lax.axis_size("tensor")
    return lax.ppermute(values, "tensor", [(i, i ^ bit) for i in range(size)])


def widen(values):
    rows = values.shape[0]
    size = lax.axis_size("tensor")
    me = lax.axis_index("tensor")
    pieces = [(0, values)]
    bit = size // 2
    while bit:
        pieces = pieces + [(code ^ bit, swap_with(piece, bit)) for code, piece in pieces]
        bit //= 2
    whole = jnp.zeros((rows * size, values.shape[1]), values.dtype)
    for code, piece in pieces:
        whole = lax.dynamic_update_slice(whole, piece, ((me ^ code) * rows, 0))
    return whole


def narrow(values):
    size = lax.axis_size("tensor")
    me = lax.axis_index("tensor")
    rows = values.shape[0] // size
    pieces = {
        code: lax.dynamic_slice_in_dim(values, (me ^ code) * rows, rows, 0).astype(F32) for code in range(size)
    }
    bit = 1
    while bit < size:
        kept = {}
        for code in sorted(pieces, reverse=True):
            if not code & bit:
                other = swap_with(pieces[code ^ bit].astype(BF16), bit)
                kept[code] = pieces[code] + other.astype(F32)
        pieces = kept
        bit *= 2
    return pieces[0]


def sum_over_tensor(values):
    bit = 1
    while bit < lax.axis_size("tensor"):
        values = values + swap_with(values, bit)
        bit *= 2
    return values


def after(values, *earlier):
    return lax.optimization_barrier((values,) + earlier)[0]


class Ring:
    def __init__(self, depth):
        self.size = lax.axis_size("dp")
        self.native = self.size % 2 == 1 or depth % LANES != 0 or self.size > 8
        self.depth = depth
        size = self.size
        order = list(range(0, size, 2)) + list(range(size - 1 - size % 2, 0, -2))
        self.order = order
        self.forward = [(order[i], order[(i + 1) % size]) for i in range(size)]
        self.backward = [(b, a) for a, b in self.forward]
        place = [order.index(i) for i in range(size)]
        self.place = jnp.asarray(place, jnp.int32)[lax.axis_index("dp")]
        self.chains = [None, None]
        self.turn = 0

    def send(self, values, way):
        return lax.ppermute(values, "dp", self.forward if way > 0 else self.backward)

    def queued(self, values):
        token = self.chains[self.turn]
        return values if token is None else after(values, *token)

    def finished(self, *token):
        self.chains[self.turn] = token
        self.turn = 1 - self.turn

    def gather(self, own):
        if self.native:
            return lax.all_gather(own, "dp", axis=0, tiled=True)
        way = 1 if self.turn == 0 else -1
        half = self.size // 2
        own = self.queued(own)
        blocks = {0: own}
        near, far = own, own
        for k in range(1, half + 1):
            near = self.send(near, way)
            blocks[(way * k) % self.size] = near
            if k < half:
                far = self.send(far, -way)
                blocks[(-way * k) % self.size] = far
        self.finished(near, far)
        return jnp.concatenate([blocks[k] for k in range(self.size)], axis=0)

    def scatter(self, values):
        values = values.astype(BF16)
        if self.native:
            return lax.psum_scatter(values, "dp", scatter_dimension=0, tiled=True).astype(F32)
        way = 1 if self.turn == 0 else -1
        half = self.size // 2

        def block(k):
            at = (k % self.size) * self.depth
            return values[at : at + self.depth]

        near = self.send(self.queued(block(-way * half)), way)
        far = self.send(self.queued(block(way * (half - 1))), -way)
        for k in range(half - 1, 0, -1):
            near = self.send((near.astype(F32) + block(-way * k).astype(F32)).astype(BF16), way)
            if k > 1:
                far = self.send((far.astype(F32) + block(way * (k - 1)).astype(F32)).astype(BF16), -way)
        self.finished(near, far)
        return block(0).astype(F32) + near.astype(F32) + far.astype(F32)

    def relative(self, values):
        if self.native:
            return values
        order = jnp.asarray(self.order, jnp.int32)
        width = values.shape[1] // self.size
        return jnp.concatenate(
            [
                lax.dynamic_slice_in_dim(values, order[(self.place - k) % self.size] * width, width, 1)
                for k in range(self.size)
            ],
            axis=1,
        )

    def absolute(self, values):
        if self.native:
            return values
        width = values.shape[1] // self.size
        return jnp.concatenate(
            [
                lax.dynamic_slice_in_dim(values, ((self.place - self.order.index(i)) % self.size) * width, width, 1)
                for i in range(self.size)
            ],
            axis=1,
        )


def local(
    tokens_in,
    cotangent,
    routes,
    attn_gain,
    w_query,
    key_projection,
    value_projection,
    w_out,
    moe_gain,
    w_router,
    w_gate,
    w_up,
    w_down,
):
    rows_own = tokens_in.shape[0]
    size = lax.axis_size("tensor")
    group_rows = rows_own * size
    own_start = lax.axis_index("tensor") * rows_own
    depth = w_query.shape[1]
    q_columns, kv_columns, o_columns = w_query.shape[2], key_projection.shape[2], w_out.shape[1]
    cos, sin = rope_tables(group_rows)
    masks = [route_masks(routes[layer]) for layer in range(LAYER_COUNT)]

    ring = Ring(depth)

    def own_rows(values):
        return lax.dynamic_slice_in_dim(values, own_start, rows_own, 0)

    packs, shards = [], []
    for layer in range(LAYER_COUNT):
        small = jnp.concatenate(
            [
                w_router[layer],
                attn_gain[layer][:, None],
                moe_gain[layer][:, None],
                jnp.zeros((depth, LANES - EXPERTS - 2), BF16),
            ],
            axis=1,
        )
        pack = jnp.concatenate(
            [w_query[layer], key_projection[layer], value_projection[layer], w_out[layer].T, small], axis=1
        )
        gate_shard = w_gate[layer].transpose(1, 0, 2).reshape(depth, -1)
        up_shard = w_up[layer].transpose(1, 0, 2).reshape(depth, -1)
        down_shard = w_down[layer].reshape(-1, depth).T
        shards.append((pack, gate_shard, up_shard, down_shard))
    weights = []
    for layer in range(LAYER_COUNT):
        pack, gate_weight, up_weight, down_weight = (ring.gather(shard) for shard in shards[layer])
        qkv_end = q_columns + 2 * kv_columns
        small = pack[:, qkv_end + o_columns :]
        lane = lax.broadcasted_iota(jnp.int32, (1, LANES), 1)
        weights.append(
            (
                pack[:, :qkv_end],
                pack[:, qkv_end : qkv_end + o_columns],
                jnp.where(lane < EXPERTS, small, jnp.zeros_like(small)),
                small[:, EXPERTS].astype(F32)[None, :],
                small[:, EXPERTS + 1].astype(F32)[None, :],
                gate_weight,
                up_weight,
                down_weight,
            )
        )

    tokens_in, cotangent = ring.relative(tokens_in), ring.relative(cotangent)
    residual = tokens_in.astype(F32)
    tokens_all = widen(tokens_in)
    grad_all = widen(cotangent)
    records = []
    for layer in range(LAYER_COUNT):
        qkv_weight, out_weight, router, gain_attn, gain_moe, gate_weight, up_weight, down_weight = weights[layer]
        chosen, kept = masks[layer]
        if layer == 0:
            hidden_attn = normalize(tokens_all.astype(F32), gain_attn)[2]
        else:
            hidden_attn = widen(normalize(residual, gain_attn)[2])
        before_attn = residual
        q, k, v, mixed, lse, attn_part = attention_forward(hidden_attn, qkv_weight, cos, sin, out_weight)
        residual = residual + narrow(attn_part)
        before_moe = residual
        low_moe = normalize(residual, gain_moe)[2]
        hidden_moe = widen(low_moe)
        probs = gate_probs_of(hidden_moe, router, chosen)
        gates = probs * kept
        g, u, active = experts_up(hidden_moe, gate_weight, up_weight, gates)
        residual = residual + narrow(dot_nt(active, down_weight).astype(BF16))
        records.append(
            (before_attn, hidden_attn, q, k, v, mixed, lse, before_moe, low_moe, hidden_moe, probs, gates, g, u, active)
        )
    grad = cotangent.astype(F32)
    outputs = []
    for layer in reversed(range(LAYER_COUNT)):
        qkv_weight, out_weight, router, gain_attn, gain_moe, gate_weight, up_weight, down_weight = weights[layer]
        before_attn, hidden_attn, q, k, v, mixed, lse, before_moe, low_moe, hidden_moe, probs, gates, g, u, active = (
            records[layer]
        )
        kept = masks[layer][1]
        if layer < LAYER_COUNT - 1:
            grad_all = widen(grad.astype(BF16))
        grad_down_weight = ring.scatter(dot_tn(grad_all, active))
        grad_gate, grad_up, moe_part = experts_backward(
            grad_all, gate_weight, up_weight, down_weight, g, u, gates
        )
        grad_gate_weight = ring.scatter(dot_tn(hidden_moe, grad_gate))
        grad_up_weight = ring.scatter(dot_tn(hidden_moe, grad_up))
        own = narrow(moe_part)
        width = residual.shape[1]
        grad_moe_own, grad_pairs = own[:, :width], own[:, width:] * own_rows(kept)
        own_probs = own_rows(probs)
        grad_chosen = own_probs * (grad_pairs - jnp.sum(own_probs * grad_pairs, axis=-1, keepdims=True))
        grad_logits = grad_chosen.astype(BF16)
        grad_router = dot_tn(low_moe, grad_logits)
        grad_moe_own = grad_moe_own + dot_nt(grad_logits, router)
        normed_moe, scale_moe, _ = normalize(before_moe, gain_moe)
        grad = grad + normalize_back(grad_moe_own, normed_moe, scale_moe, gain_moe)
        grad_all = widen(grad.astype(BF16))
        grad_qkv, attn_part = attention_backward(grad_all, out_weight, q, k, v, lse, qkv_weight, cos, sin)
        grad_pack = ring.scatter(
            jnp.concatenate(
                [
                    dot_tn(hidden_attn, grad_qkv).astype(BF16),
                    dot_tn(grad_all, mixed).astype(BF16),
                    grad_router.astype(BF16),
                ],
                axis=1,
            )
        )
        normed_attn, scale_attn, _ = normalize(before_attn, gain_attn)
        grad = grad + normalize_back(narrow(attn_part), normed_attn, scale_attn, gain_attn)

        pack, gate_shard, up_shard, _ = shards[layer]
        pack = pack.astype(F32)
        qkv_end = q_columns + 2 * kv_columns
        attn_term = jnp.sum(pack[:, :qkv_end] * grad_pack[:, :qkv_end], axis=1, keepdims=True)
        moe_term = jnp.sum(
            gate_shard.astype(F32) * grad_gate_weight + up_shard.astype(F32) * grad_up_weight, axis=1, keepdims=True
        )
        lane = lax.broadcasted_iota(jnp.int32, (depth, LANES), 1)
        stats = grad_pack[:, qkv_end + o_columns :]
        stats = jnp.where(lane == EXPERTS, attn_term, jnp.where(lane == EXPERTS + 1, moe_term, stats))
        stats = sum_over_tensor(stats)
        router_grad = stats[:, :EXPERTS]
        router_own = pack[:, qkv_end + o_columns : qkv_end + o_columns + EXPERTS]
        attn_gain_grad = stats[:, EXPERTS] / attn_gain[layer].astype(F32)
        moe_gain_grad = (stats[:, EXPERTS + 1] + jnp.sum(router_own * router_grad, axis=1)) / moe_gain[layer].astype(
            F32
        )
        outputs.insert(
            0,
            (
                attn_gain_grad,
                grad_pack[:, :q_columns],
                grad_pack[:, q_columns : q_columns + kv_columns],
                grad_pack[:, q_columns + kv_columns : qkv_end],
                grad_pack[:, qkv_end : qkv_end + o_columns].T,
                moe_gain_grad,
                router_grad,
                grad_gate_weight.reshape(depth, EXPERTS, -1).transpose(1, 0, 2),
                grad_up_weight.reshape(depth, EXPERTS, -1).transpose(1, 0, 2),
                grad_down_weight.T.reshape(EXPERTS, -1, depth),
            ),
        )
    stacked = tuple(jnp.stack([terms[n] for terms in outputs]) for n in range(10))
    return (ring.absolute(residual), ring.absolute(grad)) + stacked


def solution(mesh):
    placed = (
        P(("dp", "tensor"), None),
        P(("dp", "tensor"), None),
        P(None, "dp", None),
        P(None, "dp"),
        P(None, "dp", "tensor"),
        P(None, "dp", "tensor"),
        P(None, "dp", "tensor"),
        P(None, "tensor", "dp"),
        P(None, "dp"),
        P(None, "dp", None),
        P(None, None, "dp", "tensor"),
        P(None, None, "dp", "tensor"),
        P(None, None, "tensor", "dp"),
    )
    return jax.shard_map(
        local,
        mesh=mesh,
        in_specs=placed,
        out_specs=(
            P(("dp", "tensor"), None),
            P(("dp", "tensor"), None),
            P(None, "dp"),
            P(None, "dp", "tensor"),
            P(None, "dp", "tensor"),
            P(None, "dp", "tensor"),
            P(None, "tensor", "dp"),
            P(None, "dp"),
            P(None, "dp", None),
            P(None, None, "dp", "tensor"),
            P(None, None, "dp", "tensor"),
            P(None, None, "tensor", "dp"),
        ),
        check_vma=False,
    )
```

```python
import jax
import jax.numpy as jnp
from jax import lax
from jax.experimental import pallas as pl
from jax.experimental.pallas import tpu as pltpu
from jax.sharding import PartitionSpec as P

HEAD_SIZE = 64
TOPK = 8
EXPERTS = 16
LAYER_COUNT = 2
SEQUENCE_LENGTH = 1024
CAP = 512

EPSILON = 1e-06
ROPE_BASE = 10000.0
MASKED = -1e30
LANES = 128
BLOCK = 256
F32 = jnp.float32
BF16 = jnp.bfloat16
MIB = 1 << 20
QKV = 4 * LANES
OUT_END = 6 * LANES
PACK = 8 * LANES


def dot_nn(a, b):
    return lax.dot_general(a, b, (((1,), (0,)), ((), ())), preferred_element_type=F32)


def dot_nt(a, b):
    return lax.dot_general(a, b, (((1,), (1,)), ((), ())), preferred_element_type=F32)


def dot_tn(a, b):
    return lax.dot_general(a, b, (((0,), (0,)), ((), ())), preferred_element_type=F32)


def place_of(me, block):
    code = me ^ block
    return pl.multiple_of(((code & 1) * 2 + (code >> 1)) * BLOCK, BLOCK)


def half_mask(rows):
    return lax.broadcasted_iota(jnp.int32, (rows, LANES), 1) < HEAD_SIZE


def swap_halves(t):
    lane = lax.broadcasted_iota(jnp.int32, t.shape, 1) % HEAD_SIZE
    return jnp.where(
        lane < HEAD_SIZE // 2,
        pltpu.roll(t, LANES - HEAD_SIZE // 2, 1),
        pltpu.roll(t, HEAD_SIZE // 2, 1),
    )


def both_halves(t, low):
    turned = pltpu.roll(t, HEAD_SIZE, 1)
    return jnp.where(low, t, turned), jnp.where(low, turned, t)


def diagonal_mask(scores, row_block):
    rows = lax.broadcasted_iota(jnp.int32, scores.shape, 0) % BLOCK + row_block * BLOCK
    columns = lax.broadcasted_iota(jnp.int32, scores.shape, 1)
    return jnp.where(rows >= columns, scores, MASKED)


def attention_forward_kernel(
    me_ref, x_ref, pa_ref, pb_ref, cos_ref, sin_ref, q_ref, k_ref, v_ref, o_ref, lse_ref, out_ref, kd, vd
):
    rows, width = x_ref.shape
    half = width // 2
    low = half_mask(BLOCK)
    lane = lax.broadcasted_iota(jnp.int32, (BLOCK, LANES), 1)
    for i in range(rows // BLOCK):
        here = pl.ds(i * BLOCK, BLOCK)
        there = pl.ds(place_of(me_ref[0], i), BLOCK)
        qkv = dot_nn(x_ref[there, :half], pa_ref[:, :QKV]) + dot_nn(x_ref[there, half:], pb_ref[:, :QKV])
        cos, sin = cos_ref[here, :], sin_ref[here, :]

        def rope(t):
            return t * cos + swap_halves(t) * sin

        q = [(rope(qkv[:, j * LANES : (j + 1) * LANES]) * HEAD_SIZE ** (-0.5)).astype(BF16) for j in range(2)]
        k = rope(qkv[:, 2 * LANES : 3 * LANES])
        v = qkv[:, 3 * LANES :]
        k_ref[here, :] = k.astype(BF16)
        v_ref[here, :] = v.astype(BF16)
        for j, (kj, vj) in enumerate(zip(both_halves(k, low), both_halves(v, low))):
            kd[j, here, :] = kj.astype(BF16)
            vd[j, here, :] = vj.astype(BF16)
        context = (i + 1) * BLOCK
        lse_all = jnp.zeros((BLOCK, LANES), F32)
        outs = []
        for j in range(2):
            q_ref[here, j * LANES : (j + 1) * LANES] = q[j]
            zero = jnp.zeros_like(q[j])
            stacked = jnp.concatenate([jnp.where(low, q[j], zero), jnp.where(low, zero, q[j])], axis=0)
            scores = diagonal_mask(dot_nt(stacked, kd[j, :context, :]), i)
            row_max = jnp.max(scores, axis=1, keepdims=True)
            weights = jnp.exp(scores - row_max)
            total = jnp.sum(weights, axis=1, keepdims=True)
            lse = row_max + jnp.log(total)
            probs = (weights * (1.0 / total)).astype(BF16)
            mixed = dot_nn(probs, vd[j, :context, :])
            outs.append(jnp.where(low, mixed[:BLOCK], mixed[BLOCK:]).astype(BF16))
            lse_all = jnp.where(lane == 2 * j, lse[:BLOCK], lse_all)
            lse_all = jnp.where(lane == 2 * j + 1, lse[BLOCK:], lse_all)
        lse_ref[here, :] = lse_all
        mixed = jnp.concatenate(outs, axis=1)
        o_ref[there, :] = mixed
        out_ref[there, :half] = dot_nt(mixed, pa_ref[:, QKV:OUT_END]).astype(BF16)
        out_ref[there, half:] = dot_nt(mixed, pb_ref[:, QKV:OUT_END]).astype(BF16)


VMEM_SPEC = pl.BlockSpec(memory_space=pltpu.VMEM)
SMEM_SPEC = pl.BlockSpec(memory_space=pltpu.SMEM)


def attention_forward(me, x, pack, cos, sin):
    rows, width = x.shape
    shapes = (
        jax.ShapeDtypeStruct((rows, 2 * LANES), BF16),
        jax.ShapeDtypeStruct((rows, LANES), BF16),
        jax.ShapeDtypeStruct((rows, LANES), BF16),
        jax.ShapeDtypeStruct((rows, 2 * LANES), BF16),
        jax.ShapeDtypeStruct((rows, LANES), F32),
        jax.ShapeDtypeStruct((rows, width), BF16),
    )
    return pl.pallas_call(
        attention_forward_kernel,
        out_shape=shapes,
        in_specs=[SMEM_SPEC] + [VMEM_SPEC] * 5,
        scratch_shapes=[pltpu.VMEM((2, rows, LANES), BF16)] * 2,
        compiler_params=pltpu.CompilerParams(vmem_limit_bytes=40 * MIB),
        cost_estimate=pl.CostEstimate(
            flops=2 * rows * width * 768 + 4 * rows * rows * 256, bytes_accessed=12 * MIB, transcendentals=rows * rows * 2
        ),
        name="attention_forward",
    )(me, x, *pack, cos, sin)


def attention_backward_kernel(
    me_ref, dy_ref, pa_ref, pb_ref, q_ref, k_ref, v_ref, lse_ref, cos_ref, sin_ref, dqkv_ref, dx_ref, kd, vd, dk, dv
):
    rows, width = dy_ref.shape
    half = width // 2
    low = half_mask(BLOCK)
    for i in range(rows // BLOCK):
        here = pl.ds(i * BLOCK, BLOCK)
        k, v = k_ref[here, :].astype(F32), v_ref[here, :].astype(F32)
        for j, (kj, vj) in enumerate(zip(both_halves(k, low), both_halves(v, low))):
            kd[j, here, :] = kj.astype(BF16)
            vd[j, here, :] = vj.astype(BF16)
    dk[...] = jnp.zeros_like(dk)
    dv[...] = jnp.zeros_like(dv)
    for i in range(rows // BLOCK):
        here = pl.ds(i * BLOCK, BLOCK)
        there = pl.ds(place_of(me_ref[0], i), BLOCK)
        cos, sin = cos_ref[here, :], sin_ref[here, :]
        grad_mixed = (
            dot_nn(dy_ref[there, :half], pa_ref[:, QKV:OUT_END]) + dot_nn(dy_ref[there, half:], pb_ref[:, QKV:OUT_END])
        ).astype(BF16)
        lse_all = lse_ref[here, :]
        context = (i + 1) * BLOCK
        for j in range(2):
            qj = q_ref[here, j * LANES : (j + 1) * LANES]
            gj = grad_mixed[:, j * LANES : (j + 1) * LANES]
            zero = jnp.zeros_like(qj)
            q2 = jnp.concatenate([jnp.where(low, qj, zero), jnp.where(low, zero, qj)], axis=0)
            g2 = jnp.concatenate([jnp.where(low, gj, zero), jnp.where(low, zero, gj)], axis=0)
            lse = jnp.concatenate([lse_all[:, 2 * j : 2 * j + 1], lse_all[:, 2 * j + 1 : 2 * j + 2]], axis=0)
            scores = diagonal_mask(dot_nt(q2, kd[j, :context, :]), i)
            probs = jnp.exp(scores - lse)
            grad_probs = dot_nt(g2, vd[j, :context, :])
            inner = jnp.sum(probs * grad_probs, axis=1, keepdims=True)
            grad_scores = (probs * (grad_probs - inner)).astype(BF16)
            dk[j, :context, :] += dot_tn(grad_scores, q2)
            dv[j, :context, :] += dot_tn(probs.astype(BF16), g2)
            grad_q = dot_nn(grad_scores, kd[j, :context, :])
            grad_q = jnp.where(low, grad_q[:BLOCK], grad_q[BLOCK:]) * HEAD_SIZE ** (-0.5)
            dqkv_ref[there, j * LANES : (j + 1) * LANES] = (grad_q * cos - swap_halves(grad_q) * sin).astype(BF16)
    for i in range(rows // BLOCK):
        here = pl.ds(i * BLOCK, BLOCK)
        there = pl.ds(place_of(me_ref[0], i), BLOCK)
        cos, sin = cos_ref[here, :], sin_ref[here, :]

        def folded(total):
            pair = [total[j, here, :] for j in range(2)]
            pair = [t + pltpu.roll(t, HEAD_SIZE, 1) for t in pair]
            return jnp.where(low, pair[0], pair[1])

        grad_k = folded(dk)
        dqkv_ref[there, 2 * LANES : 3 * LANES] = (grad_k * cos - swap_halves(grad_k) * sin).astype(BF16)
        dqkv_ref[there, 3 * LANES :] = folded(dv).astype(BF16)
        grad_qkv = dqkv_ref[there, :]
        dx_ref[there, :half] = dot_nt(grad_qkv, pa_ref[:, :QKV]).astype(BF16)
        dx_ref[there, half:] = dot_nt(grad_qkv, pb_ref[:, :QKV]).astype(BF16)


def attention_backward(me, dy, pack, q, k, v, lse, cos, sin):
    rows, width = dy.shape
    return pl.pallas_call(
        attention_backward_kernel,
        out_shape=(jax.ShapeDtypeStruct((rows, QKV), BF16), jax.ShapeDtypeStruct((rows, width), BF16)),
        in_specs=[SMEM_SPEC] + [VMEM_SPEC] * 9,
        scratch_shapes=[pltpu.VMEM((2, rows, LANES), BF16)] * 2 + [pltpu.VMEM((2, rows, LANES), F32)] * 2,
        compiler_params=pltpu.CompilerParams(vmem_limit_bytes=48 * MIB),
        cost_estimate=pl.CostEstimate(
            flops=2 * rows * width * 768 + 10 * rows * rows * 256, bytes_accessed=12 * MIB, transcendentals=rows * rows * 2
        ),
        name="attention_backward",
    )(me, dy, *pack, q, k, v, lse, cos, sin)


def attention_weights_kernel(x_ref, dqkv_ref, dy_ref, o_ref, low_ref, dl_ref, out_ref):
    half = x_ref.shape[1] // 2
    count = OUT_END + LANES
    for n in range(2):
        at = slice(n * half, (n + 1) * half)
        to = n * count
        out_ref[:, to : to + QKV] = dot_tn(x_ref[:, at], dqkv_ref[...]).astype(BF16)
        out_ref[:, to + QKV : to + OUT_END] = dot_tn(dy_ref[:, at], o_ref[...]).astype(BF16)
        out_ref[:, to + OUT_END : to + count] = dot_tn(low_ref[:, at], dl_ref[...]).astype(BF16)


def attention_weights(x, dqkv, dy, o, low, dl):
    rows, width = x.shape
    return pl.pallas_call(
        attention_weights_kernel,
        out_shape=jax.ShapeDtypeStruct((width // 2, 2 * (OUT_END + LANES)), BF16),
        in_specs=[VMEM_SPEC] * 6,
        compiler_params=pltpu.CompilerParams(vmem_limit_bytes=32 * MIB),
        cost_estimate=pl.CostEstimate(flops=2 * rows * width * 800, bytes_accessed=9 * MIB, transcendentals=0),
        name="attention_weights",
    )(x, dqkv, dy, o, low, dl)


UP_STEP = 256
BACK_STEP = 512


def spread_gates(gates, first, count):
    lane = lax.broadcasted_iota(jnp.int32, gates.shape, 1)
    return [jnp.sum(jnp.where(lane == first + n, gates, 0.0), axis=1, keepdims=True) for n in range(count)]


def pair_columns(columns, n):
    shape = (columns[0].shape[0], LANES)
    return jnp.concatenate(
        [jnp.broadcast_to(columns[2 * n], shape), jnp.broadcast_to(columns[2 * n + 1], shape)], axis=1
    )


def experts_up_kernel(
    base_ref, x_ref, ga_ref, gb_ref, ua_ref, ub_ref, ra_ref, rb_ref, chosen_ref, kept_ref, g_ref, u_ref, a_ref, probs_ref, gates_ref
):
    step = pl.program_id(0)
    count = g_ref.shape[1] // LANES
    half = x_ref.shape[1] // 2
    xa, xb = x_ref[:, :half], x_ref[:, half:]

    @pl.when(step == 0)
    def _():
        chosen = chosen_ref[...]
        logits = jnp.where(chosen > 0, dot_nn(xa, ra_ref[...]) + dot_nn(xb, rb_ref[...]), MASKED)
        raised = jnp.exp(logits - jnp.max(logits, axis=1, keepdims=True)) * chosen
        probs = raised / jnp.sum(raised, axis=1, keepdims=True)
        probs_ref[...] = probs
        gates_ref[...] = probs * kept_ref[...]

    columns = spread_gates(gates_ref[...], base_ref[0] + step * count, count)
    for n in range(count // 2):
        at = slice(2 * n * LANES, (2 * n + 2) * LANES)
        g = dot_nn(xa, ga_ref[:, at]) + dot_nn(xb, gb_ref[:, at])
        u = dot_nn(xa, ua_ref[:, at]) + dot_nn(xb, ub_ref[:, at])
        g_ref[:, at] = g.astype(BF16)
        u_ref[:, at] = u.astype(BF16)
        a_ref[:, at] = (pair_columns(columns, n) * (g * jax.nn.sigmoid(g)) * u).astype(BF16)


def experts_up(base, x, gate_up, pack, chosen, kept):
    rows, width = x.shape
    hidden = gate_up.shape[1] // 4
    steps = hidden // UP_STEP
    whole = lambda s: (0, 0)
    weights = [pl.BlockSpec((width // 2, UP_STEP), lambda s, n=n: (0, s + n * steps)) for n in range(4)]
    saved = pl.BlockSpec((rows, UP_STEP), lambda s: (0, s))
    router = pl.BlockSpec((width // 2, LANES), lambda s: (0, OUT_END // LANES))
    wide = pl.BlockSpec((rows, LANES), whole)
    return pl.pallas_call(
        experts_up_kernel,
        grid=(steps,),
        in_specs=[SMEM_SPEC, pl.BlockSpec((rows, width), whole)] + weights + [router] * 2 + [wide] * 2,
        out_specs=[saved] * 3 + [wide] * 2,
        out_shape=(jax.ShapeDtypeStruct((rows, hidden), BF16),) * 3 + (jax.ShapeDtypeStruct((rows, LANES), F32),) * 2,
        compiler_params=pltpu.CompilerParams(vmem_limit_bytes=52 * MIB),
        cost_estimate=pl.CostEstimate(
            flops=4 * rows * width * hidden, bytes_accessed=22 * MIB, transcendentals=rows * hidden
        ),
        name="experts_up",
    )(base, x, gate_up, gate_up, gate_up, gate_up, *pack, chosen, kept)


def experts_down_kernel(a_ref, da_ref, db_ref, out_ref):
    half = out_ref.shape[1] // 2
    out_ref[:, :half] = dot_nt(a_ref[...], da_ref[...]).astype(BF16)
    out_ref[:, half:] = dot_nt(a_ref[...], db_ref[...]).astype(BF16)


def experts_down(active, down, part):
    rows, hidden = active.shape[0] // 2, active.shape[1]
    half = down.shape[0]
    steps = rows // (2 * BLOCK)
    weights = [pl.BlockSpec((half, hidden), lambda s, n=n: (0, n)) for n in range(2)]
    return pl.pallas_call(
        experts_down_kernel,
        grid=(steps,),
        in_specs=[pl.BlockSpec((2 * BLOCK, hidden), lambda s: (s + part * steps, 0))] + weights,
        out_specs=pl.BlockSpec((2 * BLOCK, 2 * half), lambda s: (s, 0)),
        out_shape=jax.ShapeDtypeStruct((rows, 2 * half), BF16),
        compiler_params=pltpu.CompilerParams(vmem_limit_bytes=32 * MIB),
        cost_estimate=pl.CostEstimate(flops=4 * rows * half * hidden, bytes_accessed=6 * MIB, transcendentals=0),
        name="experts_down",
    )(active, down, down)


def experts_backward_kernel(
    base_ref, dy_ref, ga_ref, gb_ref, ua_ref, ub_ref, da_ref, db_ref, g_ref, u_ref, gates_ref, dg_ref, du_ref, out_ref, total, slots
):
    step = pl.program_id(0)
    rows, width = dy_ref.shape
    half = width // 2
    count = g_ref.shape[1] // LANES
    first = base_ref[0] + step * count
    columns = spread_gates(gates_ref[...], first, count)
    lane = lax.broadcasted_iota(jnp.int32, (rows, LANES), 1)
    dya, dyb = dy_ref[:, :half], dy_ref[:, half:]
    sums = jnp.zeros((rows, LANES), F32)
    for n in range(count // 2):
        at = slice(2 * n * LANES, (2 * n + 2) * LANES)
        gate = pair_columns(columns, n)
        da = dot_nn(dya, da_ref[:, at]) + dot_nn(dyb, db_ref[:, at])
        g = g_ref[:, at].astype(F32)
        u = u_ref[:, at].astype(F32)
        logistic = jax.nn.sigmoid(g)
        swished = g * logistic
        inner = da * swished * u
        for m in range(2):
            total_slot = jnp.sum(inner[:, m * LANES : (m + 1) * LANES], axis=1, keepdims=True)
            sums = jnp.where(lane == first + 2 * n + m, total_slot, sums)
        scaled = gate * da
        dg_ref[:, at] = (scaled * u * logistic * (1.0 + g * (1.0 - logistic))).astype(BF16)
        du_ref[:, at] = (scaled * swished).astype(BF16)
    even = dot_nt(dg_ref[...], ga_ref[...]) + dot_nt(du_ref[...], ua_ref[...])
    odd = dot_nt(dg_ref[...], gb_ref[...]) + dot_nt(du_ref[...], ub_ref[...])

    @pl.when(step == 0)
    def _():
        total[:, :half] = even
        total[:, half:] = odd
        slots[...] = sums

    @pl.when(step == pl.num_programs(0) - 1)
    def _():
        out_ref[:, :half] = (total[:, :half] + even).astype(BF16)
        out_ref[:, half:width] = (total[:, half:] + odd).astype(BF16)
        out_ref[:, width:] = (slots[...] + sums).astype(BF16)


def experts_backward(base, dy, gate_up, down, g, u, gates):
    rows, width = dy.shape
    hidden = gate_up.shape[1] // 4
    steps = hidden // BACK_STEP
    whole = lambda s: (0, 0)
    weights = [pl.BlockSpec((width // 2, BACK_STEP), lambda s, n=n: (0, s + n * steps)) for n in range(4)]
    saved = pl.BlockSpec((rows, BACK_STEP), lambda s: (0, s))
    once = pl.Buffered(1)
    return pl.pallas_call(
        experts_backward_kernel,
        grid=(steps,),
        in_specs=[SMEM_SPEC, pl.BlockSpec((rows, width), whole, pipeline_mode=once)]
        + weights
        + weights[:2]
        + [saved] * 2
        + [pl.BlockSpec((rows, LANES), whole, pipeline_mode=once)],
        out_specs=[saved, saved, pl.BlockSpec((rows, width + LANES), whole, pipeline_mode=once)],
        out_shape=(
            jax.ShapeDtypeStruct((rows, hidden), BF16),
            jax.ShapeDtypeStruct((rows, hidden), BF16),
            jax.ShapeDtypeStruct((rows, width + LANES), BF16),
        ),
        scratch_shapes=[pltpu.VMEM((rows, width), F32), pltpu.VMEM((rows, LANES), F32)],
        compiler_params=pltpu.CompilerParams(vmem_limit_bytes=60 * MIB),
        cost_estimate=pl.CostEstimate(
            flops=6 * rows * width * hidden, bytes_accessed=38 * MIB, transcendentals=rows * hidden
        ),
        name="experts_backward",
    )(base, dy, gate_up, gate_up, gate_up, gate_up, down, down, g, u, gates)


def expert_weights_kernel(x_ref, r_ref, out_ref):
    out_ref[...] = dot_tn(x_ref[...], r_ref[...]).astype(BF16)


def expert_weights(x, rights):
    rows, width = x.shape
    hidden = rights[0].shape[1]
    steps = hidden // BACK_STEP
    outs = []
    for right in rights:
        outs.append(
            pl.pallas_call(
                expert_weights_kernel,
                grid=(2, steps),
                in_specs=[
                    pl.BlockSpec((rows, width // 2), lambda h, s: (0, h)),
                    pl.BlockSpec((rows, BACK_STEP), lambda h, s: (0, s)),
                ],
                out_specs=pl.BlockSpec((width // 2, BACK_STEP), lambda h, s: (0, h * steps + s)),
                out_shape=jax.ShapeDtypeStruct((width // 2, 2 * hidden), BF16),
                compiler_params=pltpu.CompilerParams(vmem_limit_bytes=40 * MIB),
                cost_estimate=pl.CostEstimate(
                    flops=2 * rows * width * hidden, bytes_accessed=12 * MIB, transcendentals=0
                ),
                name="expert_weights",
            )(x, right)
        )
    return outs


def normalize(residual, gain):
    scale = lax.rsqrt(jnp.mean(residual * residual, axis=-1, keepdims=True) + EPSILON)
    normed = residual * scale
    return normed, scale, (normed * gain).astype(BF16)


def normalize_back(grad_hidden, normed, scale, gain):
    grad_normed = grad_hidden * gain
    inner_mean = jnp.mean(grad_normed * normed, axis=-1, keepdims=True)
    return scale * (grad_normed - normed * inner_mean)


def rope_tables(row_count):
    positions = (jnp.arange(row_count, dtype=jnp.int32) % SEQUENCE_LENGTH).astype(F32)
    frequency = ROPE_BASE ** (-jnp.arange(0, HEAD_SIZE // 2, dtype=F32) * 2.0 / HEAD_SIZE)
    angles = positions[:, None] * frequency[None, :]
    cos, sin = jnp.cos(angles), jnp.sin(angles)
    return jnp.concatenate([cos] * 4, axis=1), jnp.concatenate([-sin, sin] * 2, axis=1)


def place_codes(size):
    return [(p % (size // 2)) * 2 + p // (size // 2) for p in range(size)]


def route_masks(routes, me):
    rows = routes.shape[0]
    size = lax.axis_size("tensor")
    own = rows // size
    starts = [(me ^ code) * own for code in place_codes(size)]
    routes = jnp.concatenate([lax.dynamic_slice_in_dim(routes, start, own, 0) for start in starts], axis=0)
    lane = lax.broadcasted_iota(jnp.int32, (rows, LANES), 1)
    chosen = routes[:, 0:1] == lane
    for k in range(1, TOPK):
        chosen = chosen | (routes[:, k : k + 1] == lane)
    position = jnp.concatenate([start + jnp.arange(own, dtype=jnp.int32) for start in starts])
    earlier = (position[:, None] > position[None, :]).astype(BF16)
    before = dot_nn(earlier, chosen.astype(BF16))
    kept = chosen & (before < CAP)
    return chosen.astype(F32), kept.astype(F32)


def swap(values, which):
    axis, bit = {"core": ("tensor", 1), "y": ("tensor", 2), "x": ("dp", 1)}[which]
    size = lax.axis_size(axis)
    return lax.ppermute(values, axis, [(i, i ^ bit) for i in range(size)])


def widen(values):
    other = swap(values, "y")
    near = [values, other]
    return jnp.concatenate(near + [swap(piece, "core") for piece in near], axis=0)


def widen_pair(values):
    half = values.shape[0] // 2
    by_y, by_x = swap(values, "y"), swap(values, "x")
    first, second = swap(by_y[:half], "x"), swap(by_x[half:], "y")
    near = [values, by_y, by_x, first, second]
    return jnp.concatenate(near + [swap(piece, "core") for piece in near], axis=0)


def added(left, right):
    return left.astype(F32) + right.astype(F32)


def narrow(values):
    rows = values.shape[0] // 4
    far, near = values[2 * rows :], values[: 2 * rows]
    out = added(near[rows:], swap(far[rows:], "core")).astype(BF16)
    out = swap(out, "y")
    return added(near[:rows], swap(far[:rows], "core")) + out.astype(F32)


def narrow_pair(near, far):
    rows = near.shape[0] // 4
    half = rows // 2
    received = swap(far, "core")

    def piece(n, lower):
        at = slice(n * rows + lower * half, n * rows + (lower + 1) * half)
        return added(near[at], received[at])

    def sent(*pieces):
        return jnp.concatenate([p.astype(BF16) for p in pieces], axis=0)

    x_first = swap(sent(piece(2, 0), piece(3, 0)), "x")
    y_first = swap(sent(piece(1, 1), piece(3, 1)), "y")
    y_second = swap(added(piece(1, 0), x_first[half:]).astype(BF16), "y")
    x_second = swap(added(piece(2, 1), y_first[half:]).astype(BF16), "x")
    upper = added(piece(0, 0), x_first[:half]) + y_second.astype(F32)
    lower = added(piece(0, 1), y_first[:half]) + x_second.astype(F32)
    return jnp.concatenate([upper, lower], axis=0)


def sum_over_tensor(values):
    for which in ("core", "y"):
        values = values + swap(values, which)
    return values


class Data:
    def __init__(self):
        size = lax.axis_size("dp")
        self.size = size
        self.groups = [list(range(0, size, 2)), list(range(1, size, 2))]
        self.odd = lax.axis_index("dp") % 2

    def by_parity(self, mine, other):
        even = self.odd == 0
        return jnp.where(even, mine, other), jnp.where(even, other, mine)

    def gather(self, own):
        return lax.all_gather(own, "dp", axis=0, tiled=True, axis_index_groups=self.groups)

    def scatter(self, values):
        total = lax.psum_scatter(values, "dp", scatter_dimension=0, tiled=True, axis_index_groups=self.groups)
        n = total.shape[1] // 2
        even, odd = total[:, :n], total[:, n:]
        return self.by_parity(even, odd)

    def relative(self, values):
        depth = values.shape[1] // self.size
        return jnp.concatenate(
            [values[:, i * depth : (i + 1) * depth] for group in self.groups for i in group], axis=1
        )

    def absolute(self, values):
        depth = values.shape[1] // self.size
        count = self.size // 2
        starts = [(part * count + n) * depth for n in range(count) for part in range(2)]
        if depth % LANES == 0:

            def kernel(in_ref, out_ref):
                for n, start in enumerate(starts):
                    out_ref[:, n * depth : (n + 1) * depth] = in_ref[:, start : start + depth]

            return pl.pallas_call(
                kernel,
                out_shape=jax.ShapeDtypeStruct(values.shape, values.dtype),
                in_specs=[VMEM_SPEC],
                name="absolute",
            )(values)
        return jnp.concatenate([values[:, start : start + depth] for start in starts], axis=1)


def local(
    tokens_in,
    cotangent,
    routes,
    attn_gain,
    w_query,
    key_projection,
    value_projection,
    w_out,
    moe_gain,
    w_router,
    w_gate,
    w_up,
    w_down,
):
    rows_own, width = tokens_in.shape
    me = lax.axis_index("tensor")
    me_array = me.reshape(1).astype(jnp.int32)
    depth = w_query.shape[1]
    q_columns, kv_columns = w_query.shape[2], key_projection.shape[2]
    cos, sin = rope_tables(rows_own * lax.axis_size("tensor"))
    data = Data()
    share = EXPERTS // 2
    base = (data.odd * share).reshape(1).astype(jnp.int32)

    packs, mine = [], []
    for layer in range(LAYER_COUNT):
        small = jnp.concatenate(
            [
                w_router[layer],
                attn_gain[layer][:, None],
                moe_gain[layer][:, None],
                jnp.zeros((depth, PACK - OUT_END - EXPERTS - 2), BF16),
            ],
            axis=1,
        )
        packs.append(
            jnp.concatenate(
                [w_query[layer], key_projection[layer], value_projection[layer], w_out[layer].T, small], axis=1
            )
        )

    def shares(weight):
        return [lax.dynamic_slice_in_dim(weight, start * share, share, 0) for start in (data.odd, 1 - data.odd)]

    gathered = []
    for layer in range(LAYER_COUNT):
        gate, up, down = shares(w_gate[layer]), shares(w_up[layer]), shares(w_down[layer])
        other = swap(jnp.concatenate([gate[1], up[1]], axis=0), "x")
        other_down = swap(down[1], "x")
        columns = [
            part.transpose(1, 0, 2).reshape(depth, -1)
            for own, got in ((gate[0], other[:share]), (up[0], other[share:]))
            for part in data.by_parity(own, got)
        ]
        down_columns = [part.reshape(-1, depth).T for part in data.by_parity(down[0], other_down)]
        gathered.append(
            (
                data.gather(packs[layer]),
                data.gather(jnp.concatenate(columns, axis=1)),
                data.gather(jnp.concatenate(down_columns, axis=1)),
            )
        )

    partner_routes = swap(routes, "x")
    masks = []
    for layer in range(LAYER_COUNT):
        own = route_masks(routes[layer], me)
        partner = route_masks(partner_routes[layer], me)
        middle = own[0].shape[0] // 2
        masks.append(
            [jnp.concatenate([a[:middle], b[:middle], a[middle:], b[middle:]]) for a, b in zip(own, partner)]
        )

    tokens_in, cotangent = data.relative(tokens_in), data.relative(cotangent)
    residual = tokens_in.astype(F32)
    tokens_all = widen(tokens_in)
    weights, records = [], []
    for layer in range(LAYER_COUNT):
        own_pack, gate_up, down = gathered[layer]
        pack = data.by_parity(own_pack, swap(own_pack, "x"))
        gain_attn, gain_moe = (
            jnp.concatenate([part[:, OUT_END + EXPERTS + n].astype(F32) for part in pack])[None, :] for n in range(2)
        )
        weights.append((pack, gain_attn, gain_moe, gate_up, down))
        chosen, kept = masks[layer]
        if layer == 0:
            hidden_attn = normalize(tokens_all.astype(F32), gain_attn)[2]
        else:
            hidden_attn = widen(normalize(residual, gain_attn)[2])
        before_attn = residual
        q, k, v, mixed, lse, attn_part = attention_forward(me_array, hidden_attn, pack, cos, sin)
        residual = residual + narrow(attn_part)
        before_moe = residual
        low_moe = normalize(residual, gain_moe)[2]
        hidden_moe = widen_pair(low_moe)
        g, u, active, probs, gates = experts_up(base, hidden_moe, gate_up, pack, chosen, kept)
        far = experts_down(active, down, 1)
        near = experts_down(active, down, 0)
        residual = residual + narrow_pair(near, far)
        records.append(
            (before_attn, hidden_attn, q, k, v, mixed, lse, before_moe, low_moe, hidden_moe, probs, gates, g, u, active)
        )
    grad = cotangent.astype(F32)
    pieces = []
    for layer in reversed(range(LAYER_COUNT)):
        pack, gain_attn, gain_moe, gate_up, down = weights[layer]
        before_attn, hidden_attn, q, k, v, mixed, lse, before_moe, low_moe, hidden_moe, probs, gates, g, u, active = (
            records[layer]
        )
        kept = masks[layer][1]
        grad_pair = widen_pair(grad.astype(BF16))
        (grad_down,) = expert_weights(grad_pair, (active,))
        grad_down = data.scatter(grad_down)
        grad_gate, grad_up, moe_part = experts_backward(base, grad_pair, gate_up, down, g, u, gates)
        middle = moe_part.shape[0] // 2
        own = narrow_pair(moe_part[:middle], moe_part[middle:])
        grad_gate, grad_up = (data.scatter(part) for part in expert_weights(hidden_moe, (grad_gate, grad_up)))
        grad_moe_own, grad_pairs = own[:, :width], own[:, width:] * kept[:rows_own]
        own_probs = probs[:rows_own]
        grad_chosen = own_probs * (grad_pairs - jnp.sum(own_probs * grad_pairs, axis=-1, keepdims=True))
        grad_logits = grad_chosen.astype(BF16)
        grad_moe_own = grad_moe_own + jnp.concatenate(
            [dot_nt(grad_logits, part[:, OUT_END : OUT_END + LANES]) for part in pack], axis=1
        )
        normed_moe, scale_moe, _ = normalize(before_moe, gain_moe)
        grad = grad + normalize_back(grad_moe_own, normed_moe, scale_moe, gain_moe)
        grad_all = widen(grad.astype(BF16))
        grad_qkv, attn_part = attention_backward(me_array, grad_all, pack, q, k, v, lse, cos, sin)
        grad_pack = data.scatter(attention_weights(hidden_attn, grad_qkv, grad_all, mixed, low_moe, grad_logits))
        normed_attn, scale_attn, _ = normalize(before_attn, gain_attn)
        grad = grad + normalize_back(narrow(attn_part), normed_attn, scale_attn, gain_attn)
        pieces.insert(0, (grad_pack, grad_gate, grad_up, grad_down))

    outputs = []
    for layer in range(LAYER_COUNT):
        grad_pack, grad_gate, grad_up, grad_down = pieces[layer]
        grad_pack = added(grad_pack[0], swap(grad_pack[1], "x"))

        def experts_of(pair, turned):
            both = data.by_parity(pair[0], swap(pair[1], "x"))
            both = jnp.stack([part.T if turned else part for part in both]).astype(F32)
            if turned:
                return both.reshape(EXPERTS, -1, depth)
            return both.reshape(2, depth, share, -1).transpose(0, 2, 1, 3).reshape(EXPERTS, depth, -1)

        grad_gate, grad_up = experts_of(grad_gate, False), experts_of(grad_up, False)
        own_pack = packs[layer].astype(F32)
        attn_term = jnp.sum(own_pack[:, :QKV] * grad_pack[:, :QKV], axis=1)[:, None]
        moe_term = jnp.sum(
            w_gate[layer].astype(F32) * grad_gate + w_up[layer].astype(F32) * grad_up, axis=(0, 2)
        )[:, None]
        lane = lax.broadcasted_iota(jnp.int32, (depth, LANES), 1)
        stats = grad_pack[:, OUT_END:]
        stats = jnp.where(lane == EXPERTS, attn_term, jnp.where(lane == EXPERTS + 1, moe_term, stats))
        stats = sum_over_tensor(stats)
        router_grad = stats[:, :EXPERTS]
        router_own = own_pack[:, OUT_END : OUT_END + EXPERTS]
        attn_gain_grad = stats[:, EXPERTS] / attn_gain[layer].astype(F32)
        moe_gain_grad = (stats[:, EXPERTS + 1] + jnp.sum(router_own * router_grad, axis=1)) / moe_gain[layer].astype(
            F32
        )
        outputs.append(
            (
                attn_gain_grad,
                grad_pack[:, :q_columns],
                grad_pack[:, q_columns : q_columns + kv_columns],
                grad_pack[:, q_columns + kv_columns : QKV],
                grad_pack[:, QKV:OUT_END].T,
                moe_gain_grad,
                router_grad,
                grad_gate,
                grad_up,
                experts_of(grad_down, True),
            )
        )
    stacked = tuple(jnp.stack([terms[n] for terms in outputs]) for n in range(10))
    return (data.absolute(residual), data.absolute(grad)) + stacked


def solution(mesh):
    placed = (
        P(("dp", "tensor"), None),
        P(("dp", "tensor"), None),
        P(None, "dp", None),
        P(None, "dp"),
        P(None, "dp", "tensor"),
        P(None, "dp", "tensor"),
        P(None, "dp", "tensor"),
        P(None, "tensor", "dp"),
        P(None, "dp"),
        P(None, "dp", None),
        P(None, None, "dp", "tensor"),
        P(None, None, "dp", "tensor"),
        P(None, None, "tensor", "dp"),
    )
    return jax.shard_map(
        local,
        mesh=mesh,
        in_specs=placed,
        out_specs=(
            P(("dp", "tensor"), None),
            P(("dp", "tensor"), None),
            P(None, "dp"),
            P(None, "dp", "tensor"),
            P(None, "dp", "tensor"),
            P(None, "dp", "tensor"),
            P(None, "tensor", "dp"),
            P(None, "dp"),
            P(None, "dp", None),
            P(None, None, "dp", "tensor"),
            P(None, None, "dp", "tensor"),
            P(None, None, "tensor", "dp"),
        ),
        check_vma=False,
    )
```

```python
import jax
import jax.numpy as jnp
from jax import lax
from jax.experimental import pallas as pl
from jax.experimental.pallas import tpu as pltpu
from jax.sharding import PartitionSpec as P

HEAD_SIZE = 64
TOPK = 8
EXPERTS = 16
LAYER_COUNT = 2
SEQUENCE_LENGTH = 1024
CAP = 512

EPSILON = 1e-06
ROPE_BASE = 10000.0
MASKED = -1e30
LANES = 128
BLOCK = 256
F32 = jnp.float32
BF16 = jnp.bfloat16
MIB = 1 << 20
QKV = 4 * LANES
OUT_END = 6 * LANES
PACK = 8 * LANES


def dot_nn(a, b):
    return lax.dot_general(a, b, (((1,), (0,)), ((), ())), preferred_element_type=F32)


def dot_nt(a, b):
    return lax.dot_general(a, b, (((1,), (1,)), ((), ())), preferred_element_type=F32)


def dot_tn(a, b):
    return lax.dot_general(a, b, (((0,), (0,)), ((), ())), preferred_element_type=F32)


def place_of(me, block):
    code = me ^ block
    return pl.multiple_of(((code & 1) * 2 + (code >> 1)) * BLOCK, BLOCK)


def half_mask(rows):
    return lax.broadcasted_iota(jnp.int32, (rows, LANES), 1) < HEAD_SIZE


def swap_halves(t):
    lane = lax.broadcasted_iota(jnp.int32, t.shape, 1) % HEAD_SIZE
    return jnp.where(
        lane < HEAD_SIZE // 2,
        pltpu.roll(t, LANES - HEAD_SIZE // 2, 1),
        pltpu.roll(t, HEAD_SIZE // 2, 1),
    )


def both_halves(t, low):
    turned = pltpu.roll(t, HEAD_SIZE, 1)
    return jnp.where(low, t, turned), jnp.where(low, turned, t)


def diagonal_mask(scores, row_block):
    rows = lax.broadcasted_iota(jnp.int32, scores.shape, 0) % BLOCK + row_block * BLOCK
    columns = lax.broadcasted_iota(jnp.int32, scores.shape, 1)
    return jnp.where(rows >= columns, scores, MASKED)


def attention_forward_kernel(
    me_ref, x_ref, pa_ref, pb_ref, cos_ref, sin_ref, q_ref, k_ref, v_ref, o_ref, lse_ref, out_ref, kd, vd
):
    rows, width = x_ref.shape
    half = width // 2
    low = half_mask(BLOCK)
    lane = lax.broadcasted_iota(jnp.int32, (BLOCK, LANES), 1)
    for i in range(rows // BLOCK):
        here = pl.ds(i * BLOCK, BLOCK)
        there = pl.ds(place_of(me_ref[0], i), BLOCK)
        qkv = dot_nn(x_ref[there, :half], pa_ref[:, :QKV]) + dot_nn(x_ref[there, half:], pb_ref[:, :QKV])
        cos, sin = cos_ref[here, :], sin_ref[here, :]

        def rope(t):
            return t * cos + swap_halves(t) * sin

        q = [(rope(qkv[:, j * LANES : (j + 1) * LANES]) * HEAD_SIZE ** (-0.5)).astype(BF16) for j in range(2)]
        k = rope(qkv[:, 2 * LANES : 3 * LANES])
        v = qkv[:, 3 * LANES :]
        k_ref[here, :] = k.astype(BF16)
        v_ref[here, :] = v.astype(BF16)
        for j, (kj, vj) in enumerate(zip(both_halves(k, low), both_halves(v, low))):
            kd[j, here, :] = kj.astype(BF16)
            vd[j, here, :] = vj.astype(BF16)
        context = (i + 1) * BLOCK
        lse_all = jnp.zeros((BLOCK, LANES), F32)
        outs = []
        for j in range(2):
            q_ref[here, j * LANES : (j + 1) * LANES] = q[j]
            zero = jnp.zeros_like(q[j])
            stacked = jnp.concatenate([jnp.where(low, q[j], zero), jnp.where(low, zero, q[j])], axis=0)
            scores = diagonal_mask(dot_nt(stacked, kd[j, :context, :]), i)
            row_max = jnp.max(scores, axis=1, keepdims=True)
            weights = jnp.exp(scores - row_max)
            total = jnp.sum(weights, axis=1, keepdims=True)
            lse = row_max + jnp.log(total)
            probs = (weights * (1.0 / total)).astype(BF16)
            mixed = dot_nn(probs, vd[j, :context, :])
            outs.append(jnp.where(low, mixed[:BLOCK], mixed[BLOCK:]).astype(BF16))
            lse_all = jnp.where(lane == 2 * j, lse[:BLOCK], lse_all)
            lse_all = jnp.where(lane == 2 * j + 1, lse[BLOCK:], lse_all)
        lse_ref[here, :] = lse_all
        mixed = jnp.concatenate(outs, axis=1)
        o_ref[there, :] = mixed
        out_ref[there, :half] = dot_nt(mixed, pa_ref[:, QKV:OUT_END]).astype(BF16)
        out_ref[there, half:] = dot_nt(mixed, pb_ref[:, QKV:OUT_END]).astype(BF16)


VMEM_SPEC = pl.BlockSpec(memory_space=pltpu.VMEM)
SMEM_SPEC = pl.BlockSpec(memory_space=pltpu.SMEM)


def attention_forward(me, x, pack, cos, sin):
    rows, width = x.shape
    shapes = (
        jax.ShapeDtypeStruct((rows, 2 * LANES), BF16),
        jax.ShapeDtypeStruct((rows, LANES), BF16),
        jax.ShapeDtypeStruct((rows, LANES), BF16),
        jax.ShapeDtypeStruct((rows, 2 * LANES), BF16),
        jax.ShapeDtypeStruct((rows, LANES), F32),
        jax.ShapeDtypeStruct((rows, width), BF16),
    )
    return pl.pallas_call(
        attention_forward_kernel,
        out_shape=shapes,
        in_specs=[SMEM_SPEC] + [VMEM_SPEC] * 5,
        scratch_shapes=[pltpu.VMEM((2, rows, LANES), BF16)] * 2,
        compiler_params=pltpu.CompilerParams(vmem_limit_bytes=40 * MIB),
        cost_estimate=pl.CostEstimate(
            flops=2 * rows * width * 768 + 4 * rows * rows * 256, bytes_accessed=12 * MIB, transcendentals=rows * rows * 2
        ),
        name="attention_forward",
    )(me, x, *pack, cos, sin)


def attention_backward_kernel(
    me_ref, dy_ref, pa_ref, pb_ref, q_ref, k_ref, v_ref, lse_ref, cos_ref, sin_ref, dqkv_ref, dx_ref, kd, vd, dk, dv
):
    rows, width = dy_ref.shape
    half = width // 2
    low = half_mask(BLOCK)
    for i in range(rows // BLOCK):
        here = pl.ds(i * BLOCK, BLOCK)
        k, v = k_ref[here, :].astype(F32), v_ref[here, :].astype(F32)
        for j, (kj, vj) in enumerate(zip(both_halves(k, low), both_halves(v, low))):
            kd[j, here, :] = kj.astype(BF16)
            vd[j, here, :] = vj.astype(BF16)
    dk[...] = jnp.zeros_like(dk)
    dv[...] = jnp.zeros_like(dv)
    for i in range(rows // BLOCK):
        here = pl.ds(i * BLOCK, BLOCK)
        there = pl.ds(place_of(me_ref[0], i), BLOCK)
        cos, sin = cos_ref[here, :], sin_ref[here, :]
        grad_mixed = (
            dot_nn(dy_ref[there, :half], pa_ref[:, QKV:OUT_END]) + dot_nn(dy_ref[there, half:], pb_ref[:, QKV:OUT_END])
        ).astype(BF16)
        lse_all = lse_ref[here, :]
        context = (i + 1) * BLOCK
        for j in range(2):
            qj = q_ref[here, j * LANES : (j + 1) * LANES]
            gj = grad_mixed[:, j * LANES : (j + 1) * LANES]
            zero = jnp.zeros_like(qj)
            q2 = jnp.concatenate([jnp.where(low, qj, zero), jnp.where(low, zero, qj)], axis=0)
            g2 = jnp.concatenate([jnp.where(low, gj, zero), jnp.where(low, zero, gj)], axis=0)
            lse = jnp.concatenate([lse_all[:, 2 * j : 2 * j + 1], lse_all[:, 2 * j + 1 : 2 * j + 2]], axis=0)
            scores = diagonal_mask(dot_nt(q2, kd[j, :context, :]), i)
            probs = jnp.exp(scores - lse)
            grad_probs = dot_nt(g2, vd[j, :context, :])
            inner = jnp.sum(probs * grad_probs, axis=1, keepdims=True)
            grad_scores = (probs * (grad_probs - inner)).astype(BF16)
            dk[j, :context, :] += dot_tn(grad_scores, q2)
            dv[j, :context, :] += dot_tn(probs.astype(BF16), g2)
            grad_q = dot_nn(grad_scores, kd[j, :context, :])
            grad_q = jnp.where(low, grad_q[:BLOCK], grad_q[BLOCK:]) * HEAD_SIZE ** (-0.5)
            dqkv_ref[there, j * LANES : (j + 1) * LANES] = (grad_q * cos - swap_halves(grad_q) * sin).astype(BF16)
    for i in range(rows // BLOCK):
        here = pl.ds(i * BLOCK, BLOCK)
        there = pl.ds(place_of(me_ref[0], i), BLOCK)
        cos, sin = cos_ref[here, :], sin_ref[here, :]

        def folded(total):
            pair = [total[j, here, :] for j in range(2)]
            pair = [t + pltpu.roll(t, HEAD_SIZE, 1) for t in pair]
            return jnp.where(low, pair[0], pair[1])

        grad_k = folded(dk)
        dqkv_ref[there, 2 * LANES : 3 * LANES] = (grad_k * cos - swap_halves(grad_k) * sin).astype(BF16)
        dqkv_ref[there, 3 * LANES :] = folded(dv).astype(BF16)
        grad_qkv = dqkv_ref[there, :]
        dx_ref[there, :half] = dot_nt(grad_qkv, pa_ref[:, :QKV]).astype(BF16)
        dx_ref[there, half:] = dot_nt(grad_qkv, pb_ref[:, :QKV]).astype(BF16)


def attention_backward(me, dy, pack, q, k, v, lse, cos, sin):
    rows, width = dy.shape
    return pl.pallas_call(
        attention_backward_kernel,
        out_shape=(jax.ShapeDtypeStruct((rows, QKV), BF16), jax.ShapeDtypeStruct((rows, width), BF16)),
        in_specs=[SMEM_SPEC] + [VMEM_SPEC] * 9,
        scratch_shapes=[pltpu.VMEM((2, rows, LANES), BF16)] * 2 + [pltpu.VMEM((2, rows, LANES), F32)] * 2,
        compiler_params=pltpu.CompilerParams(vmem_limit_bytes=48 * MIB),
        cost_estimate=pl.CostEstimate(
            flops=2 * rows * width * 768 + 10 * rows * rows * 256, bytes_accessed=12 * MIB, transcendentals=rows * rows * 2
        ),
        name="attention_backward",
    )(me, dy, *pack, q, k, v, lse, cos, sin)


def attention_weights_kernel(odd_ref, x_ref, dqkv_ref, dy_ref, o_ref, low_ref, dl_ref, own_ref, partner_ref):
    half = x_ref.shape[1] // 2
    for n, out_ref in enumerate((own_ref, partner_ref)):
        at = pl.ds(pl.multiple_of((odd_ref[0] ^ n) * half, half), half)
        out_ref[:, :QKV] = dot_tn(x_ref[:, at], dqkv_ref[...]).astype(BF16)
        out_ref[:, QKV:OUT_END] = dot_tn(dy_ref[:, at], o_ref[...]).astype(BF16)
        out_ref[:, OUT_END:] = dot_tn(low_ref[:, at], dl_ref[...]).astype(BF16)


def attention_weights(odd, x, dqkv, dy, o, low, dl):
    rows, width = x.shape
    return pl.pallas_call(
        attention_weights_kernel,
        out_shape=(jax.ShapeDtypeStruct((width // 2, OUT_END + LANES), BF16),) * 2,
        in_specs=[SMEM_SPEC] + [VMEM_SPEC] * 6,
        compiler_params=pltpu.CompilerParams(vmem_limit_bytes=32 * MIB),
        cost_estimate=pl.CostEstimate(flops=2 * rows * width * 800, bytes_accessed=9 * MIB, transcendentals=0),
        name="attention_weights",
    )(odd, x, dqkv, dy, o, low, dl)


UP_STEP = 512
BACK_STEP = 512


def spread_gates(gates, first, count):
    lane = lax.broadcasted_iota(jnp.int32, gates.shape, 1)
    return [jnp.sum(jnp.where(lane == first + n, gates, 0.0), axis=1, keepdims=True) for n in range(count)]


def pair_columns(columns, n):
    shape = (columns[0].shape[0], LANES)
    return jnp.concatenate(
        [jnp.broadcast_to(columns[2 * n], shape), jnp.broadcast_to(columns[2 * n + 1], shape)], axis=1
    )


def experts_up_kernel(
    base_ref, x_ref, ga_ref, gb_ref, ua_ref, ub_ref, ra_ref, rb_ref, chosen_ref, kept_ref, g_ref, u_ref, a_ref, probs_ref, gates_ref
):
    step = pl.program_id(0)
    count = g_ref.shape[1] // LANES
    half = x_ref.shape[1] // 2
    xa, xb = x_ref[:, :half], x_ref[:, half:]

    @pl.when(step == 0)
    def _():
        chosen = chosen_ref[...]
        logits = jnp.where(chosen > 0, dot_nn(xa, ra_ref[...]) + dot_nn(xb, rb_ref[...]), MASKED)
        raised = jnp.exp(logits - jnp.max(logits, axis=1, keepdims=True)) * chosen
        probs = raised / jnp.sum(raised, axis=1, keepdims=True)
        probs_ref[...] = probs
        gates_ref[...] = probs * kept_ref[...]

    columns = spread_gates(gates_ref[...], base_ref[0] + step * count, count)
    for n in range(count // 2):
        at = slice(2 * n * LANES, (2 * n + 2) * LANES)
        g = dot_nn(xa, ga_ref[:, at]) + dot_nn(xb, gb_ref[:, at])
        u = dot_nn(xa, ua_ref[:, at]) + dot_nn(xb, ub_ref[:, at])
        g_ref[:, at] = g.astype(BF16)
        u_ref[:, at] = u.astype(BF16)
        a_ref[:, at] = (pair_columns(columns, n) * (g * jax.nn.sigmoid(g)) * u).astype(BF16)


def experts_up(base, x, gate_up, pack, chosen, kept):
    rows, width = x.shape
    hidden = gate_up.shape[1] // 4
    steps = hidden // UP_STEP
    whole = lambda s: (0, 0)
    weights = [pl.BlockSpec((width // 2, UP_STEP), lambda s, n=n: (0, s + n * steps)) for n in range(4)]
    saved = pl.BlockSpec((rows, UP_STEP), lambda s: (0, s))
    router = pl.BlockSpec((width // 2, LANES), lambda s: (0, OUT_END // LANES))
    wide = pl.BlockSpec((rows, LANES), whole)
    return pl.pallas_call(
        experts_up_kernel,
        grid=(steps,),
        in_specs=[SMEM_SPEC, pl.BlockSpec((rows, width), whole)] + weights + [router] * 2 + [wide] * 2,
        out_specs=[saved] * 3 + [wide] * 2,
        out_shape=(jax.ShapeDtypeStruct((rows, hidden), BF16),) * 3 + (jax.ShapeDtypeStruct((rows, LANES), F32),) * 2,
        compiler_params=pltpu.CompilerParams(vmem_limit_bytes=60 * MIB),
        cost_estimate=pl.CostEstimate(
            flops=4 * rows * width * hidden, bytes_accessed=22 * MIB, transcendentals=rows * hidden
        ),
        name="experts_up",
    )(base, x, gate_up, gate_up, gate_up, gate_up, *pack, chosen, kept)


def experts_down_kernel(a_ref, da_ref, db_ref, out_ref):
    half = out_ref.shape[1] // 2
    out_ref[:, :half] = dot_nn(a_ref[...], da_ref[...]).astype(BF16)
    out_ref[:, half:] = dot_nn(a_ref[...], db_ref[...]).astype(BF16)


def experts_down(active, down):
    rows, hidden = active.shape
    half = down.shape[1]
    weights = [pl.BlockSpec((hidden, half), lambda s, n=n: (n, 0)) for n in range(2)]
    return pl.pallas_call(
        experts_down_kernel,
        grid=(rows // (2 * BLOCK),),
        in_specs=[pl.BlockSpec((2 * BLOCK, hidden), lambda s: (s, 0))] + weights,
        out_specs=pl.BlockSpec((2 * BLOCK, 2 * half), lambda s: (s, 0)),
        out_shape=jax.ShapeDtypeStruct((rows, 2 * half), BF16),
        compiler_params=pltpu.CompilerParams(vmem_limit_bytes=60 * MIB),
        cost_estimate=pl.CostEstimate(flops=4 * rows * half * hidden, bytes_accessed=6 * MIB, transcendentals=0),
        name="experts_down",
    )(active, down, down)


def experts_backward_kernel(
    base_ref, dy_ref, ga_ref, gb_ref, ua_ref, ub_ref, da_ref, db_ref, g_ref, u_ref, gates_ref, dg_ref, du_ref, out_ref, total, slots
):
    step = pl.program_id(0)
    rows, width = dy_ref.shape
    half = width // 2
    count = g_ref.shape[1] // LANES
    first = base_ref[0] + step * count
    columns = spread_gates(gates_ref[...], first, count)
    lane = lax.broadcasted_iota(jnp.int32, (rows, LANES), 1)
    dya, dyb = dy_ref[:, :half], dy_ref[:, half:]
    sums = jnp.zeros((rows, LANES), F32)
    for n in range(count // 2):
        at = slice(2 * n * LANES, (2 * n + 2) * LANES)
        gate = pair_columns(columns, n)
        da = dot_nt(dya, da_ref[at, :]) + dot_nt(dyb, db_ref[at, :])
        g = g_ref[:, at].astype(F32)
        u = u_ref[:, at].astype(F32)
        logistic = jax.nn.sigmoid(g)
        swished = g * logistic
        inner = da * swished * u
        for m in range(2):
            total_slot = jnp.sum(inner[:, m * LANES : (m + 1) * LANES], axis=1, keepdims=True)
            sums = jnp.where(lane == first + 2 * n + m, total_slot, sums)
        scaled = gate * da
        dg_ref[:, at] = (scaled * u * logistic * (1.0 + g * (1.0 - logistic))).astype(BF16)
        du_ref[:, at] = (scaled * swished).astype(BF16)
    even = dot_nt(dg_ref[...], ga_ref[...]) + dot_nt(du_ref[...], ua_ref[...])
    odd = dot_nt(dg_ref[...], gb_ref[...]) + dot_nt(du_ref[...], ub_ref[...])

    @pl.when(step == 0)
    def _():
        total[:, :half] = even
        total[:, half:] = odd
        slots[...] = sums

    @pl.when(step == pl.num_programs(0) - 1)
    def _():
        out_ref[:, :half] = (total[:, :half] + even).astype(BF16)
        out_ref[:, half:width] = (total[:, half:] + odd).astype(BF16)
        out_ref[:, width:] = (slots[...] + sums).astype(BF16)


def experts_backward(base, dy, gate_up, down, g, u, gates):
    rows, width = dy.shape
    hidden = gate_up.shape[1] // 4
    steps = hidden // BACK_STEP
    whole = lambda s: (0, 0)
    weights = [pl.BlockSpec((width // 2, BACK_STEP), lambda s, n=n: (0, s + n * steps)) for n in range(4)]
    saved = pl.BlockSpec((rows, BACK_STEP), lambda s: (0, s))
    once = pl.Buffered(1)
    return pl.pallas_call(
        experts_backward_kernel,
        grid=(steps,),
        in_specs=[SMEM_SPEC, pl.BlockSpec((rows, width), whole, pipeline_mode=once)]
        + weights
        + [pl.BlockSpec((BACK_STEP, width // 2), lambda s, n=n: (s + n * steps, 0)) for n in range(2)]
        + [saved] * 2
        + [pl.BlockSpec((rows, LANES), whole, pipeline_mode=once)],
        out_specs=[saved, saved, pl.BlockSpec((rows, width + LANES), whole, pipeline_mode=once)],
        out_shape=(
            jax.ShapeDtypeStruct((rows, hidden), BF16),
            jax.ShapeDtypeStruct((rows, hidden), BF16),
            jax.ShapeDtypeStruct((rows, width + LANES), BF16),
        ),
        scratch_shapes=[pltpu.VMEM((rows, width), F32), pltpu.VMEM((rows, LANES), F32)],
        compiler_params=pltpu.CompilerParams(vmem_limit_bytes=60 * MIB),
        cost_estimate=pl.CostEstimate(
            flops=6 * rows * width * hidden, bytes_accessed=38 * MIB, transcendentals=rows * hidden
        ),
        name="experts_backward",
    )(base, dy, gate_up, gate_up, gate_up, gate_up, down, down, g, u, gates)


def expert_weights_kernel(xn_ref, xf_ref, rn_ref, rf_ref, out_ref):
    out_ref[...] = (dot_tn(xn_ref[...], rn_ref[...]) + dot_tn(xf_ref[...], rf_ref[...])).astype(BF16)


def expert_weights(x, right):
    rows, width = x[0].shape
    hidden = right[0].shape[1]
    return pl.pallas_call(
        expert_weights_kernel,
        grid=(2,),
        in_specs=[pl.BlockSpec((rows, width // 2), lambda h: (0, h))] * 2
        + [pl.BlockSpec((rows, hidden), lambda h: (0, 0))] * 2,
        out_specs=pl.BlockSpec((width // 2, hidden), lambda h: (0, h)),
        out_shape=jax.ShapeDtypeStruct((width // 2, 2 * hidden), BF16),
        compiler_params=pltpu.CompilerParams(vmem_limit_bytes=60 * MIB),
        cost_estimate=pl.CostEstimate(flops=4 * rows * width * hidden, bytes_accessed=12 * MIB, transcendentals=0),
        name="expert_weights",
    )(*x, *right)


def gate_up_out_kernel(odd_ref, tg_ref, og_ref, tu_ref, ou_ref, wg_ref, wu_ref, *refs):
    gate_ref, up_ref, term_ref = refs[-3:]
    share = gate_ref.shape[1] // 2
    total = jnp.zeros(term_ref.shape, F32)
    for mine, start in ((True, odd_ref[0] * share), (False, (1 - odd_ref[0]) * share)):
        for e in range(share):
            at = slice(e * LANES, (e + 1) * LANES)
            dg = (tg_ref if mine else og_ref)[:, at].astype(F32)
            du = (tu_ref if mine else ou_ref)[:, at].astype(F32)
            gate_ref[0, start + e] = dg
            up_ref[0, start + e] = du
            total += dg * wg_ref[0, start + e].astype(F32) + du * wu_ref[0, start + e].astype(F32)
    term_ref[...] = total


def gate_up_out(odd, layer, totals, others, w_gate, w_up, earlier):
    layers, experts, depth, wide = w_gate.shape
    own = pl.BlockSpec((depth, others[0].shape[1]), lambda i, odd: (0, odd[0]))
    other = pl.BlockSpec(others[0].shape, lambda i, odd: (0, 0))
    block = pl.BlockSpec((1, experts, depth, wide), lambda i, odd: (layer, 0, 0, 0))
    return pl.pallas_call(
        gate_up_out_kernel,
        grid_spec=pltpu.PrefetchScalarGridSpec(
            num_scalar_prefetch=1,
            grid=(1,),
            in_specs=[own, other, own, other, block, block] + [pl.BlockSpec(memory_space=pl.ANY)] * len(earlier),
            out_specs=[block, block, pl.BlockSpec((depth, wide), lambda i, odd: (0, 0))],
        ),
        out_shape=(jax.ShapeDtypeStruct(w_gate.shape, F32),) * 2 + (jax.ShapeDtypeStruct((depth, wide), F32),),
        input_output_aliases={7 + n: n for n in range(len(earlier))},
        compiler_params=pltpu.CompilerParams(vmem_limit_bytes=24 * MIB),
        name="gate_up_out",
    )(odd, totals[0], others[0], totals[1], others[1], w_gate, w_up, *earlier)


def down_out_kernel(odd_ref, t_ref, o_ref, *refs):
    out_ref = refs[-1]
    share, wide = out_ref.shape[1] // 2, out_ref.shape[2]
    for e in range(share):
        at = slice(e * wide, (e + 1) * wide)
        out_ref[0, odd_ref[0] * share + e] = t_ref[:, at].astype(F32).T
        out_ref[0, (1 - odd_ref[0]) * share + e] = o_ref[:, at].astype(F32).T


def down_out(odd, layer, total, other, shape, earlier):
    block = pl.BlockSpec((1,) + shape[1:], lambda i, odd: (layer, 0, 0, 0))
    return pl.pallas_call(
        down_out_kernel,
        grid_spec=pltpu.PrefetchScalarGridSpec(
            num_scalar_prefetch=1,
            grid=(1,),
            in_specs=[pl.BlockSpec(other.shape, lambda i, odd: (0, odd[0])), pl.BlockSpec(other.shape, lambda i, odd: (0, 0))]
            + [pl.BlockSpec(memory_space=pl.ANY)] * len(earlier),
            out_specs=block,
        ),
        out_shape=jax.ShapeDtypeStruct(shape, F32),
        input_output_aliases={3 + n: n for n in range(len(earlier))},
        compiler_params=pltpu.CompilerParams(vmem_limit_bytes=24 * MIB),
        name="down_out",
    )(odd, total, other, *earlier)


def pack_out_kernel(t_ref, w_ref, *refs):
    q_ref, k_ref, v_ref, wo_ref, stats_ref = refs[-5:]
    total = t_ref[...].astype(F32)
    q_ref[0] = total[:, : 2 * LANES]
    k_ref[0] = total[:, 2 * LANES : 3 * LANES]
    v_ref[0] = total[:, 3 * LANES : QKV]
    wo_ref[0] = total[:, QKV:OUT_END].T
    term = jnp.sum(total[:, :QKV] * w_ref[:, :QKV].astype(F32), axis=1, keepdims=True)
    stats = total[:, OUT_END:]
    lane = lax.broadcasted_iota(jnp.int32, stats.shape, 1)
    stats_ref[...] = jnp.where(lane == EXPERTS, term, jnp.where(lane < EXPERTS, stats, 0.0))


def pack_out(layer, total, pack, earlier):
    depth, columns = total.shape
    shapes = [(depth, 2 * LANES), (depth, LANES), (depth, LANES), (2 * LANES, depth)]
    whole = lambda i: (0, 0)
    return pl.pallas_call(
        pack_out_kernel,
        grid=(1,),
        in_specs=[pl.BlockSpec(total.shape, whole), pl.BlockSpec(pack.shape, whole)]
        + [pl.BlockSpec(memory_space=pl.ANY)] * len(earlier),
        out_specs=[pl.BlockSpec((1,) + shape, lambda i: (layer, 0, 0)) for shape in shapes]
        + [pl.BlockSpec((depth, LANES), whole)],
        out_shape=tuple(jax.ShapeDtypeStruct((LAYER_COUNT,) + shape, F32) for shape in shapes)
        + (jax.ShapeDtypeStruct((depth, LANES), F32),),
        input_output_aliases={2 + n: n for n in range(len(earlier))},
        compiler_params=pltpu.CompilerParams(vmem_limit_bytes=24 * MIB),
        name="pack_out",
    )(total, pack, *earlier)


def normalize(residual, gain):
    scale = lax.rsqrt(jnp.mean(residual * residual, axis=-1, keepdims=True) + EPSILON)
    normed = residual * scale
    return normed, scale, (normed * gain).astype(BF16)


def normalize_back(grad_hidden, normed, scale, gain):
    grad_normed = grad_hidden * gain
    inner_mean = jnp.mean(grad_normed * normed, axis=-1, keepdims=True)
    return scale * (grad_normed - normed * inner_mean)


def rope_tables(row_count):
    positions = (jnp.arange(row_count, dtype=jnp.int32) % SEQUENCE_LENGTH).astype(F32)
    frequency = ROPE_BASE ** (-jnp.arange(0, HEAD_SIZE // 2, dtype=F32) * 2.0 / HEAD_SIZE)
    angles = positions[:, None] * frequency[None, :]
    cos, sin = jnp.cos(angles), jnp.sin(angles)
    return jnp.concatenate([cos] * 4, axis=1), jnp.concatenate([-sin, sin] * 2, axis=1)


def route_masks(routes, partner, me):
    rows = routes.shape[0]
    half = rows // (2 * lax.axis_size("tensor"))
    lane = lax.broadcasted_iota(jnp.int32, (rows, LANES), 1)
    earlier = (
        lax.broadcasted_iota(jnp.int32, (rows, rows), 0) > lax.broadcasted_iota(jnp.int32, (rows, rows), 1)
    ).astype(BF16)
    both = []
    for named in (routes, partner):
        chosen = named[:, 0:1] == lane
        for k in range(1, TOPK):
            chosen = chosen | (named[:, k : k + 1] == lane)
        before = dot_nn(earlier, chosen.astype(BF16))
        both.append((chosen.astype(F32), (chosen & (before < CAP)).astype(F32)))

    def placed(which, core):
        parts = []
        for lower, places in ((0, ((0, 0), (0, 2), (1, 0), (1, 2))), (1, ((0, 0), (1, 0), (0, 2), (1, 2)))):
            for x, y in places:
                start = ((me ^ (y + core)) * 2 + lower) * half
                parts.append(lax.dynamic_slice_in_dim(both[x][which], start, half, 0))
        return jnp.concatenate(parts, axis=0)

    return [[placed(which, core) for core in range(2)] for which in range(2)]


def after(values, *earlier):
    return lax.optimization_barrier((values,) + earlier)[0]


def swap(values, which):
    axis, bit = {"core": ("tensor", 1), "y": ("tensor", 2), "x": ("dp", 1)}[which]
    size = lax.axis_size(axis)
    return lax.ppermute(values, axis, [(i, i ^ bit) for i in range(size)])


def widen(values, meanwhile=None):
    other = swap(values, "y")
    sibling = swap(values, "core")
    if meanwhile is not None:
        other = after(other, *meanwhile(sibling))
    return jnp.concatenate([values, other, sibling, swap(other, "core")], axis=0)


def widen_pair(values):
    half = values.shape[0] // 2
    by_y, by_x = swap(values, "y"), swap(values, "x")
    first, second = swap(by_y[:half], "x"), swap(by_x[half:], "y")
    near = jnp.concatenate(
        [values[:half], by_y[:half], by_x[:half], first, values[half:], by_x[half:], by_y[half:], second], axis=0
    )
    return near, swap(near, "core")


def added(left, right):
    return left.astype(F32) + right.astype(F32)


def narrow(values, meanwhile=None):
    rows = values.shape[0] // 4
    far, near = values[2 * rows :], values[: 2 * rows]
    sent = added(near[rows:], swap(far[rows:], "core")).astype(BF16)
    out = swap(sent, "y")
    if meanwhile is not None:
        out = after(out, *meanwhile(sent))
    return added(near[:rows], swap(far[:rows], "core")) + out.astype(F32)


def pair_pieces(near, far):
    half = near.shape[0] // 8
    received = swap(far, "core")

    def piece(start, end):
        return added(near[start * half : end * half], received[start * half : end * half])

    return piece, piece(2, 4).astype(BF16), piece(6, 8).astype(BF16)


def pair_sum(piece, x_first, y_first):
    half = x_first.shape[0] // 2
    y_second = swap((piece(1, 2) + x_first[half:].astype(F32)).astype(BF16), "y")
    x_second = swap((piece(5, 6) + y_first[half:].astype(F32)).astype(BF16), "x")
    upper = piece(0, 1) + x_first[:half].astype(F32) + y_second.astype(F32)
    lower = piece(4, 5) + y_first[:half].astype(F32) + x_second.astype(F32)
    return jnp.concatenate([upper, lower], axis=0)


def narrow_pair(near, far, meanwhile=None):
    piece, to_x, to_y = pair_pieces(near, far)
    x_first, y_first = swap(to_x, "x"), swap(to_y, "y")
    if meanwhile is not None:
        x_first = after(x_first, *meanwhile(to_x))
    return pair_sum(piece, x_first, y_first)


def sum_over_tensor(values):
    for which in ("core", "y"):
        values = values + swap(values, which)
    return values


class Data:
    def __init__(self):
        size = lax.axis_size("dp")
        self.size = size
        self.groups = [list(range(0, size, 2)), list(range(1, size, 2))]
        self.odd = lax.axis_index("dp") % 2

    def by_parity(self, mine, other):
        even = self.odd == 0
        return jnp.where(even, mine, other), jnp.where(even, other, mine)

    def gather(self, own, axis=0):
        return lax.all_gather(own, "dp", axis=axis, tiled=True, axis_index_groups=self.groups)

    def scatter(self, values, axis=0):
        return lax.psum_scatter(values, "dp", scatter_dimension=axis, tiled=True, axis_index_groups=self.groups)

    def from_partner(self, total, axis, *earlier):
        size = total.shape[axis] // 2
        sent = lax.dynamic_slice_in_dim(total, (1 - self.odd) * size, size, axis)
        return swap(after(sent, *earlier) if earlier else sent, "x")

    def relative(self, values):
        depth = values.shape[1] // self.size
        return jnp.concatenate(
            [values[:, i * depth : (i + 1) * depth] for group in self.groups for i in group], axis=1
        )

    def absolute(self, values):
        depth = values.shape[1] // self.size
        count = self.size // 2
        starts = [(part * count + n) * depth for n in range(count) for part in range(2)]
        if depth % LANES == 0:

            def kernel(in_ref, out_ref):
                for n, start in enumerate(starts):
                    out_ref[:, n * depth : (n + 1) * depth] = in_ref[:, start : start + depth]

            return pl.pallas_call(
                kernel,
                out_shape=jax.ShapeDtypeStruct(values.shape, values.dtype),
                in_specs=[VMEM_SPEC],
                name="absolute",
            )(values)
        return jnp.concatenate([values[:, start : start + depth] for start in starts], axis=1)


def local(
    tokens_in,
    cotangent,
    routes,
    attn_gain,
    w_query,
    key_projection,
    value_projection,
    w_out,
    moe_gain,
    w_router,
    w_gate,
    w_up,
    w_down,
):
    rows_own, width = tokens_in.shape
    me = lax.axis_index("tensor")
    me_array = me.reshape(1).astype(jnp.int32)
    depth = w_query.shape[1]
    q_columns, kv_columns = w_query.shape[2], key_projection.shape[2]
    cos, sin = rope_tables(rows_own * lax.axis_size("tensor"))
    data = Data()
    share = EXPERTS // 2
    odd = data.odd.reshape(1).astype(jnp.int32)
    base = odd * share

    packs = []
    for layer in range(LAYER_COUNT):
        small = jnp.concatenate(
            [
                w_router[layer],
                attn_gain.T,
                moe_gain.T,
                jnp.zeros((depth, PACK - OUT_END - EXPERTS - 2 * LAYER_COUNT), BF16),
            ],
            axis=1,
        )
        packs.append(
            jnp.concatenate(
                [w_query[layer], key_projection[layer], value_projection[layer], w_out[layer].T, small], axis=1
            )
        )

    def shares(weight):
        return [lax.dynamic_slice_in_dim(weight, start * share, share, 0) for start in (data.odd, 1 - data.odd)]

    def gate_up_columns(layer, *earlier):
        gate, up = shares(w_gate[layer]), shares(w_up[layer])
        sent = jnp.concatenate([gate[1], up[1]], axis=0)
        other = swap(after(sent, *earlier) if earlier else sent, "x")
        columns = [
            part.transpose(1, 0, 2).reshape(depth, -1)
            for own, got in ((gate[0], other[:share]), (up[0], other[share:]))
            for part in data.by_parity(own, got)
        ]
        return jnp.concatenate(columns, axis=1)

    def down_rows(layer, *earlier):
        down = shares(w_down[layer])
        sent = after(down[1], *earlier) if earlier else down[1]
        return jnp.concatenate(
            [part.reshape(-1, depth) for part in data.by_parity(down[0], swap(sent, "x"))], axis=0
        )

    own_packs = [data.gather(packs[0])]
    tokens_in = data.relative(after(tokens_in, packs[0]))
    tokens_all = widen(tokens_in)
    columns = gate_up_columns(0, packs[0])
    gate_ups = [data.gather(columns)]
    pack = data.by_parity(own_packs[0], swap(after(own_packs[0], columns), "x"))
    rows = down_rows(0, pack[0])
    downs = [data.gather(rows, 1)]
    own_packs.append(data.gather(after(packs[1], rows)))
    next_columns, next_rows = gate_up_columns(1, pack[0]), down_rows(1, pack[0])
    gate_ups.append(data.gather(next_columns))
    downs.append(data.gather(next_rows, 1))
    masks = []

    def mask(layer, point):
        masks.append(route_masks(after(routes[layer], point), after(partner_routes[layer], point), me))
        return [*masks[-1][0], *masks[-1][1]]

    residual = tokens_in.astype(F32)
    weights, records = [], []
    for layer in range(LAYER_COUNT):
        gate_up, down = gate_ups[layer], downs[layer]
        if layer > 0:
            pack = data.by_parity(own_packs[layer], swap(after(own_packs[layer], residual), "x"))
        if layer == 0:
            gains = [
                jnp.concatenate([part[:, OUT_END + EXPERTS + n].astype(F32) for part in pack])[None, :]
                for n in range(2 * LAYER_COUNT)
            ]
        gain_attn, gain_moe = gains[layer], gains[LAYER_COUNT + layer]
        weights.append((pack, gain_attn, gain_moe, gate_up, down))
        if layer == 0:
            hidden_attn = normalize(tokens_all.astype(F32), gain_attn)[2]
            cotangent = data.relative(after(cotangent, hidden_attn))
            partner_routes = swap(after(routes, pack[0]), "x")
        else:
            hidden_attn = widen(normalize(residual, gain_attn)[2])
        before_attn = residual
        q, k, v, mixed, lse, attn_part = attention_forward(me_array, hidden_attn, pack, cos, sin)
        if layer == 0:
            held = lambda point: mask(0, point) + [next_columns, next_rows]
        else:
            held = lambda point, layer=layer: mask(layer, point)
        residual = residual + narrow(attn_part, held)
        before_moe = residual
        low_moe = normalize(residual, gain_moe)[2]
        hidden_moe = widen_pair(low_moe)
        chosen, kept = masks[layer]
        parts = [experts_up(base, hidden_moe[0], gate_up, pack, chosen[0], kept[0])]
        parts.append(experts_up(base, after(hidden_moe[1], parts[0][2]), gate_up, pack, chosen[1], kept[1]))
        g, u, active, probs, gates = zip(*parts)
        records.append(
            (before_attn, hidden_attn, q, k, v, mixed, lse, before_moe, low_moe, hidden_moe, probs[0], gates, g, u, active)
        )
        if layer < LAYER_COUNT - 1:
            active = after(active, *active)
            far, near = (experts_down(active[n], down) for n in (1, 0))
            residual = residual + narrow_pair(near, far)
    grad = cotangent.astype(F32)
    pieces = []
    half = rows_own // 2

    def own_of(values):
        return jnp.concatenate([values[:half], values[4 * half : 5 * half]], axis=0)

    for layer in reversed(range(LAYER_COUNT)):
        pack, gain_attn, gain_moe, gate_up, down = weights[layer]
        before_attn, hidden_attn, q, k, v, mixed, lse, before_moe, low_moe, hidden_moe, probs, gates, g, u, active = (
            records[layer]
        )
        kept = masks[layer][1][0]
        grad_pair = widen_pair(grad.astype(BF16))
        if layer == LAYER_COUNT - 1:
            grad_down = expert_weights(grad_pair, active)
            grad_pair = after(grad_pair, grad_down)
        parts = [experts_backward(base, grad_pair[0], gate_up, down, g[0], u[0], gates[0])]
        grad_far = after(grad_pair[1], parts[0][0])
        if layer < LAYER_COUNT - 1:
            grad_down = expert_weights((grad_pair[0], grad_far), active)
            grad_far = after(grad_far, grad_down)
        grad_down = data.scatter(grad_down)
        parts.append(experts_backward(base, grad_far, gate_up, down, g[1], u[1], gates[1]))
        grad_gate, grad_up, moe_part = zip(*parts)
        if layer == 0:
            result_first = swap(result_x, "x"), swap(result_y, "y")
            moe_part = after(moe_part, *result_first)
        made = []

        def meanwhile(point, active=active, down=down, made=made, last=layer == LAYER_COUNT - 1, right=grad_gate):
            if last:
                held = after(active, point)
                made.extend(experts_down(held[n], down) for n in (1, 0))
            else:
                made.append(expert_weights(hidden_moe, after(right, point)))
            return made

        own = narrow_pair(*moe_part, meanwhile)
        if layer == LAYER_COUNT - 1:
            far, near = made
            result_piece, result_x, result_y = pair_pieces(near, far)
            grad_gate = expert_weights(hidden_moe, after(grad_gate, far, near))
        else:
            (grad_gate,) = made
        grad_gate = data.scatter(grad_gate)
        grad_moe_own, grad_pairs = own[:, :width], own[:, width:] * own_of(kept)
        own_probs = own_of(probs)
        grad_chosen = own_probs * (grad_pairs - jnp.sum(own_probs * grad_pairs, axis=-1, keepdims=True))
        grad_logits = grad_chosen.astype(BF16)
        grad_moe_own = grad_moe_own + jnp.concatenate(
            [dot_nt(grad_logits, part[:, OUT_END : OUT_END + LANES]) for part in pack], axis=1
        )
        normed_moe, scale_moe, _ = normalize(before_moe, gain_moe)
        grad = grad + normalize_back(grad_moe_own, normed_moe, scale_moe, gain_moe)
        grad_low = grad.astype(BF16)
        made = []

        def meanwhile(point, made=made, right=grad_up):
            made.append(expert_weights(hidden_moe, after(right, point)))
            return made

        if layer == 0:
            later_pack, _, later_up, _ = pieces[0]

            def meanwhile(point, made=made, first=meanwhile):
                partners.append(data.from_partner(later_up, 1, point))
                partners.append(data.from_partner(later_pack, 1, point))
                return first(point) + partners[2:]

        grad_all = widen(grad_low, meanwhile)
        grad_up = data.scatter(made[0])
        grad_qkv, attn_part = attention_backward(me_array, grad_all, pack, q, k, v, lse, cos, sin)
        pack_product = attention_weights(odd, hidden_attn, grad_qkv, grad_all, mixed, low_moe, grad_logits)
        if layer == LAYER_COUNT - 1:
            partners = []

            def meanwhile(point, grad_down=grad_down, grad_gate=grad_gate):
                partners.extend(data.from_partner(part, 1, point) for part in (grad_down, grad_gate))
                return [*pack_product, result_x, result_y, *partners]

        else:
            meanwhile = lambda point: pack_product
        attn_own = narrow(attn_part, meanwhile)
        own_product, partner_product = pack_product
        if layer == 0:
            own_product = added(own_product, swap(partner_product, "x")).astype(BF16)
            grad_pack = data.scatter(own_product)
        else:
            halves = jnp.where(data.odd == 0, own_product, partner_product), jnp.where(
                data.odd == 0, partner_product, own_product
            )
            grad_pack = data.scatter(jnp.concatenate(halves, axis=1))
        normed_attn, scale_attn, _ = normalize(before_attn, gain_attn)
        grad = grad + normalize_back(attn_own, normed_attn, scale_attn, gain_attn)
        pieces.insert(0, (grad_pack, grad_gate, grad_up, grad_down))
    residual = residual + pair_sum(result_piece, *after(result_first, *pack_product))
    result, input_grad = data.absolute(residual), data.absolute(grad)
    stacked_experts, stacked_down, stacked_pack, stats = (), (), (), [None] * LAYER_COUNT
    lane = lax.broadcasted_iota(jnp.int32, (depth, LANES), 1)
    for layer in reversed(range(LAYER_COUNT)):
        grad_pack, grad_gate, grad_up, grad_down = pieces[layer]
        if layer > 0:
            others = partners
            columns = grad_pack.shape[1] // 2
            grad_pack = added(lax.dynamic_slice_in_dim(grad_pack, data.odd * columns, columns, 1), partners[3])
        else:
            others = [data.from_partner(part, 1, own_product) for part in (grad_down, grad_gate, grad_up)]
        stacked_down = (down_out(odd, layer, grad_down, others[0], w_down.shape, stacked_down),)
        *stacked_experts, term = gate_up_out(
            odd, layer, (grad_gate, grad_up), others[1:3], w_gate, w_up, stacked_experts
        )
        if layer == 0:
            grad_pack = after(grad_pack, term, result, input_grad, *stacked_experts, *stacked_down, stats[-1])
        *stacked_pack, stat = pack_out(layer, grad_pack, packs[layer], stacked_pack)
        stats[layer] = sum_over_tensor(jnp.where(lane == EXPERTS + 1, jnp.sum(term, axis=1, keepdims=True), stat))
    stats = jnp.stack(stats)
    router_grad = stats[:, :, :EXPERTS]
    attn_gain_grad = stats[:, :, EXPERTS] / attn_gain.astype(F32)
    moe_gain_grad = (stats[:, :, EXPERTS + 1] + jnp.sum(w_router.astype(F32) * router_grad, axis=2)) / moe_gain.astype(F32)
    grad_query, grad_key, grad_value, grad_out = stacked_pack
    return (
        result,
        input_grad,
        attn_gain_grad,
        grad_query,
        grad_key,
        grad_value,
        grad_out,
        moe_gain_grad,
        router_grad,
        *stacked_experts,
        *stacked_down,
    )


def solution(mesh):
    placed = (
        P(("dp", "tensor"), None),
        P(("dp", "tensor"), None),
        P(None, "dp", None),
        P(None, "dp"),
        P(None, "dp", "tensor"),
        P(None, "dp", "tensor"),
        P(None, "dp", "tensor"),
        P(None, "tensor", "dp"),
        P(None, "dp"),
        P(None, "dp", None),
        P(None, None, "dp", "tensor"),
        P(None, None, "dp", "tensor"),
        P(None, None, "tensor", "dp"),
    )
    return jax.shard_map(
        local,
        mesh=mesh,
        in_specs=placed,
        out_specs=(
            P(("dp", "tensor"), None),
            P(("dp", "tensor"), None),
            P(None, "dp"),
            P(None, "dp", "tensor"),
            P(None, "dp", "tensor"),
            P(None, "dp", "tensor"),
            P(None, "tensor", "dp"),
            P(None, "dp"),
            P(None, "dp", None),
            P(None, None, "dp", "tensor"),
            P(None, None, "dp", "tensor"),
            P(None, None, "tensor", "dp"),
        ),
        check_vma=False,
    )
```

```python
import jax
import jax.numpy as jnp
from jax import lax
from jax.experimental import pallas as pl
from jax.experimental.pallas import tpu as pltpu
from jax.sharding import PartitionSpec as P

HEAD_SIZE = 64
TOPK = 8
EXPERTS = 16
LAYER_COUNT = 2
SEQUENCE_LENGTH = 1024
CAP = 512

EPSILON = 1e-06
ROPE_BASE = 10000.0
MASKED = -1e30
LANES = 128
BLOCK = 256
F32 = jnp.float32
BF16 = jnp.bfloat16
MIB = 1 << 20
QKV = 4 * LANES
OUT_END = 6 * LANES
PACK = 8 * LANES


def dot_nn(a, b):
    return lax.dot_general(a, b, (((1,), (0,)), ((), ())), preferred_element_type=F32)


def dot_nt(a, b):
    return lax.dot_general(a, b, (((1,), (1,)), ((), ())), preferred_element_type=F32)


def dot_tn(a, b):
    return lax.dot_general(a, b, (((0,), (0,)), ((), ())), preferred_element_type=F32)


def place_of(me, block):
    code = me ^ block
    return pl.multiple_of(((code & 1) * 2 + (code >> 1)) * BLOCK, BLOCK)


def half_mask(rows):
    return lax.broadcasted_iota(jnp.int32, (rows, LANES), 1) < HEAD_SIZE


def swap_halves(t):
    lane = lax.broadcasted_iota(jnp.int32, t.shape, 1) % HEAD_SIZE
    return jnp.where(
        lane < HEAD_SIZE // 2,
        pltpu.roll(t, LANES - HEAD_SIZE // 2, 1),
        pltpu.roll(t, HEAD_SIZE // 2, 1),
    )


def both_halves(t, low):
    turned = pltpu.roll(t, HEAD_SIZE, 1)
    return jnp.where(low, t, turned), jnp.where(low, turned, t)


def diagonal_mask(scores, row_block):
    rows = lax.broadcasted_iota(jnp.int32, scores.shape, 0) % BLOCK + row_block * BLOCK
    columns = lax.broadcasted_iota(jnp.int32, scores.shape, 1)
    return jnp.where(rows >= columns, scores, MASKED)


def attention_forward_kernel(
    me_ref, x_ref, pa_ref, pb_ref, cos_ref, sin_ref, q_ref, k_ref, v_ref, o_ref, lse_ref, out_ref, kd, vd
):
    rows, width = x_ref.shape
    half = width // 2
    low = half_mask(BLOCK)
    lane = lax.broadcasted_iota(jnp.int32, (BLOCK, LANES), 1)
    for i in range(rows // BLOCK):
        here = pl.ds(i * BLOCK, BLOCK)
        there = pl.ds(place_of(me_ref[0], i), BLOCK)
        qkv = dot_nn(x_ref[there, :half], pa_ref[:, :QKV]) + dot_nn(x_ref[there, half:], pb_ref[:, :QKV])
        cos, sin = cos_ref[here, :], sin_ref[here, :]

        def rope(t):
            return t * cos + swap_halves(t) * sin

        q = [(rope(qkv[:, j * LANES : (j + 1) * LANES]) * HEAD_SIZE ** (-0.5)).astype(BF16) for j in range(2)]
        k = rope(qkv[:, 2 * LANES : 3 * LANES])
        v = qkv[:, 3 * LANES :]
        k_ref[here, :] = k.astype(BF16)
        v_ref[here, :] = v.astype(BF16)
        for j, (kj, vj) in enumerate(zip(both_halves(k, low), both_halves(v, low))):
            kd[j, here, :] = kj.astype(BF16)
            vd[j, here, :] = vj.astype(BF16)
        context = (i + 1) * BLOCK
        lse_all = jnp.zeros((BLOCK, LANES), F32)
        outs = []
        for j in range(2):
            q_ref[here, j * LANES : (j + 1) * LANES] = q[j]
            zero = jnp.zeros_like(q[j])
            stacked = jnp.concatenate([jnp.where(low, q[j], zero), jnp.where(low, zero, q[j])], axis=0)
            scores = diagonal_mask(dot_nt(stacked, kd[j, :context, :]), i)
            row_max = jnp.max(scores, axis=1, keepdims=True)
            weights = jnp.exp(scores - row_max)
            total = jnp.sum(weights, axis=1, keepdims=True)
            lse = row_max + jnp.log(total)
            probs = (weights * (1.0 / total)).astype(BF16)
            mixed = dot_nn(probs, vd[j, :context, :])
            outs.append(jnp.where(low, mixed[:BLOCK], mixed[BLOCK:]).astype(BF16))
            lse_all = jnp.where(lane == 2 * j, lse[:BLOCK], lse_all)
            lse_all = jnp.where(lane == 2 * j + 1, lse[BLOCK:], lse_all)
        lse_ref[here, :] = lse_all
        mixed = jnp.concatenate(outs, axis=1)
        o_ref[there, :] = mixed
        out_ref[there, :half] = dot_nt(mixed, pa_ref[:, QKV:OUT_END]).astype(BF16)
        out_ref[there, half:] = dot_nt(mixed, pb_ref[:, QKV:OUT_END]).astype(BF16)


VMEM_SPEC = pl.BlockSpec(memory_space=pltpu.VMEM)
SMEM_SPEC = pl.BlockSpec(memory_space=pltpu.SMEM)


def attention_forward(me, x, pack, cos, sin):
    rows, width = x.shape
    shapes = (
        jax.ShapeDtypeStruct((rows, 2 * LANES), BF16),
        jax.ShapeDtypeStruct((rows, LANES), BF16),
        jax.ShapeDtypeStruct((rows, LANES), BF16),
        jax.ShapeDtypeStruct((rows, 2 * LANES), BF16),
        jax.ShapeDtypeStruct((rows, LANES), F32),
        jax.ShapeDtypeStruct((rows, width), BF16),
    )
    return pl.pallas_call(
        attention_forward_kernel,
        out_shape=shapes,
        in_specs=[SMEM_SPEC] + [VMEM_SPEC] * 5,
        scratch_shapes=[pltpu.VMEM((2, rows, LANES), BF16)] * 2,
        compiler_params=pltpu.CompilerParams(vmem_limit_bytes=40 * MIB),
        cost_estimate=pl.CostEstimate(
            flops=2 * rows * width * 768 + 4 * rows * rows * 256, bytes_accessed=12 * MIB, transcendentals=rows * rows * 2
        ),
        name="attention_forward",
    )(me, x, *pack, cos, sin)


def attention_backward_kernel(
    me_ref, dy_ref, pa_ref, pb_ref, q_ref, k_ref, v_ref, lse_ref, cos_ref, sin_ref, dqkv_ref, dx_ref, kd, vd, dk, dv
):
    rows, width = dy_ref.shape
    half = width // 2
    low = half_mask(BLOCK)
    for i in range(rows // BLOCK):
        here = pl.ds(i * BLOCK, BLOCK)
        k, v = k_ref[here, :].astype(F32), v_ref[here, :].astype(F32)
        for j, (kj, vj) in enumerate(zip(both_halves(k, low), both_halves(v, low))):
            kd[j, here, :] = kj.astype(BF16)
            vd[j, here, :] = vj.astype(BF16)
    dk[...] = jnp.zeros_like(dk)
    dv[...] = jnp.zeros_like(dv)
    for i in range(rows // BLOCK):
        here = pl.ds(i * BLOCK, BLOCK)
        there = pl.ds(place_of(me_ref[0], i), BLOCK)
        cos, sin = cos_ref[here, :], sin_ref[here, :]
        grad_mixed = (
            dot_nn(dy_ref[there, :half], pa_ref[:, QKV:OUT_END]) + dot_nn(dy_ref[there, half:], pb_ref[:, QKV:OUT_END])
        ).astype(BF16)
        lse_all = lse_ref[here, :]
        context = (i + 1) * BLOCK
        for j in range(2):
            qj = q_ref[here, j * LANES : (j + 1) * LANES]
            gj = grad_mixed[:, j * LANES : (j + 1) * LANES]
            zero = jnp.zeros_like(qj)
            q2 = jnp.concatenate([jnp.where(low, qj, zero), jnp.where(low, zero, qj)], axis=0)
            g2 = jnp.concatenate([jnp.where(low, gj, zero), jnp.where(low, zero, gj)], axis=0)
            lse = jnp.concatenate([lse_all[:, 2 * j : 2 * j + 1], lse_all[:, 2 * j + 1 : 2 * j + 2]], axis=0)
            scores = diagonal_mask(dot_nt(q2, kd[j, :context, :]), i)
            probs = jnp.exp(scores - lse)
            grad_probs = dot_nt(g2, vd[j, :context, :])
            inner = jnp.sum(probs * grad_probs, axis=1, keepdims=True)
            grad_scores = (probs * (grad_probs - inner)).astype(BF16)
            dk[j, :context, :] += dot_tn(grad_scores, q2)
            dv[j, :context, :] += dot_tn(probs.astype(BF16), g2)
            grad_q = dot_nn(grad_scores, kd[j, :context, :])
            grad_q = jnp.where(low, grad_q[:BLOCK], grad_q[BLOCK:]) * HEAD_SIZE ** (-0.5)
            dqkv_ref[there, j * LANES : (j + 1) * LANES] = (grad_q * cos - swap_halves(grad_q) * sin).astype(BF16)
    for i in range(rows // BLOCK):
        here = pl.ds(i * BLOCK, BLOCK)
        there = pl.ds(place_of(me_ref[0], i), BLOCK)
        cos, sin = cos_ref[here, :], sin_ref[here, :]

        def folded(total):
            pair = [total[j, here, :] for j in range(2)]
            pair = [t + pltpu.roll(t, HEAD_SIZE, 1) for t in pair]
            return jnp.where(low, pair[0], pair[1])

        grad_k = folded(dk)
        dqkv_ref[there, 2 * LANES : 3 * LANES] = (grad_k * cos - swap_halves(grad_k) * sin).astype(BF16)
        dqkv_ref[there, 3 * LANES :] = folded(dv).astype(BF16)
        grad_qkv = dqkv_ref[there, :]
        dx_ref[there, :half] = dot_nt(grad_qkv, pa_ref[:, :QKV]).astype(BF16)
        dx_ref[there, half:] = dot_nt(grad_qkv, pb_ref[:, :QKV]).astype(BF16)


def attention_backward(me, dy, pack, q, k, v, lse, cos, sin):
    rows, width = dy.shape
    return pl.pallas_call(
        attention_backward_kernel,
        out_shape=(jax.ShapeDtypeStruct((rows, QKV), BF16), jax.ShapeDtypeStruct((rows, width), BF16)),
        in_specs=[SMEM_SPEC] + [VMEM_SPEC] * 9,
        scratch_shapes=[pltpu.VMEM((2, rows, LANES), BF16)] * 2 + [pltpu.VMEM((2, rows, LANES), F32)] * 2,
        compiler_params=pltpu.CompilerParams(vmem_limit_bytes=48 * MIB),
        cost_estimate=pl.CostEstimate(
            flops=2 * rows * width * 768 + 10 * rows * rows * 256, bytes_accessed=12 * MIB, transcendentals=rows * rows * 2
        ),
        name="attention_backward",
    )(me, dy, *pack, q, k, v, lse, cos, sin)


def attention_weights_kernel(odd_ref, x_ref, dqkv_ref, dy_ref, o_ref, low_ref, dl_ref, own_ref, partner_ref):
    half = x_ref.shape[1] // 2
    for n, out_ref in enumerate((own_ref, partner_ref)):
        at = pl.ds(pl.multiple_of((odd_ref[0] ^ n) * half, half), half)
        out_ref[:, :QKV] = dot_tn(x_ref[:, at], dqkv_ref[...]).astype(BF16)
        out_ref[:, QKV:OUT_END] = dot_tn(dy_ref[:, at], o_ref[...]).astype(BF16)
        out_ref[:, OUT_END:] = dot_tn(low_ref[:, at], dl_ref[...]).astype(BF16)


def attention_weights(odd, x, dqkv, dy, o, low, dl):
    rows, width = x.shape
    return pl.pallas_call(
        attention_weights_kernel,
        out_shape=(jax.ShapeDtypeStruct((width // 2, OUT_END + LANES), BF16),) * 2,
        in_specs=[SMEM_SPEC] + [VMEM_SPEC] * 6,
        compiler_params=pltpu.CompilerParams(vmem_limit_bytes=32 * MIB),
        cost_estimate=pl.CostEstimate(flops=2 * rows * width * 800, bytes_accessed=9 * MIB, transcendentals=0),
        name="attention_weights",
    )(odd, x, dqkv, dy, o, low, dl)


UP_STEP = 512
BACK_STEP = 512


def spread_gates(gates, first, count):
    lane = lax.broadcasted_iota(jnp.int32, gates.shape, 1)
    return [jnp.sum(jnp.where(lane == first + n, gates, 0.0), axis=1, keepdims=True) for n in range(count)]


def pair_columns(columns, n):
    shape = (columns[0].shape[0], LANES)
    return jnp.concatenate(
        [jnp.broadcast_to(columns[2 * n], shape), jnp.broadcast_to(columns[2 * n + 1], shape)], axis=1
    )


def experts_up_kernel(
    base_ref, x_ref, ga_ref, gb_ref, ua_ref, ub_ref, ra_ref, rb_ref, chosen_ref, kept_ref, g_ref, u_ref, a_ref, probs_ref, gates_ref
):
    step = pl.program_id(0)
    count = g_ref.shape[1] // LANES
    half = x_ref.shape[1] // 2
    xa, xb = x_ref[:, :half], x_ref[:, half:]

    @pl.when(step == 0)
    def _():
        chosen = chosen_ref[...]
        logits = jnp.where(chosen > 0, dot_nn(xa, ra_ref[...]) + dot_nn(xb, rb_ref[...]), MASKED)
        raised = jnp.exp(logits - jnp.max(logits, axis=1, keepdims=True)) * chosen
        probs = raised / jnp.sum(raised, axis=1, keepdims=True)
        probs_ref[...] = probs
        gates_ref[...] = probs * kept_ref[...]

    columns = spread_gates(gates_ref[...], base_ref[0] + step * count, count)
    for n in range(count // 2):
        at = slice(2 * n * LANES, (2 * n + 2) * LANES)
        g = dot_nn(xa, ga_ref[:, at]) + dot_nn(xb, gb_ref[:, at])
        u = dot_nn(xa, ua_ref[:, at]) + dot_nn(xb, ub_ref[:, at])
        g_ref[:, at] = g.astype(BF16)
        u_ref[:, at] = u.astype(BF16)
        a_ref[:, at] = (pair_columns(columns, n) * (g * jax.nn.sigmoid(g)) * u).astype(BF16)


def experts_up(base, x, gate_up, pack, chosen, kept):
    rows, width = x.shape
    hidden = gate_up.shape[1] // 4
    steps = hidden // UP_STEP
    whole = lambda s: (0, 0)
    weights = [pl.BlockSpec((width // 2, UP_STEP), lambda s, n=n: (0, s + n * steps)) for n in range(4)]
    saved = pl.BlockSpec((rows, UP_STEP), lambda s: (0, s))
    router = pl.BlockSpec((width // 2, LANES), lambda s: (0, OUT_END // LANES))
    wide = pl.BlockSpec((rows, LANES), whole)
    return pl.pallas_call(
        experts_up_kernel,
        grid=(steps,),
        in_specs=[SMEM_SPEC, pl.BlockSpec((rows, width), whole)] + weights + [router] * 2 + [wide] * 2,
        out_specs=[saved] * 3 + [wide] * 2,
        out_shape=(jax.ShapeDtypeStruct((rows, hidden), BF16),) * 3 + (jax.ShapeDtypeStruct((rows, LANES), F32),) * 2,
        compiler_params=pltpu.CompilerParams(vmem_limit_bytes=60 * MIB),
        cost_estimate=pl.CostEstimate(
            flops=4 * rows * width * hidden, bytes_accessed=22 * MIB, transcendentals=rows * hidden
        ),
        name="experts_up",
    )(base, x, gate_up, gate_up, gate_up, gate_up, *pack, chosen, kept)


def experts_down_kernel(a_ref, da_ref, db_ref, out_ref):
    half = out_ref.shape[1] // 2
    out_ref[:, :half] = dot_nn(a_ref[...], da_ref[...]).astype(BF16)
    out_ref[:, half:] = dot_nn(a_ref[...], db_ref[...]).astype(BF16)


def experts_down(active, down):
    rows, hidden = active.shape
    half = down.shape[1]
    weights = [pl.BlockSpec((hidden, half), lambda s, n=n: (n, 0)) for n in range(2)]
    return pl.pallas_call(
        experts_down_kernel,
        grid=(rows // (2 * BLOCK),),
        in_specs=[pl.BlockSpec((2 * BLOCK, hidden), lambda s: (s, 0))] + weights,
        out_specs=pl.BlockSpec((2 * BLOCK, 2 * half), lambda s: (s, 0)),
        out_shape=jax.ShapeDtypeStruct((rows, 2 * half), BF16),
        compiler_params=pltpu.CompilerParams(vmem_limit_bytes=60 * MIB),
        cost_estimate=pl.CostEstimate(flops=4 * rows * half * hidden, bytes_accessed=6 * MIB, transcendentals=0),
        name="experts_down",
    )(active, down, down)


def experts_backward_kernel(
    base_ref, dy_ref, ga_ref, gb_ref, ua_ref, ub_ref, da_ref, db_ref, g_ref, u_ref, gates_ref, dg_ref, du_ref, out_ref, total, slots
):
    step = pl.program_id(0)
    rows, width = dy_ref.shape
    half = width // 2
    count = g_ref.shape[1] // LANES
    first = base_ref[0] + step * count
    columns = spread_gates(gates_ref[...], first, count)
    lane = lax.broadcasted_iota(jnp.int32, (rows, LANES), 1)
    dya, dyb = dy_ref[:, :half], dy_ref[:, half:]
    sums = jnp.zeros((rows, LANES), F32)
    for n in range(count // 2):
        at = slice(2 * n * LANES, (2 * n + 2) * LANES)
        gate = pair_columns(columns, n)
        da = dot_nt(dya, da_ref[at, :]) + dot_nt(dyb, db_ref[at, :])
        g = g_ref[:, at].astype(F32)
        u = u_ref[:, at].astype(F32)
        logistic = jax.nn.sigmoid(g)
        swished = g * logistic
        inner = da * swished * u
        for m in range(2):
            total_slot = jnp.sum(inner[:, m * LANES : (m + 1) * LANES], axis=1, keepdims=True)
            sums = jnp.where(lane == first + 2 * n + m, total_slot, sums)
        scaled = gate * da
        dg_ref[:, at] = (scaled * u * logistic * (1.0 + g * (1.0 - logistic))).astype(BF16)
        du_ref[:, at] = (scaled * swished).astype(BF16)
    even = dot_nt(dg_ref[...], ga_ref[...]) + dot_nt(du_ref[...], ua_ref[...])
    odd = dot_nt(dg_ref[...], gb_ref[...]) + dot_nt(du_ref[...], ub_ref[...])

    @pl.when(step == 0)
    def _():
        total[:, :half] = even
        total[:, half:] = odd
        slots[...] = sums

    @pl.when(step == pl.num_programs(0) - 1)
    def _():
        out_ref[:, :half] = (total[:, :half] + even).astype(BF16)
        out_ref[:, half:width] = (total[:, half:] + odd).astype(BF16)
        out_ref[:, width:] = (slots[...] + sums).astype(BF16)


def experts_backward(base, dy, gate_up, down, g, u, gates):
    rows, width = dy.shape
    hidden = gate_up.shape[1] // 4
    steps = hidden // BACK_STEP
    whole = lambda s: (0, 0)
    weights = [pl.BlockSpec((width // 2, BACK_STEP), lambda s, n=n: (0, s + n * steps)) for n in range(4)]
    saved = pl.BlockSpec((rows, BACK_STEP), lambda s: (0, s))
    once = pl.Buffered(1)
    return pl.pallas_call(
        experts_backward_kernel,
        grid=(steps,),
        in_specs=[SMEM_SPEC, pl.BlockSpec((rows, width), whole, pipeline_mode=once)]
        + weights
        + [pl.BlockSpec((BACK_STEP, width // 2), lambda s, n=n: (s + n * steps, 0)) for n in range(2)]
        + [saved] * 2
        + [pl.BlockSpec((rows, LANES), whole, pipeline_mode=once)],
        out_specs=[saved, saved, pl.BlockSpec((rows, width + LANES), whole, pipeline_mode=once)],
        out_shape=(
            jax.ShapeDtypeStruct((rows, hidden), BF16),
            jax.ShapeDtypeStruct((rows, hidden), BF16),
            jax.ShapeDtypeStruct((rows, width + LANES), BF16),
        ),
        scratch_shapes=[pltpu.VMEM((rows, width), F32), pltpu.VMEM((rows, LANES), F32)],
        compiler_params=pltpu.CompilerParams(vmem_limit_bytes=60 * MIB),
        cost_estimate=pl.CostEstimate(
            flops=6 * rows * width * hidden, bytes_accessed=38 * MIB, transcendentals=rows * hidden
        ),
        name="experts_backward",
    )(base, dy, gate_up, gate_up, gate_up, gate_up, down, down, g, u, gates)


def expert_weights_kernel(xn_ref, xf_ref, rn_ref, rf_ref, out_ref):
    out_ref[...] = (dot_tn(xn_ref[...], rn_ref[...]) + dot_tn(xf_ref[...], rf_ref[...])).astype(BF16)


def expert_weights(x, right):
    rows, width = x[0].shape
    hidden = right[0].shape[1]
    return pl.pallas_call(
        expert_weights_kernel,
        grid=(2,),
        in_specs=[pl.BlockSpec((rows, width // 2), lambda h: (0, h))] * 2
        + [pl.BlockSpec((rows, hidden), lambda h: (0, 0))] * 2,
        out_specs=pl.BlockSpec((width // 2, hidden), lambda h: (0, h)),
        out_shape=jax.ShapeDtypeStruct((width // 2, 2 * hidden), BF16),
        compiler_params=pltpu.CompilerParams(vmem_limit_bytes=60 * MIB),
        cost_estimate=pl.CostEstimate(flops=4 * rows * width * hidden, bytes_accessed=12 * MIB, transcendentals=0),
        name="expert_weights",
    )(*x, *right)


def gate_up_out_kernel(odd_ref, tg_ref, og_ref, tu_ref, ou_ref, wg_ref, wu_ref, *refs):
    gate_ref, up_ref, term_ref = refs[-3:]
    share = gate_ref.shape[1] // 2
    total = jnp.zeros(term_ref.shape, F32)
    for mine, start in ((True, odd_ref[0] * share), (False, (1 - odd_ref[0]) * share)):
        for e in range(share):
            at = slice(e * LANES, (e + 1) * LANES)
            dg = (tg_ref if mine else og_ref)[:, at].astype(F32)
            du = (tu_ref if mine else ou_ref)[:, at].astype(F32)
            gate_ref[0, start + e] = dg
            up_ref[0, start + e] = du
            total += dg * wg_ref[0, start + e].astype(F32) + du * wu_ref[0, start + e].astype(F32)
    term_ref[...] = total


def gate_up_out(odd, layer, totals, others, w_gate, w_up, earlier):
    layers, experts, depth, wide = w_gate.shape
    own = pl.BlockSpec((depth, others[0].shape[1]), lambda i, odd: (0, odd[0]))
    other = pl.BlockSpec(others[0].shape, lambda i, odd: (0, 0))
    block = pl.BlockSpec((1, experts, depth, wide), lambda i, odd: (layer, 0, 0, 0))
    return pl.pallas_call(
        gate_up_out_kernel,
        grid_spec=pltpu.PrefetchScalarGridSpec(
            num_scalar_prefetch=1,
            grid=(1,),
            in_specs=[own, other, own, other, block, block] + [pl.BlockSpec(memory_space=pl.ANY)] * len(earlier),
            out_specs=[block, block, pl.BlockSpec((depth, wide), lambda i, odd: (0, 0))],
        ),
        out_shape=(jax.ShapeDtypeStruct(w_gate.shape, F32),) * 2 + (jax.ShapeDtypeStruct((depth, wide), F32),),
        input_output_aliases={7 + n: n for n in range(len(earlier))},
        compiler_params=pltpu.CompilerParams(vmem_limit_bytes=24 * MIB),
        name="gate_up_out",
    )(odd, totals[0], others[0], totals[1], others[1], w_gate, w_up, *earlier)


def down_out_kernel(odd_ref, t_ref, o_ref, *refs):
    out_ref = refs[-1]
    share, wide = out_ref.shape[1] // 2, out_ref.shape[2]
    for e in range(share):
        at = slice(e * wide, (e + 1) * wide)
        out_ref[0, odd_ref[0] * share + e] = t_ref[:, at].astype(F32).T
        out_ref[0, (1 - odd_ref[0]) * share + e] = o_ref[:, at].astype(F32).T


def down_out(odd, layer, total, other, shape, earlier):
    block = pl.BlockSpec((1,) + shape[1:], lambda i, odd: (layer, 0, 0, 0))
    return pl.pallas_call(
        down_out_kernel,
        grid_spec=pltpu.PrefetchScalarGridSpec(
            num_scalar_prefetch=1,
            grid=(1,),
            in_specs=[pl.BlockSpec(other.shape, lambda i, odd: (0, odd[0])), pl.BlockSpec(other.shape, lambda i, odd: (0, 0))]
            + [pl.BlockSpec(memory_space=pl.ANY)] * len(earlier),
            out_specs=block,
        ),
        out_shape=jax.ShapeDtypeStruct(shape, F32),
        input_output_aliases={3 + n: n for n in range(len(earlier))},
        compiler_params=pltpu.CompilerParams(vmem_limit_bytes=24 * MIB),
        name="down_out",
    )(odd, total, other, *earlier)


def pack_out_kernel(t_ref, w_ref, *refs):
    q_ref, k_ref, v_ref, wo_ref, stats_ref = refs[-5:]
    total = t_ref[...].astype(F32)
    q_ref[0] = total[:, : 2 * LANES]
    k_ref[0] = total[:, 2 * LANES : 3 * LANES]
    v_ref[0] = total[:, 3 * LANES : QKV]
    wo_ref[0] = total[:, QKV:OUT_END].T
    term = jnp.sum(total[:, :QKV] * w_ref[:, :QKV].astype(F32), axis=1, keepdims=True)
    stats = total[:, OUT_END:]
    lane = lax.broadcasted_iota(jnp.int32, stats.shape, 1)
    stats_ref[...] = jnp.where(lane == EXPERTS, term, jnp.where(lane < EXPERTS, stats, 0.0))


def pack_out(layer, total, pack, earlier):
    depth, columns = total.shape
    shapes = [(depth, 2 * LANES), (depth, LANES), (depth, LANES), (2 * LANES, depth)]
    whole = lambda i: (0, 0)
    return pl.pallas_call(
        pack_out_kernel,
        grid=(1,),
        in_specs=[pl.BlockSpec(total.shape, whole), pl.BlockSpec(pack.shape, whole)]
        + [pl.BlockSpec(memory_space=pl.ANY)] * len(earlier),
        out_specs=[pl.BlockSpec((1,) + shape, lambda i: (layer, 0, 0)) for shape in shapes]
        + [pl.BlockSpec((depth, LANES), whole)],
        out_shape=tuple(jax.ShapeDtypeStruct((LAYER_COUNT,) + shape, F32) for shape in shapes)
        + (jax.ShapeDtypeStruct((depth, LANES), F32),),
        input_output_aliases={2 + n: n for n in range(len(earlier))},
        compiler_params=pltpu.CompilerParams(vmem_limit_bytes=24 * MIB),
        name="pack_out",
    )(total, pack, *earlier)


def normalize(residual, gain):
    scale = lax.rsqrt(jnp.mean(residual * residual, axis=-1, keepdims=True) + EPSILON)
    normed = residual * scale
    return normed, scale, (normed * gain).astype(BF16)


def normalize_back(grad_hidden, normed, scale, gain):
    grad_normed = grad_hidden * gain
    inner_mean = jnp.mean(grad_normed * normed, axis=-1, keepdims=True)
    return scale * (grad_normed - normed * inner_mean)


def rope_tables(row_count):
    positions = (jnp.arange(row_count, dtype=jnp.int32) % SEQUENCE_LENGTH).astype(F32)
    frequency = ROPE_BASE ** (-jnp.arange(0, HEAD_SIZE // 2, dtype=F32) * 2.0 / HEAD_SIZE)
    angles = positions[:, None] * frequency[None, :]
    cos, sin = jnp.cos(angles), jnp.sin(angles)
    return jnp.concatenate([cos] * 4, axis=1), jnp.concatenate([-sin, sin] * 2, axis=1)


def route_masks(routes, partner, me):
    rows = routes.shape[0]
    half = rows // (2 * lax.axis_size("tensor"))
    lane = lax.broadcasted_iota(jnp.int32, (rows, LANES), 1)
    earlier = (
        lax.broadcasted_iota(jnp.int32, (rows, rows), 0) > lax.broadcasted_iota(jnp.int32, (rows, rows), 1)
    ).astype(BF16)
    both = []
    for named in (routes, partner):
        chosen = named[:, 0:1] == lane
        for k in range(1, TOPK):
            chosen = chosen | (named[:, k : k + 1] == lane)
        before = dot_nn(earlier, chosen.astype(BF16))
        both.append((chosen.astype(F32), (chosen & (before < CAP)).astype(F32)))

    def placed(which, core):
        parts = []
        for lower, places in ((0, ((0, 0), (0, 2), (1, 0), (1, 2))), (1, ((0, 0), (1, 0), (0, 2), (1, 2)))):
            for x, y in places:
                start = ((me ^ (y + core)) * 2 + lower) * half
                parts.append(lax.dynamic_slice_in_dim(both[x][which], start, half, 0))
        return jnp.concatenate(parts, axis=0)

    return [[placed(which, core) for core in range(2)] for which in range(2)]


def after(values, *earlier):
    return lax.optimization_barrier((values,) + earlier)[0]


def swap(values, which):
    axis, bit = {"core": ("tensor", 1), "y": ("tensor", 2), "x": ("dp", 1)}[which]
    size = lax.axis_size(axis)
    return lax.ppermute(values, axis, [(i, i ^ bit) for i in range(size)])


def widen(values, meanwhile=None):
    other = swap(values, "y")
    sibling = swap(values, "core")
    if meanwhile is not None:
        other = after(other, *meanwhile(sibling))
    return jnp.concatenate([values, other, sibling, swap(other, "core")], axis=0)


def widen_pair(values):
    half = values.shape[0] // 2
    by_y, by_x = swap(values, "y"), swap(values, "x")
    first, second = swap(by_y[:half], "x"), swap(by_x[half:], "y")
    near = jnp.concatenate(
        [values[:half], by_y[:half], by_x[:half], first, values[half:], by_x[half:], by_y[half:], second], axis=0
    )
    return near, swap(near, "core")


def added(left, right):
    return left.astype(F32) + right.astype(F32)


def narrow(values, meanwhile=None):
    rows = values.shape[0] // 4
    far, near = values[2 * rows :], values[: 2 * rows]
    sent = added(near[rows:], swap(far[rows:], "core")).astype(BF16)
    out = swap(sent, "y")
    if meanwhile is not None:
        out = after(out, *meanwhile(sent))
    return added(near[:rows], swap(far[:rows], "core")) + out.astype(F32)


def pair_pieces(near, far):
    half = near.shape[0] // 8
    received = swap(far, "core")

    def piece(start, end):
        return added(near[start * half : end * half], received[start * half : end * half])

    return piece, piece(2, 4).astype(BF16), piece(6, 8).astype(BF16)


def pair_sum(piece, x_first, y_first, meanwhile=None):
    half = x_first.shape[0] // 2
    to_y = (piece(1, 2) + x_first[half:].astype(F32)).astype(BF16)
    to_x = (piece(5, 6) + y_first[half:].astype(F32)).astype(BF16)
    y_second, x_second = swap(to_y, "y"), swap(to_x, "x")
    if meanwhile is not None:
        y_second = after(y_second, *meanwhile((to_x, to_y)))
    upper = piece(0, 1) + x_first[:half].astype(F32) + y_second.astype(F32)
    lower = piece(4, 5) + y_first[:half].astype(F32) + x_second.astype(F32)
    return jnp.concatenate([upper, lower], axis=0)


def narrow_pair(near, far, meanwhile=None, later=None):
    piece, to_x, to_y = pair_pieces(near, far)
    x_first, y_first = swap(to_x, "x"), swap(to_y, "y")
    if meanwhile is not None:
        x_first = after(x_first, *meanwhile((to_x, to_y)))
    return pair_sum(piece, x_first, y_first, later)


def sum_over_tensor(values):
    for which in ("core", "y"):
        values = values + swap(values, which)
    return values


class Data:
    def __init__(self):
        size = lax.axis_size("dp")
        self.size = size
        self.groups = [list(range(0, size, 2)), list(range(1, size, 2))]
        self.odd = lax.axis_index("dp") % 2

    def by_parity(self, mine, other):
        even = self.odd == 0
        return jnp.where(even, mine, other), jnp.where(even, other, mine)

    def gather(self, own, axis=0):
        return lax.all_gather(own, "dp", axis=axis, tiled=True, axis_index_groups=self.groups)

    def scatter(self, values, axis=0):
        return lax.psum_scatter(values, "dp", scatter_dimension=axis, tiled=True, axis_index_groups=self.groups)

    def from_partner(self, total, axis, *earlier):
        size = total.shape[axis] // 2
        sent = lax.dynamic_slice_in_dim(total, (1 - self.odd) * size, size, axis)
        return swap(after(sent, *earlier) if earlier else sent, "x")

    def relative(self, values):
        depth = values.shape[1] // self.size
        return jnp.concatenate(
            [values[:, i * depth : (i + 1) * depth] for group in self.groups for i in group], axis=1
        )

    def absolute(self, values):
        depth = values.shape[1] // self.size
        count = self.size // 2
        starts = [(part * count + n) * depth for n in range(count) for part in range(2)]
        if depth % LANES == 0:

            def kernel(in_ref, out_ref):
                for n, start in enumerate(starts):
                    out_ref[:, n * depth : (n + 1) * depth] = in_ref[:, start : start + depth]

            return pl.pallas_call(
                kernel,
                out_shape=jax.ShapeDtypeStruct(values.shape, values.dtype),
                in_specs=[VMEM_SPEC],
                name="absolute",
            )(values)
        return jnp.concatenate([values[:, start : start + depth] for start in starts], axis=1)


def local(
    tokens_in,
    cotangent,
    routes,
    attn_gain,
    w_query,
    key_projection,
    value_projection,
    w_out,
    moe_gain,
    w_router,
    w_gate,
    w_up,
    w_down,
):
    rows_own, width = tokens_in.shape
    me = lax.axis_index("tensor")
    me_array = me.reshape(1).astype(jnp.int32)
    depth = w_query.shape[1]
    q_columns, kv_columns = w_query.shape[2], key_projection.shape[2]
    cos, sin = rope_tables(rows_own * lax.axis_size("tensor"))
    data = Data()
    share = EXPERTS // 2
    odd = data.odd.reshape(1).astype(jnp.int32)
    base = odd * share

    packs = []
    for layer in range(LAYER_COUNT):
        small = jnp.concatenate(
            [
                w_router[layer],
                attn_gain.T,
                moe_gain.T,
                jnp.zeros((depth, PACK - OUT_END - EXPERTS - 2 * LAYER_COUNT), BF16),
            ],
            axis=1,
        )
        packs.append(
            jnp.concatenate(
                [w_query[layer], key_projection[layer], value_projection[layer], w_out[layer].T, small], axis=1
            )
        )

    def shares(weight):
        return [lax.dynamic_slice_in_dim(weight, start * share, share, 0) for start in (data.odd, 1 - data.odd)]

    def gate_up_columns(layer, *earlier):
        gate, up = shares(w_gate[layer]), shares(w_up[layer])
        sent = jnp.concatenate([gate[1], up[1]], axis=0)
        other = swap(after(sent, *earlier) if earlier else sent, "x")
        columns = [
            part.transpose(1, 0, 2).reshape(depth, -1)
            for own, got in ((gate[0], other[:share]), (up[0], other[share:]))
            for part in data.by_parity(own, got)
        ]
        return jnp.concatenate(columns, axis=1)

    def down_rows(layer, *earlier):
        down = shares(w_down[layer])
        sent = after(down[1], *earlier) if earlier else down[1]
        return jnp.concatenate(
            [part.reshape(-1, depth) for part in data.by_parity(down[0], swap(sent, "x"))], axis=0
        )

    own_packs = [data.gather(packs[0])]
    tokens_in = data.relative(after(tokens_in, packs[0]))
    tokens_all = widen(tokens_in)
    columns = gate_up_columns(0, packs[0])
    gate_ups = [data.gather(columns)]
    pack = data.by_parity(own_packs[0], swap(after(own_packs[0], columns), "x"))
    rows = down_rows(0, pack[0])
    downs = [data.gather(rows, 1)]
    own_packs.append(data.gather(after(packs[1], rows)))
    next_columns, next_rows = gate_up_columns(1, pack[0]), down_rows(1, pack[0])
    gate_ups.append(data.gather(next_columns))
    downs.append(data.gather(next_rows, 1))
    masks = []

    def mask(layer, point):
        masks.append(route_masks(after(routes[layer], point), after(partner_routes[layer], point), me))
        return [*masks[-1][0], *masks[-1][1]]

    residual = tokens_in.astype(F32)
    weights, records = [], []
    for layer in range(LAYER_COUNT):
        gate_up, down = gate_ups[layer], downs[layer]
        if layer > 0:
            pack = data.by_parity(own_packs[layer], swap(after(own_packs[layer], residual), "x"))
        if layer == 0:
            gains = [
                jnp.concatenate([part[:, OUT_END + EXPERTS + n].astype(F32) for part in pack])[None, :]
                for n in range(2 * LAYER_COUNT)
            ]
        gain_attn, gain_moe = gains[layer], gains[LAYER_COUNT + layer]
        weights.append((pack, gain_attn, gain_moe, gate_up, down))
        if layer == 0:
            hidden_attn = normalize(tokens_all.astype(F32), gain_attn)[2]
            cotangent = data.relative(after(cotangent, hidden_attn))
            partner_routes = swap(after(routes, pack[0]), "x")
        else:
            hidden_attn = widen(normalize(residual, gain_attn)[2])
        before_attn = residual
        q, k, v, mixed, lse, attn_part = attention_forward(me_array, hidden_attn, pack, cos, sin)
        if layer == 0:
            held = lambda point: mask(0, point) + [next_columns, next_rows]
        else:
            held = lambda point, layer=layer: mask(layer, point)
        residual = residual + narrow(attn_part, held)
        before_moe = residual
        low_moe = normalize(residual, gain_moe)[2]
        hidden_moe = widen_pair(low_moe)
        chosen, kept = masks[layer]
        parts = [experts_up(base, hidden_moe[0], gate_up, pack, chosen[0], kept[0])]
        parts.append(experts_up(base, after(hidden_moe[1], parts[0][2]), gate_up, pack, chosen[1], kept[1]))
        g, u, active, probs, gates = zip(*parts)
        records.append(
            (before_attn, hidden_attn, q, k, v, mixed, lse, before_moe, low_moe, hidden_moe, probs[0], gates, g, u, active)
        )
        if layer < LAYER_COUNT - 1:
            active = after(active, *active)
            far, near = (experts_down(active[n], down) for n in (1, 0))
            residual = residual + narrow_pair(near, far)
    grad = cotangent.astype(F32)
    pieces = []
    half = rows_own // 2

    def own_of(values):
        return jnp.concatenate([values[:half], values[4 * half : 5 * half]], axis=0)

    for layer in reversed(range(LAYER_COUNT)):
        pack, gain_attn, gain_moe, gate_up, down = weights[layer]
        before_attn, hidden_attn, q, k, v, mixed, lse, before_moe, low_moe, hidden_moe, probs, gates, g, u, active = (
            records[layer]
        )
        kept = masks[layer][1][0]
        grad_pair = widen_pair(grad.astype(BF16))
        if layer == LAYER_COUNT - 1:
            grad_down = expert_weights(grad_pair, active)
            grad_pair = after(grad_pair, grad_down)
        parts = [experts_backward(base, grad_pair[0], gate_up, down, g[0], u[0], gates[0])]
        grad_far = after(grad_pair[1], parts[0][0])
        if layer < LAYER_COUNT - 1:
            grad_down = expert_weights((grad_pair[0], grad_far), active)
            grad_far = after(grad_far, grad_down)
        grad_down = data.scatter(grad_down)
        parts.append(experts_backward(base, grad_far, gate_up, down, g[1], u[1], gates[1]))
        grad_gate, grad_up, moe_part = zip(*parts)
        if layer == 0:
            result_first = swap(result_x, "x"), swap(result_y, "y")
            moe_part = after(moe_part, *result_first)
        made = []
        last = layer == LAYER_COUNT - 1

        def meanwhile(point, active=active, down=down, made=made, last=last, right=grad_gate):
            if last:
                held = after(active, *point)
                made.extend(experts_down(held[n], down) for n in (1, 0))
            else:
                made.append(expert_weights(hidden_moe, after(right, point[0])))
            return made

        def later(point, made=made, right=grad_gate if last else grad_up):
            made.append(expert_weights(hidden_moe, after(right, *point)))
            return made[-1:]

        own = narrow_pair(*moe_part, meanwhile, later)
        if last:
            far, near, grad_gate = made
            result_piece, result_x, result_y = pair_pieces(near, far)
        else:
            grad_gate, grad_up = made
        grad_gate = data.scatter(grad_gate)
        if not last:
            grad_up = data.scatter(grad_up)
        grad_moe_own, grad_pairs = own[:, :width], own[:, width:] * own_of(kept)
        own_probs = own_of(probs)
        grad_chosen = own_probs * (grad_pairs - jnp.sum(own_probs * grad_pairs, axis=-1, keepdims=True))
        grad_logits = grad_chosen.astype(BF16)
        grad_moe_own = grad_moe_own + jnp.concatenate(
            [dot_nt(grad_logits, part[:, OUT_END : OUT_END + LANES]) for part in pack], axis=1
        )
        normed_moe, scale_moe, _ = normalize(before_moe, gain_moe)
        grad = grad + normalize_back(grad_moe_own, normed_moe, scale_moe, gain_moe)
        grad_low = grad.astype(BF16)
        made = []
        if last:

            def meanwhile(point, made=made, right=grad_up):
                made.append(expert_weights(hidden_moe, after(right, point)))
                return made

        else:
            later_pack, _, later_up, _ = pieces[0]

            def meanwhile(point):
                partners.extend(data.from_partner(part, 1, point) for part in (later_up, later_pack))
                return partners[2:]

        grad_all = widen(grad_low, meanwhile)
        if last:
            grad_up = data.scatter(made[0])
        grad_qkv, attn_part = attention_backward(me_array, grad_all, pack, q, k, v, lse, cos, sin)
        pack_product = attention_weights(odd, hidden_attn, grad_qkv, grad_all, mixed, low_moe, grad_logits)
        if layer == LAYER_COUNT - 1:
            partners = []

            def meanwhile(point, grad_down=grad_down, grad_gate=grad_gate):
                partners.extend(data.from_partner(part, 1, point) for part in (grad_down, grad_gate))
                return [*pack_product, result_x, result_y, *partners]

        else:
            meanwhile = lambda point: pack_product
        attn_own = narrow(attn_part, meanwhile)
        own_product, partner_product = pack_product
        if layer == 0:
            own_product = added(own_product, swap(partner_product, "x")).astype(BF16)
            grad_pack = data.scatter(own_product)
        else:
            halves = jnp.where(data.odd == 0, own_product, partner_product), jnp.where(
                data.odd == 0, partner_product, own_product
            )
            grad_pack = data.scatter(jnp.concatenate(halves, axis=1))
        normed_attn, scale_attn, _ = normalize(before_attn, gain_attn)
        grad = grad + normalize_back(attn_own, normed_attn, scale_attn, gain_attn)
        pieces.insert(0, (grad_pack, grad_gate, grad_up, grad_down))
    residual = residual + pair_sum(result_piece, *after(result_first, *pack_product))
    result, input_grad = data.absolute(residual), data.absolute(grad)
    stacked_experts, stacked_down, stacked_pack, stats = (), (), (), [None] * LAYER_COUNT
    lane = lax.broadcasted_iota(jnp.int32, (depth, LANES), 1)
    for layer in reversed(range(LAYER_COUNT)):
        grad_pack, grad_gate, grad_up, grad_down = pieces[layer]
        if layer > 0:
            others = partners
            columns = grad_pack.shape[1] // 2
            grad_pack = added(lax.dynamic_slice_in_dim(grad_pack, data.odd * columns, columns, 1), partners[3])
        else:
            others = [data.from_partner(part, 1, own_product) for part in (grad_down, grad_gate, grad_up)]
        stacked_down = (down_out(odd, layer, grad_down, others[0], w_down.shape, stacked_down),)
        *stacked_experts, term = gate_up_out(
            odd, layer, (grad_gate, grad_up), others[1:3], w_gate, w_up, stacked_experts
        )
        if layer == 0:
            grad_pack = after(grad_pack, term, result, input_grad, *stacked_experts, *stacked_down, stats[-1])
        *stacked_pack, stat = pack_out(layer, grad_pack, packs[layer], stacked_pack)
        stats[layer] = sum_over_tensor(jnp.where(lane == EXPERTS + 1, jnp.sum(term, axis=1, keepdims=True), stat))
    stats = jnp.stack(stats)
    router_grad = stats[:, :, :EXPERTS]
    attn_gain_grad = stats[:, :, EXPERTS] / attn_gain.astype(F32)
    moe_gain_grad = (stats[:, :, EXPERTS + 1] + jnp.sum(w_router.astype(F32) * router_grad, axis=2)) / moe_gain.astype(F32)
    grad_query, grad_key, grad_value, grad_out = stacked_pack
    return (
        result,
        input_grad,
        attn_gain_grad,
        grad_query,
        grad_key,
        grad_value,
        grad_out,
        moe_gain_grad,
        router_grad,
        *stacked_experts,
        *stacked_down,
    )


def solution(mesh):
    placed = (
        P(("dp", "tensor"), None),
        P(("dp", "tensor"), None),
        P(None, "dp", None),
        P(None, "dp"),
        P(None, "dp", "tensor"),
        P(None, "dp", "tensor"),
        P(None, "dp", "tensor"),
        P(None, "tensor", "dp"),
        P(None, "dp"),
        P(None, "dp", None),
        P(None, None, "dp", "tensor"),
        P(None, None, "dp", "tensor"),
        P(None, None, "tensor", "dp"),
    )
    return jax.shard_map(
        local,
        mesh=mesh,
        in_specs=placed,
        out_specs=(
            P(("dp", "tensor"), None),
            P(("dp", "tensor"), None),
            P(None, "dp"),
            P(None, "dp", "tensor"),
            P(None, "dp", "tensor"),
            P(None, "dp", "tensor"),
            P(None, "tensor", "dp"),
            P(None, "dp"),
            P(None, "dp", None),
            P(None, None, "dp", "tensor"),
            P(None, None, "dp", "tensor"),
            P(None, None, "tensor", "dp"),
        ),
        check_vma=False,
    )
```
